512 devices in a mesh: site: 64 (over y, z), vec: 8 (over x, core).
Axes of the slice: x: 4, y: 4, z: 16, core: 2. Of those that a mesh axis runs over, the one named last changes fastest.
Arguments:
- diag_blocks: float32 [512, 64, 128], P('site'), as said below
- hop_blocks: float32 [512, 4, 64, 128], P('site'), may hold values from -0.1875 to 0.1875
- neighbors: int32 [512, 8], P('site'), may hold values from 0 to 511, as said below
- start_basis: float32 [512, 128, 512], P('site', None, 'vec'), may hold values from -6 to 6
Outputs:
- basis: float32 [512, 128, 512], P('site', None, 'vec')
- projected: float32 [512, 512], P(None, 'vec')
The draws below stay inside these ranges and needn't reach their ends.
Inputs may be any that keep to these rules, and one draw needn't show every extreme that they name: neighbors[s, d] is the site one step forward (d = 0, 1, 2, 3 along x, y, z, t) or back (d = 4 + k along the same k) of site s on a periodic 2 x 2 x 2 x 64 lattice; rows j * 8 to (j + 1) * 8 - 1 hold time slice j in an arbitrary order, so the t neighbours lie in the next and previous slice (wrapping) and the others in the same slice. `diag_blocks`: each diagonal block is Hermitian: its left half is symmetric and its right half antisymmetric.
All inputs are finite; a program needn't handle non-finite values.
Results may differ from the reference program's by a relative error of at most 0.00021.
Values sent between devices are 32-bit elements; how exact they have to be, the bound alone decides.
No kernel may reach another device: no remote copies, remote signals or barrier semaphores. Data moves between devices by JAX's collectives and lax.ppermute only.
A program may use at most 64 MiB of HBM per device.

```python
import math
import jax
import jax.numpy as jnp
from jax import lax

DOF = 64
COLS = 512
LX = 2
LY = 2
LZ = 2
DEGREE = 4
ITERS = 1
SITES_DEV = 8
NSITES = 512


def draw_diag_blocks(key, part):
    keys = jax.random.split(jax.random.fold_in(key, 11), 3)
    spread = 0.57 / math.sqrt(DOF)
    first_noise = jax.random.normal(keys[0], (NSITES, DOF, DOF), jnp.float32) * spread
    second_noise = jax.random.normal(keys[1], (NSITES, DOF, DOF), jnp.float32) * spread
    real_noise = (first_noise + jnp.swapaxes(first_noise, 1, 2)) * 0.70710678
    imag_noise = (second_noise - jnp.swapaxes(second_noise, 1, 2)) * 0.70710678
    slices = NSITES // SITES_DEV
    slope_level = (jnp.arange(NSITES) // SITES_DEV).astype(jnp.float32) / max(slices - 1, 1)
    site_mass = 2.7 + 0.6 * slope_level
    site_mass = site_mass + jax.random.uniform(keys[2], (NSITES,), jnp.float32, -0.3, 0.3)
    identity = jnp.eye(DOF, dtype=jnp.float32)
    real_part = real_noise + site_mass[:, None, None] * identity
    return jnp.concatenate([real_part, imag_noise], axis=2)


def draw_neighbors(key, part):
    slices = NSITES // SITES_DEV
    keys = jax.random.split(jax.random.fold_in(key, 5), slices)

    def one_order(subkey):
        return jax.random.permutation(subkey, SITES_DEV)
    storage = jax.vmap(one_order)(keys).astype(jnp.int32)
    position = jnp.argsort(storage, axis=1).astype(jnp.int32)
    x_coord = storage // (LY * LZ)
    y_coord = storage // LZ % LY
    z_coord = storage % LZ
    t_coord = jnp.broadcast_to(jnp.arange(slices, dtype=jnp.int32)[:, None], storage.shape)

    def locate(t_new, x_new, y_new, z_new):
        spatial = (x_new % LX * LY + y_new % LY) * LZ + z_new % LZ
        t_mod = t_new % slices
        return t_mod * SITES_DEV + position[t_mod, spatial]
    columns = [locate(t_coord, x_coord + 1, y_coord, z_coord), locate(t_coord, x_coord, y_coord + 1, z_coord), locate(t_coord, x_coord, y_coord, z_coord + 1), locate(t_coord + 1, x_coord, y_coord, z_coord), locate(t_coord, x_coord - 1, y_coord, z_coord), locate(t_coord, x_coord, y_coord - 1, z_coord), locate(t_coord, x_coord, y_coord, z_coord - 1), locate(t_coord - 1, x_coord, y_coord, z_coord)]
    return jnp.stack(columns, -1).reshape(NSITES, 8).astype(jnp.int32)


def block_scale(own_key, shape, cuts, low, top_value):
    gain, own = 1.0, jax.random.fold_in(own_key, 6)
    for axis_at, blocks in cuts:
        steps = jnp.exp(jax.random.uniform(jax.random.fold_in(own, axis_at), (blocks,), jnp.float32, low / len(cuts), top_value / len(cuts)))
        gain = gain * jnp.repeat(steps, shape[axis_at] // blocks).reshape([-1 if axis == axis_at else 1 for axis in range(len(shape))])
    return gain


def centred(stream_key, extent, scale, limit, cuts=(), kind=jnp.bfloat16):
    drawn = jax.random.normal(stream_key, extent, jnp.float32) * scale
    if len(cuts) > 0:
        drawn = block_scale(stream_key, extent, cuts, -0.22, 0.18) * drawn
    return jnp.clip(drawn, min=-limit, max=limit).astype(kind)


def setup_inputs(seed: int = 0) -> dict:
    key_list = jax.random.split(jax.random.key(seed), 5)
    return {
        "diag_blocks": draw_diag_blocks(jax.random.fold_in(key_list[4], 71), 0),
        "hop_blocks": centred(key_list[1], (NSITES, 4, DOF, 2 * DOF), (17 * DOF) ** -0.5, 0.1875, ((0, 64),), jnp.float32),
        "neighbors": draw_neighbors(jax.random.fold_in(key_list[4], 71), 0),
        "start_basis": centred(key_list[3], (NSITES, 2 * DOF, COLS), 1.0, 6.0, ((0, 64), (2, 8)), jnp.float32),
    }


filter_center = 3.7
filter_radius = 3.1
highest = lax.Precision.HIGHEST

def block_action(weights, vectors):
    half_size = weights.shape[-2]
    real_part = vectors[..., :half_size, :]
    imag_part = vectors[..., half_size:, :]
    stacked = jnp.stack([jnp.concatenate([real_part, -imag_part], -2), jnp.concatenate([imag_part, real_part], -2)], -3)
    result = jnp.einsum('...ab,...kbc->...kac', weights, stacked, precision=highest)
    return result.reshape(vectors.shape)

def adjoint_action(weights, vectors):
    half_size = weights.shape[-2]
    stacked = jnp.stack([vectors[..., :half_size, :], vectors[..., half_size:, :]], -3)
    result = jnp.einsum('...ab,...kac->...kbc', weights, stacked, precision=highest)
    upper_part = result[..., 0, :half_size, :] + result[..., 1, half_size:, :]
    lower_part = result[..., 1, :half_size, :] - result[..., 0, half_size:, :]
    return jnp.concatenate([upper_part, lower_part], -2)

def operate(vectors, diag_blocks, hop_blocks, neighbors):
    summed = block_action(diag_blocks, vectors)
    for direction in range(4):
        nearby = jnp.take(vectors, neighbors[:, direction], axis=0)
        summed = summed + block_action(hop_blocks[:, direction], nearby)
        backward = adjoint_action(hop_blocks[:, direction], vectors)
        summed = summed + jnp.take(backward, neighbors[:, 4 + direction], axis=0)
    return summed

def filtered(start_block, operator_apply):
    previous = start_block
    current = (operator_apply(start_block) - filter_center * start_block) / filter_radius
    for order_step in range(DEGREE - 1):
        following = 2.0 * (operator_apply(current) - filter_center * current) / filter_radius - previous
        previous, current = (current, following)
    return current

def reference(diag_blocks, hop_blocks, neighbors, start_basis):

    def operator_apply(vectors):
        return operate(vectors, diag_blocks, hop_blocks, neighbors)
    total_rows = NSITES * 2 * DOF
    identity = jnp.eye(COLS, dtype=jnp.float32)
    basis = start_basis
    projected = jnp.zeros((COLS, COLS), jnp.float32)
    for sweep_index in range(ITERS):
        filtered_block = filtered(basis, operator_apply)
        everything = filtered_block.reshape(total_rows, COLS)
        gram_matrix = jnp.einsum('rc,rd->cd', everything, everything, precision=highest) / total_rows
        lower_factor = jnp.linalg.cholesky(gram_matrix)
        inverse = jax.scipy.linalg.solve_triangular(lower_factor, identity, lower=True)
        basis_flat = jnp.einsum('rc,kc->rk', everything, inverse, precision=highest)
        basis = basis_flat.reshape(start_basis.shape)
        image_block = operator_apply(basis).reshape(total_rows, COLS)
        moment = jnp.einsum('rc,rk->ck', everything, image_block, precision=highest)
        projected = jnp.dot(inverse, moment, precision=highest) / total_rows
    return (basis, projected)
```

```python
import functools

import jax
import jax.numpy as jnp
from jax import lax
from jax.experimental import pallas as pl
from jax.experimental.pallas import tpu as pltpu
from jax.sharding import PartitionSpec as P

DEGREE = 4
CENTER = 3.7
RADIUS = 3.1
NEWTON_LIMIT = 12
NEWTON_DONE = 1e-6
VMEM_LIMIT = 44 * 1024 * 1024

f32 = jnp.float32
bf16 = jnp.bfloat16
VMEM_SPEC = pl.BlockSpec(memory_space=pltpu.VMEM)
SMEM_SPEC = pl.BlockSpec(memory_space=pltpu.SMEM)


def call(kernel, out_shape, n_smem, n_vmem, scratch=(), flops=0, moved=0, name=None):
    return pl.pallas_call(
        kernel,
        out_shape=out_shape,
        in_specs=[SMEM_SPEC] * n_smem + [VMEM_SPEC] * n_vmem,
        out_specs=jax.tree.map(lambda _: VMEM_SPEC, out_shape),
        scratch_shapes=list(scratch),
        compiler_params=pltpu.CompilerParams(vmem_limit_bytes=VMEM_LIMIT),
        cost_estimate=pl.CostEstimate(flops=flops, bytes_accessed=moved, transcendentals=0),
        name=name,
    )


def split(x):
    high = x.astype(bf16)
    return high, (x - high.astype(f32)).astype(bf16)


def left_operand(x):
    high, low = split(x)
    return jnp.concatenate([high, low, high], axis=1)


def adjoint(block):
    turned = block.T
    half = turned.shape[0] // 2
    return jnp.concatenate([turned[:half], -turned[half:]], axis=1)


def low_lanes(shape):
    return lax.broadcasted_iota(jnp.int32, shape, len(shape) - 1) < shape[-1] // 2


def swapped(x):
    return pltpu.roll(x, x.shape[-1] // 2, axis=x.ndim - 1)


def prepare_kernel(near, diag, hop, hop_back, own_ref, time_ref):
    sites, half, wide = diag.shape
    rows = lax.broadcasted_iota(jnp.int32, (half, wide), 0)
    cols = lax.broadcasted_iota(jnp.int32, (half, wide), 1)
    unit = jnp.where(rows == cols, CENTER, 0.0)
    for s in range(sites):
        parts = [diag[s] - unit]
        for d in range(3):
            parts.append(hop[s, d] + adjoint(hop[near[s, 4 + d] % sites, d]))
        own_ref[s] = left_operand(jnp.concatenate(parts, axis=1) * (1.0 / RADIUS))
        parts = [hop[s, 3], adjoint(hop_back[near[s, 7] % sites])]
        time_ref[s] = left_operand(jnp.concatenate(parts, axis=1) * (1.0 / RADIUS))


def spread(x, high_ref, low_ref):
    for n in range(x.shape[0]):
        xp = x[n]
        half = xp.shape[0]
        xs = swapped(xp)
        xq = jnp.where(low_lanes(xp.shape), -xs, xs)
        high_ref[n, :half], low_ref[n, :half] = split(xp)
        high_ref[n, half:], low_ref[n, half:] = split(xq)


def own_kernel(near, x, mats, out, high, low):
    sites = x.shape[0]
    spread(x, high, low)
    for s in range(sites):
        index = [s] + [near[s, d] % sites for d in range(3)]
        h = jnp.concatenate([high[n] for n in index], axis=0)
        l = jnp.concatenate([low[n] for n in index], axis=0)
        out[s] = jnp.dot(
            mats[s], jnp.concatenate([h, h, l], axis=0), preferred_element_type=f32
        )


def time_kernel(mode, near, own, ahead, behind, mats, *rest):
    *more, out, ahigh, alow, bhigh, blow = rest
    sites = own.shape[0]
    spread(ahead, ahigh, alow)
    spread(behind, bhigh, blow)
    for s in range(sites):
        n, m = near[s, 3] % sites, near[s, 7] % sites
        h = jnp.concatenate([ahigh[n], bhigh[m]], axis=0)
        l = jnp.concatenate([alow[n], blow[m]], axis=0)
        applied = own[s] + jnp.dot(
            mats[s], jnp.concatenate([h, h, l], axis=0), preferred_element_type=f32
        )
        if mode == "first":
            out[s] = applied
        elif mode == "next":
            out[s] = 2.0 * applied - more[0][s]
        else:
            out[s] = RADIUS * applied + CENTER * more[0][s]


def product_kernel(everything, own, image, out):
    low = low_lanes(own.shape)
    f, h = own[...], image[...]
    real = jnp.where(low, f, swapped(h))
    imag = jnp.where(low, swapped(f), h)
    left = left_operand(jnp.concatenate([real.T, imag.T], axis=1))
    for p in range(out.shape[0]):
        a, b = everything[2 * p], everything[2 * p + 1]
        both = jnp.concatenate(
            [jnp.where(low, a, swapped(b)), jnp.where(low, swapped(a), b)], axis=0
        )
        high, small = split(both)
        out[p] = jnp.dot(
            left, jnp.concatenate([high, high, small], axis=0), preferred_element_type=f32
        )


def sum_kernel(parts, out):
    total = parts[0]
    for i in range(1, parts.shape[0]):
        total = total + parts[i]
    for i in range(out.shape[0]):
        out[i] = total


NT = (((1,), (1,)), ((), ()))
NN = (((1,), (0,)), ((), ()))


def multiply(a, b, dims):
    ah, al = split(a)
    bh, bl = split(b)
    dot = functools.partial(lax.dot_general, dimension_numbers=dims, preferred_element_type=f32)
    return dot(ah, bh) + (dot(al, bh) + dot(ah, bl))


def inverse_kernel(count, gathered, out, scaled, factor, product):
    n = out.shape[0]
    devices, quarters, rows_each, lanes = gathered.shape
    for v in range(devices):
        for b in range(quarters):
            scaled[v * rows_each : (v + 1) * rows_each, b * lanes : (b + 1) * lanes] = (
                gathered[v, b] * (1.0 / count)
            )
    rows = lax.broadcasted_iota(jnp.int32, (n, n), 0)
    cols = lax.broadcasted_iota(jnp.int32, (n, n), 1)
    on_diag = rows == cols
    weight = jnp.where(rows > cols, 1.0, jnp.where(on_diag, 0.5, 0.0))
    unit = jnp.where(on_diag, 1.0, 0.0)
    matrix = scaled[...]
    only_diag = jnp.where(on_diag, matrix, 0.0)
    scale_row = lax.rsqrt(jnp.sum(only_diag, axis=0, keepdims=True))
    scale_col = lax.rsqrt(jnp.sum(only_diag, axis=1, keepdims=True))
    matrix = matrix * scale_row * scale_col
    scaled[...] = matrix
    factor[...] = unit - weight * (matrix - unit)

    def go_on(state):
        step, size = state
        return jnp.logical_and(step < NEWTON_LIMIT, jnp.logical_not(size < NEWTON_DONE))

    def improve(state):
        step, _ = state
        current = factor[...]
        product[...] = multiply(current, scaled[...], NN)
        error = multiply(product[...], current, NT) - unit
        size = jnp.sum(error * error)
        factor[...] = current - multiply(weight * error, current, NN)
        return step + 1, size

    _, size = lax.while_loop(go_on, improve, (jnp.int32(0), jnp.float32(1.0)))

    @pl.when(jnp.logical_not(size < NEWTON_DONE))
    def _():
        factor[...] = unit

        def eliminate(j, carry):
            pivot_row = scaled[pl.ds(j, 1), :]
            here = lax.broadcasted_iota(jnp.int32, (1, n), 1) == j
            pivot = jnp.sum(jnp.where(here, pivot_row, 0.0))
            a = scaled[...]
            column = jnp.sum(jnp.where(cols == j, a, 0.0), axis=1, keepdims=True) / pivot
            below = lax.broadcasted_iota(jnp.int32, (n, 1), 0) > j
            column = jnp.where(below, column, 0.0)
            r_row = factor[pl.ds(j, 1), :]
            scaled[...] = a - column * pivot_row
            factor[...] = factor[...] - column * r_row
            factor[pl.ds(j, 1), :] = r_row * lax.rsqrt(jnp.full_like(r_row, pivot))
            return carry

        lax.fori_loop(0, n, eliminate, 0)

    out[...] = factor[...] * scale_row


def basis_kernel(place, everything, inverse, out):
    devices, _, wide = everything.shape
    half = wide // 2
    mine = inverse[pl.ds(pl.multiple_of(place[0] * half, half), half), :]
    low = low_lanes((half, wide))
    top, bottom = [], []
    for p in range(devices // 2):
        r = mine[:, p * wide : (p + 1) * wide]
        rs = swapped(r)
        top += [jnp.where(low, r, 0.0), jnp.where(low, rs, 0.0)]
        bottom += [jnp.where(low, 0.0, rs), jnp.where(low, 0.0, r)]
    right = jnp.concatenate(
        [jnp.concatenate(top, axis=1), jnp.concatenate(bottom, axis=1)], axis=0
    )
    left = jnp.concatenate([everything[u] for u in range(devices)], axis=1)
    packed = multiply(left, right, NT)
    sites = out.shape[0]
    for s in range(sites):
        block = packed[s * half : (s + 1) * half]
        out[s, :half] = block[:, :half]
        out[s, half:] = block[:, half:]


def projected_kernel(count, place, moments, inverse, out):
    devices, quarters, rows_each, _ = moments.shape
    mine = inverse[pl.ds(pl.multiple_of(place[0] * rows_each, rows_each), rows_each), :]
    moment = jnp.concatenate(
        [
            jnp.concatenate([moments[v, b] for b in range(quarters)], axis=1)
            for v in range(devices)
        ],
        axis=0,
    )
    half_way = multiply(mine, moment, NN)
    out[...] = multiply(inverse[...], half_way, NT) * (1.0 / count)


def passed_along(x, by):
    size = lax.axis_size("site")
    return lax.ppermute(x, "site", [(i, (i + by) % size) for i in range(size)])


def local(diag_blocks, hop_blocks, neighbors, start_basis):
    sites, both, cols = start_basis.shape
    half = both // 2
    wide = 2 * cols
    devices = lax.axis_size("vec")
    slices = lax.axis_size("site")
    all_cols = cols * devices
    count = sites * both * slices
    place = lax.axis_index("vec").astype(jnp.int32).reshape(1)
    shape = jax.ShapeDtypeStruct
    block = shape((sites, half, wide), f32)

    current = jnp.concatenate([start_basis[:, :half], start_basis[:, half:]], axis=-1)
    hop_back = passed_along(hop_blocks[:, 3], 1)
    own_mats, time_mats = call(
        prepare_kernel,
        (
            shape((sites, half, 3 * 4 * both), bf16),
            shape((sites, half, 3 * 2 * both), bf16),
        ),
        1,
        3,
        flops=1 << 24,
        moved=1 << 22,
        name="prepare",
    )(neighbors, diag_blocks, hop_blocks, hop_back)

    stack = pltpu.VMEM((sites, both, wide), bf16)

    def apply(vectors, mode, *more):
        ahead = passed_along(vectors, -1)
        behind = passed_along(vectors, 1)
        own = call(
            own_kernel,
            block,
            1,
            2,
            scratch=[stack] * 2,
            flops=sites * half * 12 * both * wide * 2,
            moved=1 << 21,
            name="own_slice",
        )(neighbors, vectors, own_mats)
        return call(
            functools.partial(time_kernel, mode),
            block,
            1,
            4 + len(more),
            scratch=[stack] * 4,
            flops=sites * half * 6 * both * wide * 2,
            moved=1 << 21,
            name="next_slices",
        )(neighbors, own, ahead, behind, time_mats, *more)

    previous = current
    current = apply(current, "first")
    for _ in range(DEGREE - 1):
        previous, current = current, apply(current, "next", previous)

    flat = current.reshape(sites * half, wide)
    everything = lax.all_gather(flat, "vec", axis=0)
    image = apply(current, "image", current).reshape(sites * half, wide)
    quarters = all_cols // wide
    products = call(
        product_kernel,
        shape((quarters, wide, wide), f32),
        0,
        3,
        flops=6 * all_cols * wide * sites * both,
        moved=1 << 22,
        name="products",
    )(everything, flat, image)

    chunk = quarters * wide // slices
    parts = lax.all_to_all(
        products.reshape(slices, chunk, wide), "site", 0, 0, tiled=True
    )
    summed = call(
        sum_kernel,
        shape((slices, chunk, wide), f32),
        0,
        1,
        moved=1 << 19,
        name="sum_parts",
    )(parts)
    whole = lax.all_to_all(summed, "site", 0, 0, tiled=True).reshape(quarters, wide, wide)
    gram = lax.all_gather(whole[:, :cols], "vec", axis=0)
    moments = lax.all_gather(whole[:, cols:], "vec", axis=0)

    inverse = call(
        functools.partial(inverse_kernel, float(count)),
        shape((all_cols, all_cols), f32),
        0,
        1,
        scratch=[pltpu.VMEM((all_cols, all_cols), f32)] * 3,
        flops=9 * 6 * all_cols**3,
        moved=1 << 21,
        name="inverse_factor",
    )(gram)
    basis = call(
        basis_kernel,
        shape((sites, both, cols), f32),
        1,
        2,
        flops=12 * all_cols * wide * sites * half,
        moved=1 << 22,
        name="basis",
    )(place, everything, inverse)
    projected = call(
        functools.partial(projected_kernel, float(count)),
        shape((all_cols, cols), f32),
        1,
        2,
        flops=12 * all_cols * all_cols * cols,
        moved=1 << 22,
        name="projected",
    )(place, moments, inverse)
    return basis, projected


def solution(mesh):
    placed = (
        P("site", None, None),
        P("site", None, None, None),
        P("site", None),
        P("site", None, "vec"),
    )
    return jax.shard_map(
        local,
        mesh=mesh,
        in_specs=placed,
        out_specs=(P("site", None, "vec"), P(None, "vec")),
        check_vma=False,
    )
```

```python
import functools

import jax
import jax.numpy as jnp
from jax import lax
from jax.experimental import pallas as pl
from jax.experimental.pallas import tpu as pltpu
from jax.sharding import PartitionSpec as P

DEGREE = 4
CENTER = 3.7
RADIUS = 3.1
NEWTON_LIMIT = 12
NEWTON_DONE = 1e-6
VMEM_LIMIT = 44 * 1024 * 1024

f32 = jnp.float32
bf16 = jnp.bfloat16
VMEM_SPEC = pl.BlockSpec(memory_space=pltpu.VMEM)
SMEM_SPEC = pl.BlockSpec(memory_space=pltpu.SMEM)


def call(kernel, out_shape, n_smem, n_vmem, scratch=(), flops=0, moved=0, name=None):
    return pl.pallas_call(
        kernel,
        out_shape=out_shape,
        in_specs=[SMEM_SPEC] * n_smem + [VMEM_SPEC] * n_vmem,
        out_specs=jax.tree.map(lambda _: VMEM_SPEC, out_shape),
        scratch_shapes=list(scratch),
        compiler_params=pltpu.CompilerParams(vmem_limit_bytes=VMEM_LIMIT),
        cost_estimate=pl.CostEstimate(flops=flops, bytes_accessed=moved, transcendentals=0),
        name=name,
    )


def split(x):
    high = x.astype(bf16)
    return high, (x - high.astype(f32)).astype(bf16)


NT = (((1,), (1,)), ((), ()))
NN = (((1,), (0,)), ((), ()))


def left_operand(x):
    high, low = split(x)
    return jnp.concatenate([high, low, high], axis=1)


def low_lanes(shape):
    return lax.broadcasted_iota(jnp.int32, shape, len(shape) - 1) < shape[-1] // 2


def swapped(x):
    return pltpu.roll(x, x.shape[-1] // 2, axis=x.ndim - 1)


def transposed(block):
    turned = block.T
    half = turned.shape[0] // 2
    return jnp.concatenate([turned[:half], turned[half:]], axis=1)


def conjugated(block):
    return jnp.where(low_lanes(block.shape), block, -block)


def right_operand(block):
    turned = swapped(block)
    full = jnp.concatenate([block, jnp.where(low_lanes(block.shape), -turned, turned)], axis=0)
    high, low = split(full * (1.0 / RADIUS))
    return jnp.concatenate([high, high, low], axis=0)


def backward_kernel(near, x, hop, out, hop_out):
    for s in range(x.shape[0]):
        block = hop[s, 0]
        hop_out[s] = block
        out[s] = jnp.dot(
            left_operand(x[s]), right_operand(conjugated(block)), preferred_element_type=f32
        )


def prepare_kernel(near, diag, hop, own_ref, ahead_ref):
    sites, half, wide = diag.shape
    rows = lax.broadcasted_iota(jnp.int32, (half, wide), 0)
    cols = lax.broadcasted_iota(jnp.int32, (half, wide), 1)
    unit = jnp.where(rows == cols, CENTER, 0.0)
    for s in range(sites):
        parts = [right_operand(transposed(diag[s]) - unit)]
        for d in range(3):
            other = hop[lax.rem(near[s, 4 + d], sites), d]
            parts.append(right_operand(transposed(hop[s, d]) + conjugated(other)))
        own_ref[s] = jnp.concatenate(parts, axis=0)
        ahead_ref[s] = right_operand(transposed(hop[s, 3]))


def prepare_back_kernel(near, hop_back, back_ref):
    sites = hop_back.shape[0]
    for s in range(sites):
        back_ref[s] = right_operand(conjugated(hop_back[lax.rem(near[s, 7], sites)]))


def own_kernel(near, x, mats, out, spread):
    sites = x.shape[0]
    for n in range(sites):
        spread[n] = left_operand(x[n])
    for s in range(sites):
        index = [s] + [lax.rem(near[s, d], sites) for d in range(3)]
        left = jnp.concatenate([spread[n] for n in index], axis=1)
        out[s] = jnp.dot(left, mats[s], preferred_element_type=f32)


def first_kernel(near, own, ahead, received, ahead_mats, out):
    sites = own.shape[0]
    for s in range(sites):
        left = left_operand(ahead[lax.rem(near[s, 3], sites)])
        part = jnp.dot(left, ahead_mats[s], preferred_element_type=f32)
        out[s] = own[s] + part + received[lax.rem(near[s, 7], sites)]


def next_kernel(mode, near, own, ahead, behind, ahead_mats, back_mats, more, out):
    sites = own.shape[0]
    for s in range(sites):
        left = left_operand(ahead[lax.rem(near[s, 3], sites)])
        right = left_operand(behind[lax.rem(near[s, 7], sites)])
        applied = own[s] + jnp.dot(
            jnp.concatenate([left, right], axis=1),
            jnp.concatenate([ahead_mats[s], back_mats[s]], axis=0),
            preferred_element_type=f32,
        )
        if mode == "next":
            out[s] = 2.0 * applied - more[s]
        else:
            out[s] = RADIUS * applied + CENTER * more[s]


def product_kernel(place, everything, own, image, out):
    devices = everything.shape[0]
    sites, cols, wide = own.shape
    f = jnp.concatenate([own[s] for s in range(sites)], axis=1)
    h = jnp.concatenate([image[s] for s in range(sites)], axis=1)
    left = left_operand(jnp.concatenate([f, h], axis=0))
    third = sites * wide
    shift = place[0]
    tiles = devices // 2
    for p in range(tiles):
        both = []
        for j in (2 * p, 2 * p + 1):
            u = lax.rem(shift + j, devices)
            both.append(
                jnp.concatenate(
                    [everything[u, s * cols : (s + 1) * cols] for s in range(sites)], axis=1
                )
            )
        high, low = split(jnp.concatenate(both, axis=0))
        dot = functools.partial(lax.dot_general, dimension_numbers=NT, preferred_element_type=f32)
        tile = dot(left[:, : 2 * third], jnp.concatenate([high, high], axis=1)) + dot(
            left[:, :third], low
        )
        if p < 2:
            out[p * cols : (p + 1) * cols] = tile[:cols]
        elif p == 2:
            out[2 * cols : 2 * cols + cols // 2] = jnp.concatenate(
                [tile[: cols // 2, :cols], tile[cols // 2 : cols, :cols]], axis=1
            )
        start = 5 * cols // 2 + p * cols
        out[start : start + cols] = tile[cols:]
    start = 5 * cols // 2 + tiles * cols
    out[start:] = jnp.zeros((out.shape[0] - start, wide), f32)


def sum_kernel(parts, out):
    total = parts[0]
    for i in range(1, parts.shape[0]):
        total = total + parts[i]
    for i in range(out.shape[0]):
        out[i] = total


def multiply(a, b, dims):
    ah, al = split(a)
    bh, bl = split(b)
    dot = functools.partial(lax.dot_general, dimension_numbers=dims, preferred_element_type=f32)
    return dot(ah, bh) + (dot(al, bh) + dot(ah, bl))


def inverse_kernel(count, gathered, out, scaled, factor, product):
    n = out.shape[0]
    devices, _, wide = gathered.shape
    half = wide // 2
    blocks = {}
    for v in range(devices):
        for j in range(5):
            if j < 4:
                rows = gathered[v, (j // 2) * half : (j // 2 + 1) * half]
                block = rows[:, (j % 2) * half : (j % 2 + 1) * half]
            else:
                rows = gathered[v, wide:]
                block = jnp.concatenate([rows[:, :half], rows[:, half:]], axis=0)
            blocks[v, (v + j) % devices] = block
            if 0 < j < 4:
                blocks[(v + j) % devices, v] = block.T
    for v in range(devices):
        line = jnp.concatenate([blocks[v, u] for u in range(devices)], axis=1)
        scaled[v * half : (v + 1) * half, :] = line * (1.0 / count)
    rows = lax.broadcasted_iota(jnp.int32, (n, n), 0)
    cols = lax.broadcasted_iota(jnp.int32, (n, n), 1)
    on_diag = rows == cols
    weight = jnp.where(rows > cols, 1.0, jnp.where(on_diag, 0.5, 0.0))
    unit = jnp.where(on_diag, 1.0, 0.0)
    matrix = scaled[...]
    only_diag = jnp.where(on_diag, matrix, 0.0)
    scale_row = lax.rsqrt(jnp.sum(only_diag, axis=0, keepdims=True))
    scale_col = lax.rsqrt(jnp.sum(only_diag, axis=1, keepdims=True))
    matrix = matrix * scale_row * scale_col
    scaled[...] = matrix
    factor[...] = unit - weight * (matrix - unit)

    def go_on(state):
        step, size = state
        return jnp.logical_and(step < NEWTON_LIMIT, jnp.logical_not(size < NEWTON_DONE))

    def improve(state):
        step, _ = state
        current = factor[...]
        product[...] = multiply(current, scaled[...], NN)
        error = multiply(product[...], current, NT) - unit
        size = jnp.sum(error * error)
        factor[...] = current - multiply(weight * error, current, NN)
        return step + 1, size

    _, size = lax.while_loop(go_on, improve, (jnp.int32(0), jnp.float32(1.0)))

    @pl.when(jnp.logical_not(size < NEWTON_DONE))
    def _():
        factor[...] = unit

        def eliminate(j, carry):
            pivot_row = scaled[pl.ds(j, 1), :]
            here = lax.broadcasted_iota(jnp.int32, (1, n), 1) == j
            pivot = jnp.sum(jnp.where(here, pivot_row, 0.0))
            a = scaled[...]
            column = jnp.sum(jnp.where(cols == j, a, 0.0), axis=1, keepdims=True) / pivot
            below = lax.broadcasted_iota(jnp.int32, (n, 1), 0) > j
            column = jnp.where(below, column, 0.0)
            r_row = factor[pl.ds(j, 1), :]
            scaled[...] = a - column * pivot_row
            factor[...] = factor[...] - column * r_row
            factor[pl.ds(j, 1), :] = r_row * lax.rsqrt(jnp.full_like(r_row, pivot))
            return carry

        lax.fori_loop(0, n, eliminate, 0)

    out[...] = factor[...] * scale_row


def basis_kernel(place, everything, inverse, out):
    devices = everything.shape[0]
    sites, cols, wide = out.shape
    mine = inverse[pl.ds(pl.multiple_of(place[0] * cols, cols), cols), :]
    right = jnp.concatenate(
        [
            jnp.concatenate(
                [everything[u, s * cols : (s + 1) * cols] for s in range(sites)], axis=1
            )
            for u in range(devices)
        ],
        axis=0,
    )
    result = multiply(mine, right, NN)
    for s in range(sites):
        out[s] = result[:, s * wide : (s + 1) * wide]


def projected_kernel(count, place, moments, inverse, out):
    devices, _, wide = moments.shape
    half = wide // 2
    tiles = devices // 2
    low = low_lanes((half, wide))
    lines = []
    for v in range(devices):
        turned = [moments[v, p * half : (p + 1) * half] for p in range(tiles)]
        line = []
        for q in range(tiles):
            j = (2 * q - v) % devices
            if v % 2 == 0:
                line.append(turned[j // 2])
            else:
                line.append(swapped(jnp.where(low, turned[(j // 2 + 1) % tiles], turned[j // 2])))
        lines.append(jnp.concatenate(line, axis=1))
    moment = jnp.concatenate(lines, axis=0)
    mine = inverse[pl.ds(pl.multiple_of(place[0] * half, half), half), :]
    half_way = multiply(mine, moment, NN)
    out[...] = multiply(half_way, inverse[...], NT) * (1.0 / count)


def passed_along(x, by):
    size = lax.axis_size("site")
    return lax.ppermute(x, "site", [(i, (i + by) % size) for i in range(size)])


def local(diag_blocks, hop_blocks, neighbors, start_basis):
    sites, both, cols = start_basis.shape
    half = both // 2
    devices = lax.axis_size("vec")
    slices = lax.axis_size("site")
    all_cols = cols * devices
    count = float(sites * both * slices)
    place = lax.axis_index("vec").astype(jnp.int32).reshape(1)
    shape = jax.ShapeDtypeStruct
    block = shape((sites, cols, both), f32)
    size = sites * cols * both * 4

    def matrices(blocks):
        return shape((sites, 3 * blocks * both, both), bf16)

    def work(blocks):
        return sites * cols * blocks * 3 * both * both * 2

    current = jnp.swapaxes(start_basis, 1, 2)
    ahead = passed_along(current, -1)
    back, links = pl.pallas_call(
        backward_kernel,
        out_shape=(block, shape((sites, half, both), f32)),
        grid=(1,),
        in_specs=[
            SMEM_SPEC,
            pl.BlockSpec((sites, cols, both), lambda i: (0, 0, 0)),
            pl.BlockSpec((sites, 1, half, both), lambda i: (0, 3, 0, 0)),
        ],
        out_specs=(
            pl.BlockSpec((sites, cols, both), lambda i: (0, 0, 0)),
            pl.BlockSpec((sites, half, both), lambda i: (0, 0, 0)),
        ),
        compiler_params=pltpu.CompilerParams(vmem_limit_bytes=VMEM_LIMIT),
        cost_estimate=pl.CostEstimate(
            flops=work(1), bytes_accessed=4 * size, transcendentals=0
        ),
        name="backward",
    )(neighbors, current, hop_blocks)
    received = passed_along(back, 1)
    links_back = passed_along(links, 1)
    own_mats, ahead_mats = call(
        prepare_kernel,
        (matrices(4), matrices(1)),
        1,
        2,
        flops=1 << 24,
        moved=1 << 23,
        name="prepare",
    )(neighbors, diag_blocks, hop_blocks)
    back_mats = call(
        prepare_back_kernel, matrices(1), 1, 1, flops=1 << 22, moved=1 << 21, name="prepare_back"
    )(neighbors, links_back)

    def own_part(vectors):
        return call(
            own_kernel,
            block,
            1,
            2,
            scratch=[pltpu.VMEM((sites, cols, 3 * both), bf16)],
            flops=work(4),
            moved=8 * size,
            name="own_slice",
        )(neighbors, vectors, own_mats)

    def apply(vectors, mode, more):
        ahead = passed_along(vectors, -1)
        behind = passed_along(vectors, 1)
        return call(
            functools.partial(next_kernel, mode),
            block,
            1,
            6,
            flops=work(2),
            moved=8 * size,
            name="next_slices",
        )(neighbors, own_part(vectors), ahead, behind, ahead_mats, back_mats, more)

    previous = current
    current = call(first_kernel, block, 1, 4, flops=work(1), moved=6 * size, name="first_step")(
        neighbors, own_part(current), ahead, received, ahead_mats
    )
    for _ in range(DEGREE - 1):
        previous, current = current, apply(current, "next", previous)

    everything = lax.all_gather(current.reshape(sites * cols, both), "vec", axis=0)
    image = apply(current, "image", current)
    kept = 5 * cols // 2
    products = call(
        product_kernel,
        shape((slices * 8, both), f32),
        1,
        3,
        flops=6 * all_cols * 2 * cols * sites * both,
        moved=1 << 22,
        name="products",
    )(place, everything, current, image)

    parts = lax.all_to_all(products.reshape(slices, 8, both), "site", 0, 0, tiled=True)
    summed = call(
        sum_kernel, shape((slices, 8, both), f32), 0, 1, moved=1 << 19, name="sum_parts"
    )(parts)
    whole = lax.all_to_all(summed, "site", 0, 0, tiled=True).reshape(slices * 8, both)
    moments = lax.all_gather(whole[kept : kept + all_cols // 2], "vec", axis=0)
    gram = lax.all_gather(whole[:kept], "vec", axis=0)

    inverse = call(
        functools.partial(inverse_kernel, count),
        shape((all_cols, all_cols), f32),
        0,
        1,
        scratch=[pltpu.VMEM((all_cols, all_cols), f32)] * 3,
        flops=9 * 6 * all_cols**3,
        moved=1 << 21,
        name="inverse_factor",
    )(gram)
    basis = call(
        basis_kernel,
        block,
        1,
        2,
        flops=6 * all_cols * cols * sites * both,
        moved=1 << 22,
        name="basis",
    )(place, everything, inverse)
    projected = call(
        functools.partial(projected_kernel, count),
        shape((cols, all_cols), f32),
        1,
        2,
        flops=12 * all_cols * all_cols * cols,
        moved=1 << 22,
        name="projected",
    )(place, moments, inverse)
    return jnp.swapaxes(basis, 1, 2), projected.T


def solution(mesh):
    placed = (
        P("site", None, None),
        P("site", None, None, None),
        P("site", None),
        P("site", None, "vec"),
    )
    return jax.shard_map(
        local,
        mesh=mesh,
        in_specs=placed,
        out_specs=(P("site", None, "vec"), P(None, "vec")),
        check_vma=False,
    )
```

```python
import functools

import jax
import jax.numpy as jnp
from jax import lax
from jax.experimental import pallas as pl
from jax.experimental.pallas import tpu as pltpu
from jax.sharding import PartitionSpec as P

DEGREE = 4
CENTER = 3.7
RADIUS = 3.1
NEWTON_LIMIT = 12
NEWTON_DONE = 1e-6
VMEM_LIMIT = 44 * 1024 * 1024

f32 = jnp.float32
bf16 = jnp.bfloat16
VMEM_SPEC = pl.BlockSpec(memory_space=pltpu.VMEM)
SMEM_SPEC = pl.BlockSpec(memory_space=pltpu.SMEM)


def call(kernel, out_shape, n_smem, n_vmem, scratch=(), flops=0, moved=0, name=None):
    return pl.pallas_call(
        kernel,
        out_shape=out_shape,
        in_specs=[SMEM_SPEC] * n_smem + [VMEM_SPEC] * n_vmem,
        out_specs=jax.tree.map(lambda _: VMEM_SPEC, out_shape),
        scratch_shapes=list(scratch),
        compiler_params=pltpu.CompilerParams(vmem_limit_bytes=VMEM_LIMIT),
        cost_estimate=pl.CostEstimate(flops=flops, bytes_accessed=moved, transcendentals=0),
        name=name,
    )


def split(x):
    high = x.astype(bf16)
    return high, (x - high.astype(f32)).astype(bf16)


NT = (((1,), (1,)), ((), ()))
NN = (((1,), (0,)), ((), ()))


def left_operand(x):
    high, low = split(x)
    return jnp.concatenate([high, low, high], axis=1)


def low_lanes(shape):
    return lax.broadcasted_iota(jnp.int32, shape, len(shape) - 1) < shape[-1] // 2


def swapped(x):
    return pltpu.roll(x, x.shape[-1] // 2, axis=x.ndim - 1)


def transposed(block):
    turned = block.T
    half = turned.shape[0] // 2
    return jnp.concatenate([turned[:half], turned[half:]], axis=1)


def conjugated(block):
    return jnp.where(low_lanes(block.shape), block, -block)


def right_operand(block):
    turned = swapped(block)
    full = jnp.concatenate([block, jnp.where(low_lanes(block.shape), -turned, turned)], axis=0)
    high, low = split(full * (1.0 / RADIUS))
    return jnp.concatenate([high, high, low], axis=0)


def backward_kernel(x, hop, out, back_ref):
    for s in range(x.shape[0]):
        back = right_operand(conjugated(hop[s, 0]))
        back_ref[s] = back
        out[s] = jnp.dot(left_operand(x[s]), back, preferred_element_type=f32)


def prepare_kernel(near, diag, hop, own_ref, ahead_ref):
    sites, half, wide = diag.shape
    rows = lax.broadcasted_iota(jnp.int32, (half, wide), 0)
    cols = lax.broadcasted_iota(jnp.int32, (half, wide), 1)
    unit = jnp.where(rows == cols, CENTER, 0.0)
    for s in range(sites):
        parts = [right_operand(transposed(diag[s]) - unit)]
        for d in range(3):
            other = hop[lax.rem(near[s, 4 + d], sites), d]
            parts.append(right_operand(transposed(hop[s, d]) + conjugated(other)))
        own_ref[s] = jnp.concatenate(parts, axis=0)
        ahead_ref[s] = right_operand(transposed(hop[s, 3]))


def own_kernel(near, x, mats, out, spread):
    sites = x.shape[0]
    for n in range(sites):
        spread[n] = left_operand(x[n])
    for s in range(sites):
        index = [s] + [lax.rem(near[s, d], sites) for d in range(3)]
        left = jnp.concatenate([spread[n] for n in index], axis=1)
        out[s] = jnp.dot(left, mats[s], preferred_element_type=f32)


def step_kernel(mode, near, own, ahead, received, ahead_mats, *rest):
    sites = own.shape[0]
    more = rest[0] if mode != "first" else None
    back_mats, out, back = rest[-3:] if mode != "image" else (None, rest[-1], None)
    for s in range(sites):
        left = left_operand(ahead[lax.rem(near[s, 3], sites)])
        part = jnp.dot(left, ahead_mats[s], preferred_element_type=f32)
        applied = own[s] + (part + received[lax.rem(near[s, 7], sites)])
        if mode == "first":
            result = applied
        elif mode == "next":
            result = 2.0 * applied - more[s]
        else:
            result = RADIUS * applied + CENTER * more[s]
        out[s] = result
        if mode != "image":
            back[s] = jnp.dot(left_operand(result), back_mats[s], preferred_element_type=f32)


def product_kernel(place, everything, own, image, out):
    devices = everything.shape[0]
    sites, cols, wide = own.shape
    f = jnp.concatenate([own[s] for s in range(sites)], axis=1)
    h = jnp.concatenate([image[s] for s in range(sites)], axis=1)
    left = left_operand(jnp.concatenate([f, h], axis=0))
    third = sites * wide
    shift = place[0]
    tiles = devices // 2
    for p in range(tiles):
        both = []
        for j in (2 * p, 2 * p + 1):
            u = lax.rem(shift + j, devices)
            both.append(
                jnp.concatenate(
                    [everything[u, s * cols : (s + 1) * cols] for s in range(sites)], axis=1
                )
            )
        high, low = split(jnp.concatenate(both, axis=0))
        dot = functools.partial(lax.dot_general, dimension_numbers=NT, preferred_element_type=f32)
        tile = dot(left[:, : 2 * third], jnp.concatenate([high, high], axis=1)) + dot(
            left[:, :third], low
        )
        if p < 2:
            out[p * cols : (p + 1) * cols] = tile[:cols]
        elif p == 2:
            out[2 * cols : 2 * cols + cols // 2] = jnp.concatenate(
                [tile[: cols // 2, :cols], tile[cols // 2 : cols, :cols]], axis=1
            )
        start = 5 * cols // 2 + p * cols
        out[start : start + cols] = tile[cols:]
    start = 5 * cols // 2 + tiles * cols
    out[start:] = jnp.zeros((out.shape[0] - start, wide), f32)


def sum_kernel(parts, out):
    total = parts[0]
    for i in range(1, parts.shape[0]):
        total = total + parts[i]
    for i in range(out.shape[0]):
        out[i] = total


def multiply(a, b, dims):
    ah, al = split(a)
    bh, bl = split(b)
    dot = functools.partial(lax.dot_general, dimension_numbers=dims, preferred_element_type=f32)
    return dot(ah, bh) + (dot(al, bh) + dot(ah, bl))


def inverse_kernel(count, gathered, out, scaled, factor, product):
    n = out.shape[0]
    devices, _, wide = gathered.shape
    half = wide // 2
    blocks = {}
    for v in range(devices):
        for j in range(5):
            if j < 4:
                rows = gathered[v, (j // 2) * half : (j // 2 + 1) * half]
                block = rows[:, (j % 2) * half : (j % 2 + 1) * half]
            else:
                rows = gathered[v, wide:]
                block = jnp.concatenate([rows[:, :half], rows[:, half:]], axis=0)
            blocks[v, (v + j) % devices] = block
            if 0 < j < 4:
                blocks[(v + j) % devices, v] = block.T
    for v in range(devices):
        line = jnp.concatenate([blocks[v, u] for u in range(devices)], axis=1)
        scaled[v * half : (v + 1) * half, :] = line * (1.0 / count)
    rows = lax.broadcasted_iota(jnp.int32, (n, n), 0)
    cols = lax.broadcasted_iota(jnp.int32, (n, n), 1)
    on_diag = rows == cols
    weight = jnp.where(rows > cols, 1.0, jnp.where(on_diag, 0.5, 0.0))
    unit = jnp.where(on_diag, 1.0, 0.0)
    matrix = scaled[...]
    only_diag = jnp.where(on_diag, matrix, 0.0)
    scale_row = lax.rsqrt(jnp.sum(only_diag, axis=0, keepdims=True))
    scale_col = lax.rsqrt(jnp.sum(only_diag, axis=1, keepdims=True))
    matrix = matrix * scale_row * scale_col
    scaled[...] = matrix
    factor[...] = unit - weight * (matrix - unit)

    def go_on(state):
        step, size = state
        return jnp.logical_and(step < NEWTON_LIMIT, jnp.logical_not(size < NEWTON_DONE))

    def improve(state):
        step, _ = state
        current = factor[...]
        product[...] = multiply(current, scaled[...], NN)
        error = multiply(product[...], current, NT) - unit
        size = jnp.sum(error * error)
        factor[...] = current - multiply(weight * error, current, NN)
        return step + 1, size

    _, size = lax.while_loop(go_on, improve, (jnp.int32(0), jnp.float32(1.0)))

    @pl.when(jnp.logical_not(size < NEWTON_DONE))
    def _():
        factor[...] = unit

        def eliminate(j, carry):
            pivot_row = scaled[pl.ds(j, 1), :]
            here = lax.broadcasted_iota(jnp.int32, (1, n), 1) == j
            pivot = jnp.sum(jnp.where(here, pivot_row, 0.0))
            a = scaled[...]
            column = jnp.sum(jnp.where(cols == j, a, 0.0), axis=1, keepdims=True) / pivot
            below = lax.broadcasted_iota(jnp.int32, (n, 1), 0) > j
            column = jnp.where(below, column, 0.0)
            r_row = factor[pl.ds(j, 1), :]
            scaled[...] = a - column * pivot_row
            factor[...] = factor[...] - column * r_row
            factor[pl.ds(j, 1), :] = r_row * lax.rsqrt(jnp.full_like(r_row, pivot))
            return carry

        lax.fori_loop(0, n, eliminate, 0)

    out[...] = factor[...] * scale_row


def basis_kernel(place, everything, inverse, out):
    devices = everything.shape[0]
    sites, cols, wide = out.shape
    mine = inverse[pl.ds(pl.multiple_of(place[0] * cols, cols), cols), :]
    right = jnp.concatenate(
        [
            jnp.concatenate(
                [everything[u, s * cols : (s + 1) * cols] for s in range(sites)], axis=1
            )
            for u in range(devices)
        ],
        axis=0,
    )
    result = multiply(mine, right, NN)
    for s in range(sites):
        out[s] = result[:, s * wide : (s + 1) * wide]


def projected_kernel(count, place, moments, inverse, out):
    devices, _, wide = moments.shape
    half = wide // 2
    tiles = devices // 2
    low = low_lanes((half, wide))
    lines = []
    for v in range(devices):
        turned = [moments[v, p * half : (p + 1) * half] for p in range(tiles)]
        line = []
        for q in range(tiles):
            j = (2 * q - v) % devices
            if v % 2 == 0:
                line.append(turned[j // 2])
            else:
                line.append(swapped(jnp.where(low, turned[(j // 2 + 1) % tiles], turned[j // 2])))
        lines.append(jnp.concatenate(line, axis=1))
    moment = jnp.concatenate(lines, axis=0)
    mine = inverse[pl.ds(pl.multiple_of(place[0] * half, half), half), :]
    half_way = multiply(mine, moment, NN)
    out[...] = multiply(half_way, inverse[...], NT) * (1.0 / count)


def passed_along(x, by):
    size = lax.axis_size("site")
    return lax.ppermute(x, "site", [(i, (i + by) % size) for i in range(size)])


def local(diag_blocks, hop_blocks, neighbors, start_basis):
    sites, both, cols = start_basis.shape
    half = both // 2
    devices = lax.axis_size("vec")
    slices = lax.axis_size("site")
    all_cols = cols * devices
    count = float(sites * both * slices)
    place = lax.axis_index("vec").astype(jnp.int32).reshape(1)
    shape = jax.ShapeDtypeStruct
    block = shape((sites, cols, both), f32)
    size = sites * cols * both * 4

    def matrices(blocks):
        return shape((sites, 3 * blocks * both, both), bf16)

    def work(blocks):
        return sites * cols * blocks * 3 * both * both * 2

    current = jnp.swapaxes(start_basis, 1, 2)
    back, back_mats = pl.pallas_call(
        backward_kernel,
        out_shape=(block, matrices(1)),
        grid=(1,),
        in_specs=[
            pl.BlockSpec((sites, cols, both), lambda i: (0, 0, 0)),
            pl.BlockSpec((sites, 1, half, both), lambda i: (0, 3, 0, 0)),
        ],
        out_specs=(
            pl.BlockSpec((sites, cols, both), lambda i: (0, 0, 0)),
            pl.BlockSpec((sites, 3 * both, both), lambda i: (0, 0, 0)),
        ),
        compiler_params=pltpu.CompilerParams(vmem_limit_bytes=VMEM_LIMIT),
        cost_estimate=pl.CostEstimate(
            flops=work(1), bytes_accessed=4 * size, transcendentals=0
        ),
        name="backward",
    )(current, hop_blocks)
    own_mats, ahead_mats = call(
        prepare_kernel,
        (matrices(4), matrices(1)),
        1,
        2,
        flops=1 << 24,
        moved=1 << 23,
        name="prepare",
    )(neighbors, diag_blocks, hop_blocks)

    def apply(vectors, back, mode, *more):
        ahead = passed_along(vectors, -1)
        received = passed_along(back, 1)
        own = call(
            own_kernel,
            block,
            1,
            2,
            scratch=[pltpu.VMEM((sites, cols, 3 * both), bf16)],
            flops=work(4),
            moved=8 * size,
            name="own_slice",
        )(neighbors, vectors, own_mats)
        if mode != "image":
            more = (*more, back_mats)
        return call(
            functools.partial(step_kernel, mode),
            block if mode == "image" else (block, block),
            1,
            4 + len(more),
            flops=work(2),
            moved=8 * size,
            name="next_slices",
        )(neighbors, own, ahead, received, ahead_mats, *more)

    previous = current
    current, back = apply(current, back, "first")
    for _ in range(DEGREE - 1):
        following, back = apply(current, back, "next", previous)
        previous, current = current, following

    everything = lax.all_gather(current.reshape(sites * cols, both), "vec", axis=0)
    image = apply(current, back, "image", current)
    kept = 5 * cols // 2
    products = call(
        product_kernel,
        shape((slices * 8, both), f32),
        1,
        3,
        flops=6 * all_cols * 2 * cols * sites * both,
        moved=1 << 22,
        name="products",
    )(place, everything, current, image)

    parts = lax.all_to_all(products.reshape(slices, 8, both), "site", 0, 0, tiled=True)
    summed = call(
        sum_kernel, shape((slices, 8, both), f32), 0, 1, moved=1 << 19, name="sum_parts"
    )(parts)
    whole = lax.all_to_all(summed, "site", 0, 0, tiled=True).reshape(slices * 8, both)
    moments = lax.all_gather(whole[kept : kept + all_cols // 2], "vec", axis=0)
    gram = lax.all_gather(whole[:kept], "vec", axis=0)

    inverse = call(
        functools.partial(inverse_kernel, count),
        shape((all_cols, all_cols), f32),
        0,
        1,
        scratch=[pltpu.VMEM((all_cols, all_cols), f32)] * 3,
        flops=9 * 6 * all_cols**3,
        moved=1 << 21,
        name="inverse_factor",
    )(gram)
    basis = call(
        basis_kernel,
        block,
        1,
        2,
        flops=6 * all_cols * cols * sites * both,
        moved=1 << 22,
        name="basis",
    )(place, everything, inverse)
    projected = call(
        functools.partial(projected_kernel, count),
        shape((cols, all_cols), f32),
        1,
        2,
        flops=12 * all_cols * all_cols * cols,
        moved=1 << 22,
        name="projected",
    )(place, moments, inverse)
    return jnp.swapaxes(basis, 1, 2), projected.T


def solution(mesh):
    placed = (
        P("site", None, None),
        P("site", None, None, None),
        P("site", None),
        P("site", None, "vec"),
    )
    return jax.shard_map(
        local,
        mesh=mesh,
        in_specs=placed,
        out_specs=(P("site", None, "vec"), P(None, "vec")),
        check_vma=False,
    )
```

```python
import functools

import jax
import jax.numpy as jnp
from jax import lax
from jax.experimental import pallas as pl
from jax.experimental.pallas import tpu as pltpu
from jax.sharding import PartitionSpec as P

DEGREE = 4
CENTER = 3.7
RADIUS = 3.1
NEWTON_LIMIT = 12
NEWTON_DONE = 1e-6
VMEM_LIMIT = 44 * 1024 * 1024

f32 = jnp.float32
bf16 = jnp.bfloat16
VMEM_SPEC = pl.BlockSpec(memory_space=pltpu.VMEM)
SMEM_SPEC = pl.BlockSpec(memory_space=pltpu.SMEM)


def call(kernel, out_shape, n_smem, n_vmem, scratch=(), flops=0, moved=0, name=None):
    return pl.pallas_call(
        kernel,
        out_shape=out_shape,
        in_specs=[SMEM_SPEC] * n_smem + [VMEM_SPEC] * n_vmem,
        out_specs=jax.tree.map(lambda _: VMEM_SPEC, out_shape),
        scratch_shapes=list(scratch),
        compiler_params=pltpu.CompilerParams(vmem_limit_bytes=VMEM_LIMIT),
        cost_estimate=pl.CostEstimate(flops=flops, bytes_accessed=moved, transcendentals=0),
        name=name,
    )


def split(x):
    high = x.astype(bf16)
    return high, (x - high.astype(f32)).astype(bf16)


NT = (((1,), (1,)), ((), ()))
NN = (((1,), (0,)), ((), ()))


def left_operand(x):
    high, low = split(x)
    return jnp.concatenate([high, low, high], axis=1)


def low_lanes(shape):
    return lax.broadcasted_iota(jnp.int32, shape, len(shape) - 1) < shape[-1] // 2


def swapped(x):
    return pltpu.roll(x, x.shape[-1] // 2, axis=x.ndim - 1)


def transposed(block):
    turned = block.T
    half = turned.shape[0] // 2
    return jnp.concatenate([turned[:half], turned[half:]], axis=1)


def conjugated(block):
    return jnp.where(low_lanes(block.shape), block, -block)


def right_operand(block):
    turned = swapped(block)
    full = jnp.concatenate([block, jnp.where(low_lanes(block.shape), -turned, turned)], axis=0)
    high, low = split(full * (1.0 / RADIUS))
    return jnp.concatenate([high, high, low], axis=0)


def backward_kernel(near, x, hop, out, hop_out):
    for s in range(x.shape[0]):
        block = hop[s, 0]
        hop_out[s] = block
        out[s] = jnp.dot(
            left_operand(x[s]), right_operand(conjugated(block)), preferred_element_type=f32
        )


def prepare_kernel(near, diag, hop, own_ref, ahead_ref):
    sites, half, wide = diag.shape
    rows = lax.broadcasted_iota(jnp.int32, (half, wide), 0)
    cols = lax.broadcasted_iota(jnp.int32, (half, wide), 1)
    unit = jnp.where(rows == cols, CENTER, 0.0)
    for s in range(sites):
        parts = [right_operand(transposed(diag[s]) - unit)]
        for d in range(3):
            other = hop[lax.rem(near[s, 4 + d], sites), d]
            parts.append(right_operand(transposed(hop[s, d]) + conjugated(other)))
        own_ref[s] = jnp.concatenate(parts, axis=0)
        ahead_ref[s] = right_operand(transposed(hop[s, 3]))


def prepare_back_kernel(near, hop_back, back_ref):
    sites = hop_back.shape[0]
    for s in range(sites):
        back_ref[s] = right_operand(conjugated(hop_back[lax.rem(near[s, 7], sites)]))


def own_kernel(near, x, mats, out, spread):
    sites = x.shape[0]
    for n in range(sites):
        spread[n] = left_operand(x[n])
    for s in range(sites):
        index = [s] + [lax.rem(near[s, d], sites) for d in range(3)]
        left = jnp.concatenate([spread[n] for n in index], axis=1)
        out[s] = jnp.dot(left, mats[s], preferred_element_type=f32)


def first_kernel(near, own, ahead, received, ahead_mats, out):
    sites = own.shape[0]
    for s in range(sites):
        left = left_operand(ahead[lax.rem(near[s, 3], sites)])
        part = jnp.dot(left, ahead_mats[s], preferred_element_type=f32)
        out[s] = own[s] + part + received[lax.rem(near[s, 7], sites)]


def next_kernel(mode, near, own, ahead, behind, ahead_mats, back_mats, more, out):
    sites = own.shape[0]
    for s in range(sites):
        left = left_operand(ahead[lax.rem(near[s, 3], sites)])
        right = left_operand(behind[lax.rem(near[s, 7], sites)])
        applied = own[s] + jnp.dot(
            jnp.concatenate([left, right], axis=1),
            jnp.concatenate([ahead_mats[s], back_mats[s]], axis=0),
            preferred_element_type=f32,
        )
        if mode == "next":
            out[s] = 2.0 * applied - more[s]
        else:
            out[s] = RADIUS * applied + CENTER * more[s]


def senders(devices):
    chips = devices // 2
    table = []
    for v in range(devices):
        x, c = v // 2, v % 2
        opposite = (x + chips // 2) % chips
        table.append(
            [
                2 * ((x - 1) % chips) + c,
                2 * ((x + 1) % chips) + 1 - c,
                2 * x + 1 - c,
                2 * opposite + (1 - c if x < chips // 2 else c),
            ]
        )
    return table


def product_kernel(own, image, first, second, third, fourth, out):
    sites, cols, wide = own.shape

    def flat(ref):
        return jnp.concatenate([ref[s] for s in range(sites)], axis=1)

    f = flat(own)
    high, low = split(jnp.concatenate([f, flat(image)], axis=0))
    left = jnp.concatenate([high, low], axis=1)
    half = cols // 2
    dot = functools.partial(lax.dot_general, dimension_numbers=NT, preferred_element_type=f32)
    for p, group in enumerate(((own, first), (second, third), (fourth,))):
        h, l = split(jnp.concatenate([f if r is own else flat(r) for r in group], axis=0))
        tile = dot(left, jnp.concatenate([h, h], axis=1)) + dot(high, l)
        for i in range(2):
            part = tile[i * cols : (i + 1) * cols]
            start = i * (5 * half) + p * cols
            if len(group) == 2:
                out[start : start + cols] = part
            else:
                out[start : start + half] = jnp.concatenate([part[:half], part[half:]], axis=1)
    out[10 * half :] = jnp.zeros((out.shape[0] - 10 * half, wide), f32)


def lines_of(gathered):
    devices, _, wide = gathered.shape
    half = wide // 2
    blocks = {}
    for v, others in enumerate(senders(devices)):
        for j, u in enumerate([v, *others]):
            if j < 4:
                rows = gathered[v, (j // 2) * half : (j // 2 + 1) * half]
                block = rows[:, (j % 2) * half : (j % 2 + 1) * half]
            else:
                rows = gathered[v, wide : wide + half // 2]
                block = jnp.concatenate([rows[:, :half], rows[:, half:]], axis=0)
            blocks[v, u] = block
    for v in range(devices):
        for u in range(devices):
            if (v, u) not in blocks:
                blocks[v, u] = blocks[u, v].T
    return [
        jnp.concatenate([blocks[v, u] for u in range(devices)], axis=1) for v in range(devices)
    ]


def sum_kernel(parts, out):
    total = parts[0]
    for i in range(1, parts.shape[0]):
        total = total + parts[i]
    for i in range(out.shape[0]):
        out[i] = total


def multiply(a, b, dims):
    ah, al = split(a)
    bh, bl = split(b)
    dot = functools.partial(lax.dot_general, dimension_numbers=dims, preferred_element_type=f32)
    return dot(ah, bh) + (dot(al, bh) + dot(ah, bl))


def inverse_kernel(count, gathered, out, scaled, factor, product):
    n = out.shape[0]
    half = gathered.shape[2] // 2
    for v, line in enumerate(lines_of(gathered)):
        scaled[v * half : (v + 1) * half, :] = line * (1.0 / count)
    rows = lax.broadcasted_iota(jnp.int32, (n, n), 0)
    cols = lax.broadcasted_iota(jnp.int32, (n, n), 1)
    on_diag = rows == cols
    weight = jnp.where(rows > cols, 1.0, jnp.where(on_diag, 0.5, 0.0))
    unit = jnp.where(on_diag, 1.0, 0.0)
    matrix = scaled[...]
    only_diag = jnp.where(on_diag, matrix, 0.0)
    scale_row = lax.rsqrt(jnp.sum(only_diag, axis=0, keepdims=True))
    scale_col = lax.rsqrt(jnp.sum(only_diag, axis=1, keepdims=True))
    matrix = matrix * scale_row * scale_col
    scaled[...] = matrix
    factor[...] = unit - weight * (matrix - unit)

    def go_on(state):
        step, size = state
        return jnp.logical_and(step < NEWTON_LIMIT, jnp.logical_not(size < NEWTON_DONE))

    def improve(state):
        step, _ = state
        current = factor[...]
        product[...] = multiply(current, scaled[...], NN)
        error = multiply(product[...], current, NT) - unit
        size = jnp.sum(error * error)
        factor[...] = current - multiply(weight * error, current, NN)
        return step + 1, size

    _, size = lax.while_loop(go_on, improve, (jnp.int32(0), jnp.float32(1.0)))

    @pl.when(jnp.logical_not(size < NEWTON_DONE))
    def _():
        factor[...] = unit

        def eliminate(j, carry):
            pivot_row = scaled[pl.ds(j, 1), :]
            here = lax.broadcasted_iota(jnp.int32, (1, n), 1) == j
            pivot = jnp.sum(jnp.where(here, pivot_row, 0.0))
            a = scaled[...]
            column = jnp.sum(jnp.where(cols == j, a, 0.0), axis=1, keepdims=True) / pivot
            below = lax.broadcasted_iota(jnp.int32, (n, 1), 0) > j
            column = jnp.where(below, column, 0.0)
            r_row = factor[pl.ds(j, 1), :]
            scaled[...] = a - column * pivot_row
            factor[...] = factor[...] - column * r_row
            factor[pl.ds(j, 1), :] = r_row * lax.rsqrt(jnp.full_like(r_row, pivot))
            return carry

        lax.fori_loop(0, n, eliminate, 0)

    out[...] = factor[...] * scale_row


def basis_kernel(place, everything, inverse, out):
    devices = everything.shape[0]
    sites, cols, wide = out.shape
    mine = inverse[pl.ds(pl.multiple_of(place[0] * cols, cols), cols), :]
    right = jnp.concatenate(
        [
            jnp.concatenate(
                [everything[u, s * cols : (s + 1) * cols] for s in range(sites)], axis=1
            )
            for u in range(devices)
        ],
        axis=0,
    )
    result = multiply(mine, right, NN)
    for s in range(sites):
        out[s] = result[:, s * wide : (s + 1) * wide]


def projected_kernel(count, place, moments, inverse, out):
    half = moments.shape[2] // 2
    moment = jnp.concatenate(lines_of(moments), axis=0)
    mine = inverse[pl.ds(pl.multiple_of(place[0] * half, half), half), :]
    half_way = multiply(mine, moment, NN)
    out[...] = multiply(half_way, inverse[...], NT) * (1.0 / count)


def passed_along(x, by):
    size = lax.axis_size("site")
    return lax.ppermute(x, "site", [(i, (i + by) % size) for i in range(size)])


def local(diag_blocks, hop_blocks, neighbors, start_basis):
    sites, both, cols = start_basis.shape
    half = both // 2
    devices = lax.axis_size("vec")
    slices = lax.axis_size("site")
    all_cols = cols * devices
    count = float(sites * both * slices)
    place = lax.axis_index("vec").astype(jnp.int32).reshape(1)
    shape = jax.ShapeDtypeStruct
    block = shape((sites, cols, both), f32)
    size = sites * cols * both * 4

    def matrices(blocks):
        return shape((sites, 3 * blocks * both, both), bf16)

    def work(blocks):
        return sites * cols * blocks * 3 * both * both * 2

    current = jnp.swapaxes(start_basis, 1, 2)
    ahead = passed_along(current, -1)
    back, links = pl.pallas_call(
        backward_kernel,
        out_shape=(block, shape((sites, half, both), f32)),
        grid=(1,),
        in_specs=[
            SMEM_SPEC,
            pl.BlockSpec((sites, cols, both), lambda i: (0, 0, 0)),
            pl.BlockSpec((sites, 1, half, both), lambda i: (0, 3, 0, 0)),
        ],
        out_specs=(
            pl.BlockSpec((sites, cols, both), lambda i: (0, 0, 0)),
            pl.BlockSpec((sites, half, both), lambda i: (0, 0, 0)),
        ),
        compiler_params=pltpu.CompilerParams(vmem_limit_bytes=VMEM_LIMIT),
        cost_estimate=pl.CostEstimate(
            flops=work(1), bytes_accessed=4 * size, transcendentals=0
        ),
        name="backward",
    )(neighbors, current, hop_blocks)
    received = passed_along(back, 1)
    links_back = passed_along(links, 1)
    own_mats, ahead_mats = call(
        prepare_kernel,
        (matrices(4), matrices(1)),
        1,
        2,
        flops=1 << 24,
        moved=1 << 23,
        name="prepare",
    )(neighbors, diag_blocks, hop_blocks)
    back_mats = call(
        prepare_back_kernel, matrices(1), 1, 1, flops=1 << 22, moved=1 << 21, name="prepare_back"
    )(neighbors, links_back)

    def own_part(vectors):
        return call(
            own_kernel,
            block,
            1,
            2,
            scratch=[pltpu.VMEM((sites, cols, 3 * both), bf16)],
            flops=work(4),
            moved=8 * size,
            name="own_slice",
        )(neighbors, vectors, own_mats)

    def apply(vectors, mode, more):
        ahead = passed_along(vectors, -1)
        behind = passed_along(vectors, 1)
        return call(
            functools.partial(next_kernel, mode),
            block,
            1,
            6,
            flops=work(2),
            moved=8 * size,
            name="next_slices",
        )(neighbors, own_part(vectors), ahead, behind, ahead_mats, back_mats, more)

    previous = current
    current = call(first_kernel, block, 1, 4, flops=work(1), moved=6 * size, name="first_step")(
        neighbors, own_part(current), ahead, received, ahead_mats
    )
    for _ in range(DEGREE - 1):
        previous, current = current, apply(current, "next", previous)

    image = apply(current, "image", current)
    table = senders(devices)
    others = [
        lax.ppermute(current, "vec", [(table[v][i], v) for v in range(devices)]) for i in range(4)
    ]
    kept = 5 * cols // 2
    products = call(
        product_kernel,
        shape((slices * 8, both), f32),
        0,
        6,
        flops=6 * 5 * cols * 2 * cols * sites * both,
        moved=1 << 22,
        name="products",
    )(current, image, *others)
    flat, _ = lax.optimization_barrier((current.reshape(sites * cols, both), products))
    everything = lax.all_gather(flat, "vec", axis=0)

    parts = lax.all_to_all(products.reshape(slices, 8, both), "site", 0, 0, tiled=True)
    summed = call(
        sum_kernel, shape((slices, 8, both), f32), 0, 1, moved=1 << 19, name="sum_parts"
    )(parts)
    whole = lax.all_to_all(summed, "site", 0, 0, tiled=True).reshape(slices * 8, both)
    moments = lax.all_gather(whole[kept : kept + all_cols // 2], "vec", axis=0)
    gram = lax.all_gather(whole[:kept], "vec", axis=0)

    inverse = call(
        functools.partial(inverse_kernel, count),
        shape((all_cols, all_cols), f32),
        0,
        1,
        scratch=[pltpu.VMEM((all_cols, all_cols), f32)] * 3,
        flops=9 * 6 * all_cols**3,
        moved=1 << 21,
        name="inverse_factor",
    )(gram)
    basis = call(
        basis_kernel,
        block,
        1,
        2,
        flops=6 * all_cols * cols * sites * both,
        moved=1 << 22,
        name="basis",
    )(place, everything, inverse)
    projected = call(
        functools.partial(projected_kernel, count),
        shape((cols, all_cols), f32),
        1,
        2,
        flops=12 * all_cols * all_cols * cols,
        moved=1 << 22,
        name="projected",
    )(place, moments, inverse)
    return jnp.swapaxes(basis, 1, 2), projected.T


def solution(mesh):
    placed = (
        P("site", None, None),
        P("site", None, None, None),
        P("site", None),
        P("site", None, "vec"),
    )
    return jax.shard_map(
        local,
        mesh=mesh,
        in_specs=placed,
        out_specs=(P("site", None, "vec"), P(None, "vec")),
        check_vma=False,
    )
```

```python
import functools

import jax
import jax.numpy as jnp
from jax import lax
from jax.experimental import pallas as pl
from jax.experimental.pallas import tpu as pltpu
from jax.sharding import PartitionSpec as P

DEGREE = 4
CENTER = 3.7
RADIUS = 3.1
NEWTON_LIMIT = 12
NEWTON_DONE = 1e-6
VMEM_LIMIT = 44 * 1024 * 1024
VMEM_WHOLE = 44 * 1024 * 1024

f32 = jnp.float32
bf16 = jnp.bfloat16
VMEM_SPEC = pl.BlockSpec(memory_space=pltpu.VMEM)
SMEM_SPEC = pl.BlockSpec(memory_space=pltpu.SMEM)


def call(
    kernel,
    out_shape,
    n_smem,
    n_vmem,
    scratch=(),
    flops=0,
    moved=0,
    name=None,
):
    return pl.pallas_call(
        kernel,
        out_shape=out_shape,
        in_specs=[SMEM_SPEC] * n_smem + [VMEM_SPEC] * n_vmem,
        out_specs=jax.tree.map(lambda _: VMEM_SPEC, out_shape),
        scratch_shapes=list(scratch),
        compiler_params=pltpu.CompilerParams(vmem_limit_bytes=VMEM_LIMIT),
        cost_estimate=pl.CostEstimate(flops=flops, bytes_accessed=moved, transcendentals=0),
        name=name,
    )


def split(x):
    high = x.astype(bf16)
    return high, (x - high.astype(f32)).astype(bf16)


NT = (((1,), (1,)), ((), ()))
NN = (((1,), (0,)), ((), ()))


def stacked(x):
    return jnp.concatenate(split(x), axis=0)


def three_products(parts, high, low):
    m = parts.shape[0] // 2
    both = jnp.dot(parts, high, preferred_element_type=f32)
    return both[:m] + (both[m:] + jnp.dot(parts[:m], low, preferred_element_type=f32))


def low_lanes(shape):
    return lax.broadcasted_iota(jnp.int32, shape, len(shape) - 1) < shape[-1] // 2


def swapped(x):
    return pltpu.roll(x, x.shape[-1] // 2, axis=x.ndim - 1)


def transposed(block):
    turned = block.T
    half = turned.shape[0] // 2
    return jnp.concatenate([turned[:half], turned[half:]], axis=1)


def conjugated(block):
    return jnp.where(low_lanes(block.shape), block, -block)


def right_operand(block):
    turned = swapped(block)
    full = jnp.concatenate([block, jnp.where(low_lanes(block.shape), -turned, turned)], axis=0)
    return split(full * (1.0 / RADIUS))


def backward_kernel(x, hop, out, high, low):
    for s in range(x.shape[0]):
        high[s], low[s] = right_operand(conjugated(hop[s, 0]))
        out[s] = three_products(stacked(x[s]), high[s], low[s])


def prepare_kernel(near, diag, hop, own_high, own_low, ahead_high, ahead_low):
    sites, half, wide = diag.shape
    rows = lax.broadcasted_iota(jnp.int32, (half, wide), 0)
    cols = lax.broadcasted_iota(jnp.int32, (half, wide), 1)
    unit = jnp.where(rows == cols, CENTER, 0.0)
    for s in range(sites):
        own_high[s, :wide], own_low[s, :wide] = right_operand(transposed(diag[s]) - unit)
        for d in range(3):
            place = slice((1 + d) * wide, (2 + d) * wide)
            other = hop[lax.rem(near[s, 4 + d], sites), d]
            own_high[s, place], own_low[s, place] = right_operand(
                transposed(hop[s, d]) + conjugated(other)
            )
        ahead_high[s], ahead_low[s] = right_operand(transposed(hop[s, 3]))


def own_kernel(near, x, high, low, out, spread):
    sites = x.shape[0]
    for n in range(sites):
        spread[n] = stacked(x[n])
    for s in range(sites):
        index = [s] + [lax.rem(near[s, d], sites) for d in range(3)]
        parts = jnp.concatenate([spread[n] for n in index], axis=1)
        out[s] = three_products(parts, high[s], low[s])


def step_kernel(mode, near, own, ahead, received, ahead_high, ahead_low, *rest):
    sites = own.shape[0]
    more = rest[0] if mode != "first" else None
    if mode == "image":
        out, back = rest[-1], None
    else:
        back_high, back_low, out, back = rest[-4:]
    for s in range(sites):
        parts = stacked(ahead[lax.rem(near[s, 3], sites)])
        part = three_products(parts, ahead_high[s], ahead_low[s])
        applied = own[s] + (part + received[lax.rem(near[s, 7], sites)])
        if mode == "first":
            out[s] = applied
        elif mode == "next":
            out[s] = 2.0 * applied - more[s]
        else:
            out[s] = RADIUS * applied + CENTER * more[s]
    if back is not None:
        for s in range(sites):
            back[s] = three_products(stacked(out[s]), back_high[s], back_low[s])


def senders(devices):
    chips = devices // 2
    table = []
    for v in range(devices):
        x, c = v // 2, v % 2
        opposite = (x + chips // 2) % chips
        table.append(
            [
                2 * ((x - 1) % chips) + c,
                2 * ((x + 1) % chips) + 1 - c,
                2 * x + 1 - c,
                2 * opposite + (1 - c if x < chips // 2 else c),
            ]
        )
    return table


def product_kernel(own, image, first, second, third, fourth, out):
    sites, cols, wide = own.shape

    def flat(ref):
        return jnp.concatenate([ref[s] for s in range(sites)], axis=1)

    f = flat(own)
    high, low = split(jnp.concatenate([f, flat(image)], axis=0))
    left = jnp.concatenate([high, low], axis=1)
    half = cols // 2
    dot = functools.partial(lax.dot_general, dimension_numbers=NT, preferred_element_type=f32)
    for p, group in enumerate(((own, first), (second, third), (fourth,))):
        h, l = split(jnp.concatenate([f if r is own else flat(r) for r in group], axis=0))
        tile = dot(left, jnp.concatenate([h, h], axis=1)) + dot(high, l)
        for i in range(2):
            part = tile[i * cols : (i + 1) * cols]
            start = i * (5 * half) + p * cols
            if len(group) == 2:
                out[start : start + cols] = part
            else:
                out[start : start + half] = jnp.concatenate([part[:half], part[half:]], axis=1)
    out[10 * half :] = jnp.zeros((out.shape[0] - 10 * half, wide), f32)


def lines_of(gathered):
    devices, _, wide = gathered.shape
    half = wide // 2
    blocks = {}
    for v, others in enumerate(senders(devices)):
        for j, u in enumerate([v, *others]):
            if j < 4:
                rows = gathered[v, (j // 2) * half : (j // 2 + 1) * half]
                block = rows[:, (j % 2) * half : (j % 2 + 1) * half]
            else:
                rows = gathered[v, wide : wide + half // 2]
                block = jnp.concatenate([rows[:, :half], rows[:, half:]], axis=0)
            blocks[v, u] = block
    for v in range(devices):
        for u in range(devices):
            if (v, u) not in blocks:
                blocks[v, u] = blocks[u, v].T
    return [
        jnp.concatenate([blocks[v, u] for u in range(devices)], axis=1) for v in range(devices)
    ]


def sum_kernel(parts, out):
    total = parts[0]
    for i in range(1, parts.shape[0]):
        total = total + parts[i]
    for i in range(out.shape[0]):
        out[i] = total


def multiply(a, b, dims):
    ah, al = split(a)
    bh, bl = split(b)
    dot = functools.partial(lax.dot_general, dimension_numbers=dims, preferred_element_type=f32)
    return dot(ah, bh) + (dot(al, bh) + dot(ah, bl))


def inverse_kernel(count, gathered, out, scaled, factor):
    n = out.shape[0]
    half = gathered.shape[2] // 2
    for v, line in enumerate(lines_of(gathered)):
        scaled[v * half : (v + 1) * half, :] = line * (1.0 / count)
    rows = lax.broadcasted_iota(jnp.int32, (n, n), 0)
    cols = lax.broadcasted_iota(jnp.int32, (n, n), 1)
    on_diag = rows == cols
    weight = jnp.where(rows > cols, 1.0, jnp.where(on_diag, 0.5, 0.0))
    unit = jnp.where(on_diag, 1.0, 0.0)
    matrix = scaled[...]
    only_diag = jnp.where(on_diag, matrix, 0.0)
    scale_row = lax.rsqrt(jnp.sum(only_diag, axis=0, keepdims=True))
    scale_col = lax.rsqrt(jnp.sum(only_diag, axis=1, keepdims=True))
    matrix = matrix * scale_row * scale_col
    scaled[...] = matrix
    factor[...] = unit - weight * (matrix - unit)

    mid = n // 2
    dot = functools.partial(lax.dot_general, preferred_element_type=f32)
    square = (mid, mid)
    r, c = (lax.broadcasted_iota(jnp.int32, square, i) for i in range(2))
    small_weight = jnp.where(r > c, 1.0, jnp.where(r == c, 0.5, 0.0))
    small_unit = jnp.where(r == c, 1.0, 0.0)

    def improve(product, cut):
        s1 = cut(scaled[:, :mid])
        s2 = cut(scaled[:, mid:])
        top = cut(factor[:mid, :mid])
        side = cut(factor[mid:, :mid])
        low = cut(factor[mid:, mid:])
        lower = cut(factor[mid:, :])

        def part(x, piece):
            return tuple(y[piece] for y in x)

        t11 = cut(product(top, part(s1, slice(0, mid)), NN))
        t21 = cut(product(lower, s1, NN))
        t22 = cut(product(lower, s2, NN))
        e11 = product(t11, top, NT) - small_unit
        e21 = product(t21, top, NT)
        e22 = product(t21, side, NT) + product(t22, low, NT) - small_unit
        p11, p22 = small_weight * e11, small_weight * e22
        size = jnp.sum(p11 * p11 + p22 * p22 + e21 * e21)
        p11, p21, p22 = cut(p11), cut(e21), cut(p22)
        factor[:mid, :mid] = factor[:mid, :mid] - product(p11, top, NN)
        factor[mid:, :mid] = factor[mid:, :mid] - (
            product(p21, top, NN) + product(p22, side, NN)
        )
        factor[mid:, mid:] = factor[mid:, mid:] - product(p22, low, NN)
        return size

    def once(a, b, dims):
        return dot(a[0], b[0], dimension_numbers=dims)

    def thrice(a, b, dims):
        (ah, al), (bh, bl) = a, b
        return dot(ah, bh, dimension_numbers=dims) + (
            dot(al, bh, dimension_numbers=dims) + dot(ah, bl, dimension_numbers=dims)
        )

    improve(once, lambda x: (x.astype(bf16),))

    def go_on(state):
        step, size = state
        return jnp.logical_and(step < NEWTON_LIMIT, jnp.logical_not(size < NEWTON_DONE))

    def body(state):
        return state[0] + 1, improve(thrice, split)

    _, size = lax.while_loop(go_on, body, (jnp.int32(0), jnp.float32(1.0)))

    @pl.when(jnp.logical_not(size < NEWTON_DONE))
    def _():
        factor[...] = unit

        def eliminate(j, carry):
            pivot_row = scaled[pl.ds(j, 1), :]
            here = lax.broadcasted_iota(jnp.int32, (1, n), 1) == j
            pivot = jnp.sum(jnp.where(here, pivot_row, 0.0))
            a = scaled[...]
            column = jnp.sum(jnp.where(cols == j, a, 0.0), axis=1, keepdims=True) / pivot
            below = lax.broadcasted_iota(jnp.int32, (n, 1), 0) > j
            column = jnp.where(below, column, 0.0)
            r_row = factor[pl.ds(j, 1), :]
            scaled[...] = a - column * pivot_row
            factor[...] = factor[...] - column * r_row
            factor[pl.ds(j, 1), :] = r_row * lax.rsqrt(jnp.full_like(r_row, pivot))
            return carry

        lax.fori_loop(0, n, eliminate, 0)

    out[...] = factor[...] * scale_row


def basis_kernel(place, vectors, inverse, out):
    sites, columns, _ = out.shape
    mine = inverse[pl.ds(pl.multiple_of(place[0] * columns, columns), columns), :]
    for s in range(sites):
        block = jnp.concatenate(
            [vectors[u, s * columns : (s + 1) * columns] for u in range(vectors.shape[0])],
            axis=0,
        )
        out[s] = multiply(mine, block, NN)


def projected_kernel(count, place, moments, inverse, out):
    half = moments.shape[2] // 2
    moment = jnp.concatenate(lines_of(moments), axis=0)
    mine = inverse[pl.ds(pl.multiple_of(place[0] * half, half), half), :]
    half_way = multiply(mine, moment, NN)
    out[...] = multiply(half_way, inverse[...], NT) * (1.0 / count)


def passed_along(x, by):
    size = lax.axis_size("site")
    return lax.ppermute(x, "site", [(i, (i + by) % size) for i in range(size)])


def local(diag_blocks, hop_blocks, neighbors, start_basis):
    sites, both, cols = start_basis.shape
    half = both // 2
    devices = lax.axis_size("vec")
    slices = lax.axis_size("site")
    all_cols = cols * devices
    count = float(sites * both * slices)
    place = lax.axis_index("vec").astype(jnp.int32).reshape(1)
    shape = jax.ShapeDtypeStruct
    block = shape((sites, cols, both), f32)
    size = sites * cols * both * 4

    def matrices(blocks):
        return (shape((sites, blocks * both, both), bf16),) * 2

    def work(blocks):
        return sites * cols * blocks * 3 * both * both * 2

    current = jnp.swapaxes(start_basis, 1, 2)
    back, *back_mats = pl.pallas_call(
        backward_kernel,
        out_shape=(block, *matrices(1)),
        grid=(1,),
        in_specs=[
            pl.BlockSpec((sites, cols, both), lambda i: (0, 0, 0)),
            pl.BlockSpec((sites, 1, half, both), lambda i: (0, 3, 0, 0)),
        ],
        out_specs=(
            pl.BlockSpec((sites, cols, both), lambda i: (0, 0, 0)),
            *[pl.BlockSpec((sites, both, both), lambda i: (0, 0, 0))] * 2,
        ),
        compiler_params=pltpu.CompilerParams(vmem_limit_bytes=VMEM_WHOLE),
        cost_estimate=pl.CostEstimate(
            flops=work(1), bytes_accessed=4 * size, transcendentals=0
        ),
        name="backward",
    )(current, hop_blocks)
    mats = call(
        prepare_kernel,
        (*matrices(4), *matrices(1)),
        1,
        2,
        flops=1 << 24,
        moved=1 << 23,
        name="prepare",
    )(neighbors, diag_blocks, hop_blocks)
    own_mats, ahead_mats = mats[:2], mats[2:]

    def apply(vectors, back, mode, *more):
        ahead = passed_along(vectors, -1)
        received = passed_along(back, 1)
        own = call(
            own_kernel,
            block,
            1,
            3,
            scratch=[pltpu.VMEM((sites, 2 * cols, both), bf16)],
            flops=work(4),
            moved=8 * size,
            name="own_slice",
        )(neighbors, vectors, *own_mats)
        if mode != "image":
            more = (*more, *back_mats)
        return call(
            functools.partial(step_kernel, mode),
            block if mode == "image" else (block, block),
            1,
            5 + len(more),
            flops=work(1),
            moved=8 * size,
            name="next_slices",
        )(neighbors, own, ahead, received, *ahead_mats, *more)

    previous = current
    current, back = apply(current, back, "first")
    for _ in range(DEGREE - 1):
        following, back = apply(current, back, "next", previous)
        previous, current = current, following

    image = apply(current, back, "image", current)
    table = senders(devices)
    others = [
        lax.ppermute(current, "vec", [(table[v][i], v) for v in range(devices)]) for i in range(4)
    ]
    kept = 5 * cols // 2
    products = call(
        product_kernel,
        shape((slices * 8, both), f32),
        0,
        6,
        flops=6 * 5 * cols * 2 * cols * sites * both,
        moved=1 << 22,
        name="products",
    )(current, image, *others)
    flat, _ = lax.optimization_barrier((current.reshape(sites * cols, both), products))
    everything = lax.all_gather(flat, "vec", axis=0)

    parts = lax.all_to_all(products.reshape(slices, 8, both), "site", 0, 0, tiled=True)
    summed = call(
        sum_kernel, shape((slices, 8, both), f32), 0, 1, moved=1 << 19, name="sum_parts"
    )(parts)
    whole = lax.all_to_all(summed, "site", 0, 0, tiled=True).reshape(slices * 8, both)
    whole, everything = lax.optimization_barrier((whole, everything))
    moments = lax.all_gather(whole[kept : kept + all_cols // 2], "vec", axis=0)
    gram = lax.all_gather(whole[:kept], "vec", axis=0)

    inverse = call(
        functools.partial(inverse_kernel, count),
        shape((all_cols, all_cols), f32),
        0,
        1,
        scratch=[pltpu.VMEM((all_cols, all_cols), f32)] * 2,
        flops=9 * 6 * all_cols**3,
        moved=1 << 21,
        name="inverse_factor",
    )(gram)
    basis = call(
        basis_kernel,
        block,
        1,
        2,
        flops=6 * all_cols * cols * sites * both,
        moved=1 << 22,
        name="basis",
    )(place, everything, inverse)
    projected = call(
        functools.partial(projected_kernel, count),
        shape((cols, all_cols), f32),
        1,
        2,
        flops=12 * all_cols * all_cols * cols,
        moved=1 << 22,
        name="projected",
    )(place, moments, inverse)
    return jnp.swapaxes(basis, 1, 2), projected.T


def solution(mesh):
    placed = (
        P("site", None, None),
        P("site", None, None, None),
        P("site", None),
        P("site", None, "vec"),
    )
    return jax.shard_map(
        local,
        mesh=mesh,
        in_specs=placed,
        out_specs=(P("site", None, "vec"), P(None, "vec")),
        check_vma=False,
    )
```

```python
import functools

import jax
import jax.numpy as jnp
from jax import lax
from jax.experimental import pallas as pl
from jax.experimental.pallas import tpu as pltpu
from jax.sharding import PartitionSpec as P

DEGREE = 4
CENTER = 3.7
RADIUS = 3.1
NEWTON_LIMIT = 12
NEWTON_DONE = 1e-6
VMEM_LIMIT = 44 * 1024 * 1024
VMEM_WHOLE = 44 * 1024 * 1024

f32 = jnp.float32
bf16 = jnp.bfloat16
VMEM_SPEC = pl.BlockSpec(memory_space=pltpu.VMEM)
SMEM_SPEC = pl.BlockSpec(memory_space=pltpu.SMEM)


def call(
    kernel,
    out_shape,
    n_smem,
    n_vmem,
    scratch=(),
    flops=0,
    moved=0,
    name=None,
):
    return pl.pallas_call(
        kernel,
        out_shape=out_shape,
        in_specs=[SMEM_SPEC] * n_smem + [VMEM_SPEC] * n_vmem,
        out_specs=jax.tree.map(lambda _: VMEM_SPEC, out_shape),
        scratch_shapes=list(scratch),
        compiler_params=pltpu.CompilerParams(vmem_limit_bytes=VMEM_LIMIT),
        cost_estimate=pl.CostEstimate(flops=flops, bytes_accessed=moved, transcendentals=0),
        name=name,
    )


def split(x):
    high = x.astype(bf16)
    return high, (x - high.astype(f32)).astype(bf16)


def repeat_kernel(x, out):
    for i in range(out.shape[0]):
        out[i] = x[: out.shape[1]]


NT = (((1,), (1,)), ((), ()))
NN = (((1,), (0,)), ((), ()))


def stacked(x):
    return jnp.concatenate(split(x), axis=0)


def three_products(parts, high, low):
    m = parts.shape[0] // 2
    both = jnp.dot(parts, high, preferred_element_type=f32)
    return both[:m] + (both[m:] + jnp.dot(parts[:m], low, preferred_element_type=f32))


def low_lanes(shape):
    return lax.broadcasted_iota(jnp.int32, shape, len(shape) - 1) < shape[-1] // 2


def swapped(x):
    return pltpu.roll(x, x.shape[-1] // 2, axis=x.ndim - 1)


def transposed(block):
    turned = block.T
    half = turned.shape[0] // 2
    return jnp.concatenate([turned[:half], turned[half:]], axis=1)


def conjugated(block):
    return jnp.where(low_lanes(block.shape), block, -block)


def right_operand(block):
    turned = swapped(block)
    full = jnp.concatenate([block, jnp.where(low_lanes(block.shape), -turned, turned)], axis=0)
    return split(full * (1.0 / RADIUS))


def backward_kernel(x, hop, out, high, low):
    for s in range(x.shape[0]):
        high[s], low[s] = right_operand(conjugated(hop[s, 0]))
        out[s] = three_products(stacked(x[s]), high[s], low[s])


def prepare_kernel(near, diag, hop, own_high, own_low, ahead_high, ahead_low):
    sites, half, wide = diag.shape
    rows = lax.broadcasted_iota(jnp.int32, (half, wide), 0)
    cols = lax.broadcasted_iota(jnp.int32, (half, wide), 1)
    unit = jnp.where(rows == cols, CENTER, 0.0)
    for s in range(sites):
        own_high[s, :wide], own_low[s, :wide] = right_operand(transposed(diag[s]) - unit)
        for d in range(3):
            place = slice((1 + d) * wide, (2 + d) * wide)
            other = hop[lax.rem(near[s, 4 + d], sites), d]
            own_high[s, place], own_low[s, place] = right_operand(
                transposed(hop[s, d]) + conjugated(other)
            )
        ahead_high[s], ahead_low[s] = right_operand(transposed(hop[s, 3]))


def own_kernel(near, x, high, low, out, spread):
    sites = x.shape[0]
    for n in range(sites):
        spread[n] = stacked(x[n])
    for s in range(sites):
        index = [s] + [lax.rem(near[s, d], sites) for d in range(3)]
        parts = jnp.concatenate([spread[n] for n in index], axis=1)
        out[s] = three_products(parts, high[s], low[s])


def step_kernel(mode, near, own, ahead, received, ahead_high, ahead_low, *rest):
    sites = own.shape[0]
    more = rest[0] if mode != "first" else None
    if mode == "image":
        out, back = rest[-1], None
    else:
        back_high, back_low, out, back = rest[-4:]
    for s in range(sites):
        parts = stacked(ahead[lax.rem(near[s, 3], sites)])
        part = three_products(parts, ahead_high[s], ahead_low[s])
        applied = own[s] + (part + received[lax.rem(near[s, 7], sites)])
        if mode == "first":
            out[s] = applied
        elif mode == "next":
            out[s] = 2.0 * applied - more[s]
        else:
            out[s] = RADIUS * applied + CENTER * more[s]
    if back is not None:
        for s in range(sites):
            back[s] = three_products(stacked(out[s]), back_high[s], back_low[s])


def senders(devices):
    chips = devices // 2
    table = []
    for v in range(devices):
        x, c = v // 2, v % 2
        opposite = (x + chips // 2) % chips
        table.append(
            [
                2 * ((x - 1) % chips) + c,
                2 * ((x + 1) % chips) + 1 - c,
                2 * x + 1 - c,
                2 * opposite + (1 - c if x < chips // 2 else c),
            ]
        )
    return table


def product_kernel(own, image, first, second, third, fourth, out):
    sites, cols, wide = own.shape

    def flat(ref):
        return jnp.concatenate([ref[s] for s in range(sites)], axis=1)

    f = flat(own)
    high, low = split(jnp.concatenate([f, flat(image)], axis=0))
    left = jnp.concatenate([high, low], axis=1)
    half = cols // 2
    dot = functools.partial(lax.dot_general, dimension_numbers=NT, preferred_element_type=f32)
    for p, group in enumerate(((own, first), (second, third), (fourth,))):
        h, l = split(jnp.concatenate([f if r is own else flat(r) for r in group], axis=0))
        tile = dot(left, jnp.concatenate([h, h], axis=1)) + dot(high, l)
        for i in range(2):
            part = tile[i * cols : (i + 1) * cols]
            start = i * (5 * half) + p * cols
            if len(group) == 2:
                out[start : start + cols] = part
            else:
                out[start : start + half] = jnp.concatenate([part[:half], part[half:]], axis=1)
    out[10 * half :] = jnp.zeros((out.shape[0] - 10 * half, wide), f32)


def lines_of(gathered, which):
    devices, _, wide = gathered.shape
    half = wide // 2
    at = which * 5 * half // 2
    blocks = {}
    for v, others in enumerate(senders(devices)):
        for j, u in enumerate([v, *others]):
            if j < 4:
                start = at + (j // 2) * half
                rows = gathered[v, start : start + half]
                block = rows[:, (j % 2) * half : (j % 2 + 1) * half]
            else:
                rows = gathered[v, at + wide : at + wide + half // 2]
                block = jnp.concatenate([rows[:, :half], rows[:, half:]], axis=0)
            blocks[v, u] = block
    for v in range(devices):
        for u in range(devices):
            if (v, u) not in blocks:
                blocks[v, u] = blocks[u, v].T
    return [
        jnp.concatenate([blocks[v, u] for u in range(devices)], axis=1) for v in range(devices)
    ]


def sum_kernel(parts, out):
    total = parts[0]
    for i in range(1, parts.shape[0]):
        total = total + parts[i]
    for i in range(out.shape[0]):
        out[i] = total


def multiply(a, b, dims):
    ah, al = split(a)
    bh, bl = split(b)
    dot = functools.partial(lax.dot_general, dimension_numbers=dims, preferred_element_type=f32)
    return dot(ah, bh) + (dot(al, bh) + dot(ah, bl))


def inverse_kernel(count, gathered, out, scaled, factor):
    n = out.shape[0]
    half = gathered.shape[2] // 2
    for v, line in enumerate(lines_of(gathered, 0)):
        scaled[v * half : (v + 1) * half, :] = line * (1.0 / count)
    rows = lax.broadcasted_iota(jnp.int32, (n, n), 0)
    cols = lax.broadcasted_iota(jnp.int32, (n, n), 1)
    on_diag = rows == cols
    weight = jnp.where(rows > cols, 1.0, jnp.where(on_diag, 0.5, 0.0))
    unit = jnp.where(on_diag, 1.0, 0.0)
    matrix = scaled[...]
    only_diag = jnp.where(on_diag, matrix, 0.0)
    scale_row = lax.rsqrt(jnp.sum(only_diag, axis=0, keepdims=True))
    scale_col = lax.rsqrt(jnp.sum(only_diag, axis=1, keepdims=True))
    matrix = matrix * scale_row * scale_col
    scaled[...] = matrix
    factor[...] = unit - weight * (matrix - unit)

    mid = n // 2
    dot = functools.partial(lax.dot_general, preferred_element_type=f32)
    square = (mid, mid)
    r, c = (lax.broadcasted_iota(jnp.int32, square, i) for i in range(2))
    small_weight = jnp.where(r > c, 1.0, jnp.where(r == c, 0.5, 0.0))
    small_unit = jnp.where(r == c, 1.0, 0.0)

    def improve(product, cut):
        s1 = cut(scaled[:, :mid])
        s2 = cut(scaled[:, mid:])
        top = cut(factor[:mid, :mid])
        side = cut(factor[mid:, :mid])
        low = cut(factor[mid:, mid:])
        lower = cut(factor[mid:, :])

        def part(x, piece):
            return tuple(y[piece] for y in x)

        t11 = cut(product(top, part(s1, slice(0, mid)), NN))
        t21 = cut(product(lower, s1, NN))
        t22 = cut(product(lower, s2, NN))
        e11 = product(t11, top, NT) - small_unit
        e21 = product(t21, top, NT)
        e22 = product(t21, side, NT) + product(t22, low, NT) - small_unit
        p11, p22 = small_weight * e11, small_weight * e22
        size = jnp.sum(p11 * p11 + p22 * p22 + e21 * e21)
        p11, p21, p22 = cut(p11), cut(e21), cut(p22)
        factor[:mid, :mid] = factor[:mid, :mid] - product(p11, top, NN)
        factor[mid:, :mid] = factor[mid:, :mid] - (
            product(p21, top, NN) + product(p22, side, NN)
        )
        factor[mid:, mid:] = factor[mid:, mid:] - product(p22, low, NN)
        return size

    def once(a, b, dims):
        return dot(a[0], b[0], dimension_numbers=dims)

    def thrice(a, b, dims):
        (ah, al), (bh, bl) = a, b
        return dot(ah, bh, dimension_numbers=dims) + (
            dot(al, bh, dimension_numbers=dims) + dot(ah, bl, dimension_numbers=dims)
        )

    improve(once, lambda x: (x.astype(bf16),))

    def go_on(state):
        step, size = state
        return jnp.logical_and(step < NEWTON_LIMIT, jnp.logical_not(size < NEWTON_DONE))

    def body(state):
        return state[0] + 1, improve(thrice, split)

    _, size = lax.while_loop(go_on, body, (jnp.int32(0), jnp.float32(1.0)))

    @pl.when(jnp.logical_not(size < NEWTON_DONE))
    def _():
        factor[...] = unit

        def eliminate(j, carry):
            pivot_row = scaled[pl.ds(j, 1), :]
            here = lax.broadcasted_iota(jnp.int32, (1, n), 1) == j
            pivot = jnp.sum(jnp.where(here, pivot_row, 0.0))
            a = scaled[...]
            column = jnp.sum(jnp.where(cols == j, a, 0.0), axis=1, keepdims=True) / pivot
            below = lax.broadcasted_iota(jnp.int32, (n, 1), 0) > j
            column = jnp.where(below, column, 0.0)
            r_row = factor[pl.ds(j, 1), :]
            scaled[...] = a - column * pivot_row
            factor[...] = factor[...] - column * r_row
            factor[pl.ds(j, 1), :] = r_row * lax.rsqrt(jnp.full_like(r_row, pivot))
            return carry

        lax.fori_loop(0, n, eliminate, 0)

    out[...] = factor[...] * scale_row


def basis_kernel(place, vectors, inverse, out):
    sites, columns, _ = out.shape
    mine = inverse[pl.ds(pl.multiple_of(place[0] * columns, columns), columns), :]
    for s in range(sites):
        block = jnp.concatenate(
            [vectors[u, s * columns : (s + 1) * columns] for u in range(vectors.shape[0])],
            axis=0,
        )
        out[s] = multiply(mine, block, NN)


def projected_kernel(count, place, gathered, inverse, out):
    half = gathered.shape[2] // 2
    moment = jnp.concatenate(lines_of(gathered, 1), axis=0)
    mine = inverse[pl.ds(pl.multiple_of(place[0] * half, half), half), :]
    half_way = multiply(mine, moment, NN)
    out[...] = multiply(half_way, inverse[...], NT) * (1.0 / count)


def passed_along(x, by):
    size = lax.axis_size("site")
    return lax.ppermute(x, "site", [(i, (i + by) % size) for i in range(size)])


def local(diag_blocks, hop_blocks, neighbors, start_basis):
    sites, both, cols = start_basis.shape
    half = both // 2
    devices = lax.axis_size("vec")
    slices = lax.axis_size("site")
    all_cols = cols * devices
    count = float(sites * both * slices)
    place = lax.axis_index("vec").astype(jnp.int32).reshape(1)
    shape = jax.ShapeDtypeStruct
    block = shape((sites, cols, both), f32)
    size = sites * cols * both * 4

    def matrices(blocks):
        return (shape((sites, blocks * both, both), bf16),) * 2

    def work(blocks):
        return sites * cols * blocks * 3 * both * both * 2

    current = jnp.swapaxes(start_basis, 1, 2)
    back, *back_mats = pl.pallas_call(
        backward_kernel,
        out_shape=(block, *matrices(1)),
        grid=(1,),
        in_specs=[
            pl.BlockSpec((sites, cols, both), lambda i: (0, 0, 0)),
            pl.BlockSpec((sites, 1, half, both), lambda i: (0, 3, 0, 0)),
        ],
        out_specs=(
            pl.BlockSpec((sites, cols, both), lambda i: (0, 0, 0)),
            *[pl.BlockSpec((sites, both, both), lambda i: (0, 0, 0))] * 2,
        ),
        compiler_params=pltpu.CompilerParams(vmem_limit_bytes=VMEM_WHOLE),
        cost_estimate=pl.CostEstimate(
            flops=work(1), bytes_accessed=4 * size, transcendentals=0
        ),
        name="backward",
    )(current, hop_blocks)
    mats = call(
        prepare_kernel,
        (*matrices(4), *matrices(1)),
        1,
        2,
        flops=1 << 24,
        moved=1 << 23,
        name="prepare",
    )(neighbors, diag_blocks, hop_blocks)
    own_mats, ahead_mats = mats[:2], mats[2:]

    def apply(vectors, back, mode, *more):
        ahead = passed_along(vectors, -1)
        received = passed_along(back, 1)
        own = call(
            own_kernel,
            block,
            1,
            3,
            scratch=[pltpu.VMEM((sites, 2 * cols, both), bf16)],
            flops=work(4),
            moved=8 * size,
            name="own_slice",
        )(neighbors, vectors, *own_mats)
        if mode != "image":
            more = (*more, *back_mats)
        return call(
            functools.partial(step_kernel, mode),
            block if mode == "image" else (block, block),
            1,
            5 + len(more),
            flops=work(1),
            moved=8 * size,
            name="next_slices",
        )(neighbors, own, ahead, received, *ahead_mats, *more)

    previous = current
    current, back = apply(current, back, "first")
    for _ in range(DEGREE - 1):
        following, back = apply(current, back, "next", previous)
        previous, current = current, following

    image = apply(current, back, "image", current)
    table = senders(devices)
    others = [
        lax.ppermute(current, "vec", [(table[v][i], v) for v in range(devices)]) for i in range(4)
    ]
    kept = 5 * cols // 2
    products = call(
        product_kernel,
        shape((slices * 8, both), f32),
        0,
        6,
        flops=6 * 5 * cols * 2 * cols * sites * both,
        moved=1 << 22,
        name="products",
    )(current, image, *others)
    flat, _ = lax.optimization_barrier((current.reshape(sites * cols, both), products))
    everything = lax.all_gather(flat, "vec", axis=0)

    parts = lax.all_to_all(products.reshape(slices, 8, both), "site", 0, 0, tiled=True)
    summed = call(
        sum_kernel, shape((slices, 8, both), f32), 0, 1, moved=1 << 19, name="sum_parts"
    )(parts)
    whole = lax.all_to_all(summed, "site", 0, 0, tiled=True).reshape(slices * 8, both)
    copies = call(
        repeat_kernel,
        shape((devices, 2 * kept, both), f32),
        0,
        1,
        moved=1 << 21,
        name="repeat",
    )(whole)
    copies, everything = lax.optimization_barrier((copies, everything))
    gathered = lax.all_to_all(copies, "vec", 0, 0, tiled=True)

    inverse = call(
        functools.partial(inverse_kernel, count),
        shape((all_cols, all_cols), f32),
        0,
        1,
        scratch=[pltpu.VMEM((all_cols, all_cols), f32)] * 2,
        flops=9 * 6 * all_cols**3,
        moved=1 << 21,
        name="inverse_factor",
    )(gathered)
    basis = call(
        basis_kernel,
        block,
        1,
        2,
        flops=6 * all_cols * cols * sites * both,
        moved=1 << 22,
        name="basis",
    )(place, everything, inverse)
    projected = call(
        functools.partial(projected_kernel, count),
        shape((cols, all_cols), f32),
        1,
        2,
        flops=12 * all_cols * all_cols * cols,
        moved=1 << 22,
        name="projected",
    )(place, gathered, inverse)
    return jnp.swapaxes(basis, 1, 2), projected.T


def solution(mesh):
    placed = (
        P("site", None, None),
        P("site", None, None, None),
        P("site", None),
        P("site", None, "vec"),
    )
    return jax.shard_map(
        local,
        mesh=mesh,
        in_specs=placed,
        out_specs=(P("site", None, "vec"), P(None, "vec")),
        check_vma=False,
    )
```

```python
import functools

import jax
import jax.numpy as jnp
from jax import lax
from jax.experimental import pallas as pl
from jax.experimental.pallas import tpu as pltpu
from jax.sharding import PartitionSpec as P

DEGREE = 4
CENTER = 3.7
RADIUS = 3.1
NEWTON_LIMIT = 12
NEWTON_DONE = 1e-6
VMEM_LIMIT = 44 * 1024 * 1024
VMEM_WHOLE = 44 * 1024 * 1024

f32 = jnp.float32
bf16 = jnp.bfloat16
VMEM_SPEC = pl.BlockSpec(memory_space=pltpu.VMEM)
SMEM_SPEC = pl.BlockSpec(memory_space=pltpu.SMEM)


def call(
    kernel,
    out_shape,
    n_smem,
    n_vmem,
    scratch=(),
    flops=0,
    moved=0,
    name=None,
):
    return pl.pallas_call(
        kernel,
        out_shape=out_shape,
        in_specs=[SMEM_SPEC] * n_smem + [VMEM_SPEC] * n_vmem,
        out_specs=jax.tree.map(lambda _: VMEM_SPEC, out_shape),
        scratch_shapes=list(scratch),
        compiler_params=pltpu.CompilerParams(vmem_limit_bytes=VMEM_LIMIT),
        cost_estimate=pl.CostEstimate(flops=flops, bytes_accessed=moved, transcendentals=0),
        name=name,
    )


def split(x):
    high = x.astype(bf16)
    return high, (x - high.astype(f32)).astype(bf16)


NT = (((1,), (1,)), ((), ()))
NN = (((1,), (0,)), ((), ()))


def stacked(x):
    return jnp.concatenate(split(x), axis=0)


def three_products(parts, high, low):
    m = parts.shape[0] // 2
    both = jnp.dot(parts, high, preferred_element_type=f32)
    return both[:m] + (both[m:] + jnp.dot(parts[:m], low, preferred_element_type=f32))


def low_lanes(shape):
    return lax.broadcasted_iota(jnp.int32, shape, len(shape) - 1) < shape[-1] // 2


def swapped(x):
    return pltpu.roll(x, x.shape[-1] // 2, axis=x.ndim - 1)


def transposed(block):
    turned = block.T
    half = turned.shape[0] // 2
    return jnp.concatenate([turned[:half], turned[half:]], axis=1)


def conjugated(block):
    return jnp.where(low_lanes(block.shape), block, -block)


def right_operand(block):
    turned = swapped(block)
    full = jnp.concatenate([block, jnp.where(low_lanes(block.shape), -turned, turned)], axis=0)
    return split(full * (1.0 / RADIUS))


def in_turn(place, forward, backward):
    even = place[0] % 2 == 0
    return jnp.where(even, forward, backward), jnp.where(even, backward, forward)


def backward_kernel(place, x, hop, first, second, high, low, hop_out):
    for s in range(x.shape[0]):
        high[s], low[s] = right_operand(conjugated(hop[s, 3]))
        vectors = x[s]
        back = three_products(stacked(vectors), high[s], low[s])
        first[s], second[s] = in_turn(place, vectors, back)
        hop_out[s] = hop[s]


def prepare_kernel(near, diag, hop, own_high, own_low, ahead_high, ahead_low):
    sites, half, wide = diag.shape
    rows = lax.broadcasted_iota(jnp.int32, (half, wide), 0)
    cols = lax.broadcasted_iota(jnp.int32, (half, wide), 1)
    unit = jnp.where(rows == cols, CENTER, 0.0)
    for s in range(sites):
        own_high[s, :wide], own_low[s, :wide] = right_operand(transposed(diag[s]) - unit)
        for d in range(3):
            place = slice((1 + d) * wide, (2 + d) * wide)
            other = hop[lax.rem(near[s, 4 + d], sites), d]
            own_high[s, place], own_low[s, place] = right_operand(
                transposed(hop[s, d]) + conjugated(other)
            )
        ahead_high[s], ahead_low[s] = right_operand(transposed(hop[s, 3]))


def own_kernel(near, x, high, low, out, spread):
    sites = x.shape[0]
    for n in range(sites):
        spread[n] = stacked(x[n])
    for s in range(sites):
        index = [s] + [lax.rem(near[s, d], sites) for d in range(3)]
        parts = jnp.concatenate([spread[n] for n in index], axis=1)
        out[s] = three_products(parts, high[s], low[s])


def step_kernel(mode, near, place, own, came_first, came_second, ahead_high, ahead_low, *rest):
    sites = own.shape[0]
    more = rest[0] if mode != "first" else None
    if mode == "image":
        out = rest[-1]
    else:
        back_high, back_low, out, first, second = rest[-5:]
    for s in range(sites):
        n, m = lax.rem(near[s, 3], sites), lax.rem(near[s, 7], sites)
        ahead, _ = in_turn(place, came_first[n], came_second[n])
        _, received = in_turn(place, came_first[m], came_second[m])
        part = three_products(stacked(ahead), ahead_high[s], ahead_low[s])
        applied = own[s] + (part + received)
        if mode == "first":
            out[s] = applied
        elif mode == "next":
            out[s] = 2.0 * applied - more[s]
        else:
            out[s] = RADIUS * applied + CENTER * more[s]
    if mode != "image":
        for s in range(sites):
            vectors = out[s]
            back = three_products(stacked(vectors), back_high[s], back_low[s])
            first[s], second[s] = in_turn(place, vectors, back)


def senders(devices):
    chips = devices // 2
    table = []
    for v in range(devices):
        x, c = v // 2, v % 2
        opposite = (x + chips // 2) % chips
        table.append(
            [
                2 * ((x - 1 + 2 * c) % chips) + c,
                2 * ((x + 1) % chips) + 1 - c,
                2 * x + 1 - c,
                2 * opposite + (1 - c if x < chips // 2 else c),
            ]
        )
    return table


def product_kernel(own, image, first, second, third, fourth, out):
    sites, cols, wide = own.shape

    def flat(ref):
        return jnp.concatenate([ref[s] for s in range(sites)], axis=1)

    f = flat(own)
    high, low = split(jnp.concatenate([f, flat(image)], axis=0))
    left = jnp.concatenate([high, low], axis=1)
    half = cols // 2
    dot = functools.partial(lax.dot_general, dimension_numbers=NT, preferred_element_type=f32)
    for p, group in enumerate(((own, first), (second, third), (fourth,))):
        h, l = split(jnp.concatenate([f if r is own else flat(r) for r in group], axis=0))
        tile = dot(left, jnp.concatenate([h, h], axis=1)) + dot(high, l)
        for i in range(2):
            part = tile[i * cols : (i + 1) * cols]
            start = i * (5 * half) + p * cols
            if len(group) == 2:
                out[start : start + cols] = part
            else:
                out[start : start + half] = jnp.concatenate([part[:half], part[half:]], axis=1)
    out[10 * half :] = jnp.zeros((out.shape[0] - 10 * half, wide), f32)


def lines_of(gathered):
    devices, _, wide = gathered.shape
    half = wide // 2
    blocks = {}
    for v, others in enumerate(senders(devices)):
        for j, u in enumerate([v, *others]):
            if j < 4:
                rows = gathered[v, (j // 2) * half : (j // 2 + 1) * half]
                block = rows[:, (j % 2) * half : (j % 2 + 1) * half]
            else:
                rows = gathered[v, wide : wide + half // 2]
                block = jnp.concatenate([rows[:, :half], rows[:, half:]], axis=0)
            blocks[v, u] = block
    for v in range(devices):
        for u in range(devices):
            if (v, u) not in blocks:
                blocks[v, u] = blocks[u, v].T
    return [
        jnp.concatenate([blocks[v, u] for u in range(devices)], axis=1) for v in range(devices)
    ]


def sum_kernel(parts, out):
    total = parts[0]
    for i in range(1, parts.shape[0]):
        total = total + parts[i]
    for i in range(out.shape[0]):
        out[i] = total


def multiply(a, b, dims):
    ah, al = split(a)
    bh, bl = split(b)
    dot = functools.partial(lax.dot_general, dimension_numbers=dims, preferred_element_type=f32)
    return dot(ah, bh) + (dot(al, bh) + dot(ah, bl))


def inverse_kernel(count, gathered, out, scaled, factor):
    n = out.shape[0]
    half = gathered.shape[2] // 2
    for v, line in enumerate(lines_of(gathered)):
        scaled[v * half : (v + 1) * half, :] = line * (1.0 / count)
    rows = lax.broadcasted_iota(jnp.int32, (n, n), 0)
    cols = lax.broadcasted_iota(jnp.int32, (n, n), 1)
    on_diag = rows == cols
    weight = jnp.where(rows > cols, 1.0, jnp.where(on_diag, 0.5, 0.0))
    unit = jnp.where(on_diag, 1.0, 0.0)
    matrix = scaled[...]
    only_diag = jnp.where(on_diag, matrix, 0.0)
    scale_row = lax.rsqrt(jnp.sum(only_diag, axis=0, keepdims=True))
    scale_col = lax.rsqrt(jnp.sum(only_diag, axis=1, keepdims=True))
    matrix = matrix * scale_row * scale_col
    scaled[...] = matrix
    factor[...] = unit - weight * (matrix - unit)

    mid = n // 2
    dot = functools.partial(lax.dot_general, preferred_element_type=f32)
    square = (mid, mid)
    r, c = (lax.broadcasted_iota(jnp.int32, square, i) for i in range(2))
    small_weight = jnp.where(r > c, 1.0, jnp.where(r == c, 0.5, 0.0))
    small_unit = jnp.where(r == c, 1.0, 0.0)

    def improve(product, cut):
        s1 = cut(scaled[:, :mid])
        s2 = cut(scaled[:, mid:])
        top = cut(factor[:mid, :mid])
        side = cut(factor[mid:, :mid])
        low = cut(factor[mid:, mid:])
        lower = cut(factor[mid:, :])

        def part(x, piece):
            return tuple(y[piece] for y in x)

        t11 = cut(product(top, part(s1, slice(0, mid)), NN))
        t21 = cut(product(lower, s1, NN))
        t22 = cut(product(lower, s2, NN))
        e11 = product(t11, top, NT) - small_unit
        e21 = product(t21, top, NT)
        e22 = product(t21, side, NT) + product(t22, low, NT) - small_unit
        p11, p22 = small_weight * e11, small_weight * e22
        size = jnp.sum(p11 * p11 + p22 * p22 + e21 * e21)
        p11, p21, p22 = cut(p11), cut(e21), cut(p22)
        factor[:mid, :mid] = factor[:mid, :mid] - product(p11, top, NN)
        factor[mid:, :mid] = factor[mid:, :mid] - (
            product(p21, top, NN) + product(p22, side, NN)
        )
        factor[mid:, mid:] = factor[mid:, mid:] - product(p22, low, NN)
        return size

    def once(a, b, dims):
        return dot(a[0], b[0], dimension_numbers=dims)

    def thrice(a, b, dims):
        (ah, al), (bh, bl) = a, b
        return dot(ah, bh, dimension_numbers=dims) + (
            dot(al, bh, dimension_numbers=dims) + dot(ah, bl, dimension_numbers=dims)
        )

    improve(once, lambda x: (x.astype(bf16),))

    def go_on(state):
        step, size = state
        return jnp.logical_and(step < NEWTON_LIMIT, jnp.logical_not(size < NEWTON_DONE))

    def body(state):
        return state[0] + 1, improve(thrice, split)

    _, size = lax.while_loop(go_on, body, (jnp.int32(0), jnp.float32(1.0)))

    @pl.when(jnp.logical_not(size < NEWTON_DONE))
    def _():
        factor[...] = unit

        def eliminate(j, carry):
            pivot_row = scaled[pl.ds(j, 1), :]
            here = lax.broadcasted_iota(jnp.int32, (1, n), 1) == j
            pivot = jnp.sum(jnp.where(here, pivot_row, 0.0))
            a = scaled[...]
            column = jnp.sum(jnp.where(cols == j, a, 0.0), axis=1, keepdims=True) / pivot
            below = lax.broadcasted_iota(jnp.int32, (n, 1), 0) > j
            column = jnp.where(below, column, 0.0)
            r_row = factor[pl.ds(j, 1), :]
            scaled[...] = a - column * pivot_row
            factor[...] = factor[...] - column * r_row
            factor[pl.ds(j, 1), :] = r_row * lax.rsqrt(jnp.full_like(r_row, pivot))
            return carry

        lax.fori_loop(0, n, eliminate, 0)

    out[...] = factor[...] * scale_row


def basis_kernel(place, vectors, inverse, out):
    sites, columns, _ = out.shape
    mine = inverse[pl.ds(pl.multiple_of(place[0] * columns, columns), columns), :]
    for s in range(sites):
        block = jnp.concatenate(
            [vectors[u, s * columns : (s + 1) * columns] for u in range(vectors.shape[0])],
            axis=0,
        )
        out[s] = multiply(mine, block, NN)


def projected_kernel(count, place, moments, inverse, out):
    half = moments.shape[2] // 2
    moment = jnp.concatenate(lines_of(moments), axis=0)
    mine = inverse[pl.ds(pl.multiple_of(place[0] * half, half), half), :]
    half_way = multiply(mine, moment, NN)
    out[...] = multiply(half_way, inverse[...], NT) * (1.0 / count)


def exchanged(first, second):
    slices, devices = lax.axis_size("site"), lax.axis_size("vec")

    def pairs(way):
        return [
            (s * devices + v, ((s + (way if v % 2 == 0 else -way)) % slices) * devices + v)
            for s in range(slices)
            for v in range(devices)
        ]

    axes = ("site", "vec")
    return lax.ppermute(first, axes, pairs(-1)), lax.ppermute(second, axes, pairs(1))


def local(diag_blocks, hop_blocks, neighbors, start_basis):
    sites, both, cols = start_basis.shape
    half = both // 2
    devices = lax.axis_size("vec")
    slices = lax.axis_size("site")
    all_cols = cols * devices
    count = float(sites * both * slices)
    place = lax.axis_index("vec").astype(jnp.int32).reshape(1)
    shape = jax.ShapeDtypeStruct
    block = shape((sites, cols, both), f32)
    size = sites * cols * both * 4

    def matrices(blocks):
        return (shape((sites, blocks * both, both), bf16),) * 2

    def work(blocks):
        return sites * cols * blocks * 3 * both * both * 2

    current = jnp.swapaxes(start_basis, 1, 2)
    first, second, *back_mats, links = call(
        backward_kernel,
        (block, block, *matrices(1), shape(hop_blocks.shape, f32)),
        1,
        2,
        flops=work(1),
        moved=8 * size,
        name="backward",
    )(place, current, hop_blocks)
    mats = call(
        prepare_kernel,
        (*matrices(4), *matrices(1)),
        1,
        2,
        flops=1 << 24,
        moved=1 << 23,
        name="prepare",
    )(neighbors, diag_blocks, links)
    own_mats, ahead_mats = mats[:2], mats[2:]

    def apply(vectors, sent, mode, *more):
        came = exchanged(*sent)
        own = call(
            own_kernel,
            block,
            1,
            3,
            scratch=[pltpu.VMEM((sites, 2 * cols, both), bf16)],
            flops=work(4),
            moved=8 * size,
            name="own_slice",
        )(neighbors, vectors, *own_mats)
        if mode != "image":
            more = (*more, *back_mats)
        return call(
            functools.partial(step_kernel, mode),
            block if mode == "image" else (block, block, block),
            2,
            5 + len(more),
            flops=work(1),
            moved=8 * size,
            name="next_slices",
        )(neighbors, place, own, *came, *ahead_mats, *more)

    previous = current
    current, *sent = apply(current, (first, second), "first")
    for _ in range(DEGREE - 1):
        following, *sent = apply(current, sent, "next", previous)
        previous, current = current, following

    image = apply(current, sent, "image", current)
    table = senders(devices)
    others = [
        lax.ppermute(current, "vec", [(table[v][i], v) for v in range(devices)]) for i in range(4)
    ]
    kept = 5 * cols // 2
    products = call(
        product_kernel,
        shape((slices * 8, both), f32),
        0,
        6,
        flops=6 * 5 * cols * 2 * cols * sites * both,
        moved=1 << 22,
        name="products",
    )(current, image, *others)
    flat, _ = lax.optimization_barrier((current.reshape(sites * cols, both), products))
    everything = lax.all_gather(flat, "vec", axis=0)

    parts = lax.all_to_all(products.reshape(slices, 8, both), "site", 0, 0, tiled=True)
    summed = call(
        sum_kernel, shape((slices, 8, both), f32), 0, 1, moved=1 << 19, name="sum_parts"
    )(parts)
    whole = lax.all_to_all(summed, "site", 0, 0, tiled=True).reshape(slices * 8, both)
    whole, everything = lax.optimization_barrier((whole, everything))
    moments = lax.all_gather(whole[kept : kept + all_cols // 2], "vec", axis=0)
    gram = lax.all_gather(whole[:kept], "vec", axis=0)

    inverse = call(
        functools.partial(inverse_kernel, count),
        shape((all_cols, all_cols), f32),
        0,
        1,
        scratch=[pltpu.VMEM((all_cols, all_cols), f32)] * 2,
        flops=9 * 6 * all_cols**3,
        moved=1 << 21,
        name="inverse_factor",
    )(gram)
    basis = call(
        basis_kernel,
        block,
        1,
        2,
        flops=6 * all_cols * cols * sites * both,
        moved=1 << 22,
        name="basis",
    )(place, everything, inverse)
    projected = call(
        functools.partial(projected_kernel, count),
        shape((cols, all_cols), f32),
        1,
        2,
        flops=12 * all_cols * all_cols * cols,
        moved=1 << 22,
        name="projected",
    )(place, moments, inverse)
    return jnp.swapaxes(basis, 1, 2), projected.T


def solution(mesh):
    placed = (
        P("site", None, None),
        P("site", None, None, None),
        P("site", None),
        P("site", None, "vec"),
    )
    return jax.shard_map(
        local,
        mesh=mesh,
        in_specs=placed,
        out_specs=(P("site", None, "vec"), P(None, "vec")),
        check_vma=False,
    )
```

```python
import functools

import jax
import jax.numpy as jnp
from jax import lax
from jax.experimental import pallas as pl
from jax.experimental.pallas import tpu as pltpu
from jax.sharding import PartitionSpec as P

DEGREE = 4
CENTER = 3.7
RADIUS = 3.1
NEWTON_LIMIT = 12
NEWTON_DONE = 1e-6
VMEM_LIMIT = 44 * 1024 * 1024
VMEM_WHOLE = 44 * 1024 * 1024

f32 = jnp.float32
bf16 = jnp.bfloat16
VMEM_SPEC = pl.BlockSpec(memory_space=pltpu.VMEM)
SMEM_SPEC = pl.BlockSpec(memory_space=pltpu.SMEM)


def call(
    kernel,
    out_shape,
    n_smem,
    n_vmem,
    scratch=(),
    flops=0,
    moved=0,
    name=None,
):
    return pl.pallas_call(
        kernel,
        out_shape=out_shape,
        in_specs=[SMEM_SPEC] * n_smem + [VMEM_SPEC] * n_vmem,
        out_specs=jax.tree.map(lambda _: VMEM_SPEC, out_shape),
        scratch_shapes=list(scratch),
        compiler_params=pltpu.CompilerParams(vmem_limit_bytes=VMEM_LIMIT),
        cost_estimate=pl.CostEstimate(flops=flops, bytes_accessed=moved, transcendentals=0),
        name=name,
    )


def split(x):
    high = x.astype(bf16)
    return high, (x - high.astype(f32)).astype(bf16)


NT = (((1,), (1,)), ((), ()))
NN = (((1,), (0,)), ((), ()))


def stacked(x):
    return jnp.concatenate(split(x), axis=0)


def three_products(parts, high, low):
    m = parts.shape[0] // 2
    both = jnp.dot(parts, high, preferred_element_type=f32)
    return both[:m] + (both[m:] + jnp.dot(parts[:m], low, preferred_element_type=f32))


def low_lanes(shape):
    return lax.broadcasted_iota(jnp.int32, shape, len(shape) - 1) < shape[-1] // 2


def swapped(x):
    return pltpu.roll(x, x.shape[-1] // 2, axis=x.ndim - 1)


def transposed(block):
    turned = block.T
    half = turned.shape[0] // 2
    return jnp.concatenate([turned[:half], turned[half:]], axis=1)


def conjugated(block):
    return jnp.where(low_lanes(block.shape), block, -block)


def right_operand(block):
    turned = swapped(block)
    full = jnp.concatenate([block, jnp.where(low_lanes(block.shape), -turned, turned)], axis=0)
    return split(full * (1.0 / RADIUS))


def backward_kernel(x, hop, out, high, low, hop_out):
    for s in range(x.shape[0]):
        high[s], low[s] = right_operand(conjugated(hop[s, 3]))
        out[s] = three_products(stacked(x[s]), high[s], low[s])
        hop_out[s] = hop[s]


def prepare_kernel(near, diag, hop, own_high, own_low, ahead_high, ahead_low):
    sites, half, wide = diag.shape
    rows = lax.broadcasted_iota(jnp.int32, (half, wide), 0)
    cols = lax.broadcasted_iota(jnp.int32, (half, wide), 1)
    unit = jnp.where(rows == cols, CENTER, 0.0)
    for s in range(sites):
        own_high[s, :wide], own_low[s, :wide] = right_operand(transposed(diag[s]) - unit)
        for d in range(3):
            place = slice((1 + d) * wide, (2 + d) * wide)
            other = hop[lax.rem(near[s, 4 + d], sites), d]
            own_high[s, place], own_low[s, place] = right_operand(
                transposed(hop[s, d]) + conjugated(other)
            )
        ahead_high[s], ahead_low[s] = right_operand(transposed(hop[s, 3]))


def own_kernel(near, x, high, low, out, spread):
    sites = x.shape[0]
    for n in range(sites):
        spread[n] = stacked(x[n])
    for s in range(sites):
        index = [s] + [lax.rem(near[s, d], sites) for d in range(3)]
        parts = jnp.concatenate([spread[n] for n in index], axis=1)
        out[s] = three_products(parts, high[s], low[s])


def step_kernel(mode, near, own, ahead, received, ahead_high, ahead_low, *rest):
    sites = own.shape[0]
    more = rest[0] if mode != "first" else None
    if mode == "image":
        out, back = rest[-1], None
    else:
        back_high, back_low, out, back = rest[-4:]
    for s in range(sites):
        parts = stacked(ahead[lax.rem(near[s, 3], sites)])
        part = three_products(parts, ahead_high[s], ahead_low[s])
        applied = own[s] + (part + received[lax.rem(near[s, 7], sites)])
        if mode == "first":
            out[s] = applied
        elif mode == "next":
            out[s] = 2.0 * applied - more[s]
        else:
            out[s] = RADIUS * applied + CENTER * more[s]
    if back is not None:
        for s in range(sites):
            back[s] = three_products(stacked(out[s]), back_high[s], back_low[s])


def senders(devices):
    chips = devices // 2
    table = []
    for v in range(devices):
        x, c = v // 2, v % 2
        opposite = (x + chips // 2) % chips
        table.append(
            [
                2 * ((x - 1 + 2 * c) % chips) + c,
                2 * ((x + 1) % chips) + 1 - c,
                2 * x + 1 - c,
                2 * opposite + (1 - c if x < chips // 2 else c),
            ]
        )
    return table


def product_kernel(own, image, first, second, third, fourth, out):
    sites, cols, wide = own.shape

    def flat(ref):
        return jnp.concatenate([ref[s] for s in range(sites)], axis=1)

    f = flat(own)
    high, low = split(jnp.concatenate([f, flat(image)], axis=0))
    left = jnp.concatenate([high, low], axis=1)
    half = cols // 2
    dot = functools.partial(lax.dot_general, dimension_numbers=NT, preferred_element_type=f32)
    for p, group in enumerate(((own, first), (second, third), (fourth,))):
        h, l = split(jnp.concatenate([f if r is own else flat(r) for r in group], axis=0))
        tile = dot(left, jnp.concatenate([h, h], axis=1)) + dot(high, l)
        for i in range(2):
            part = tile[i * cols : (i + 1) * cols]
            start = i * (5 * half) + p * cols
            if len(group) == 2:
                out[start : start + cols] = part
            else:
                out[start : start + half] = jnp.concatenate([part[:half], part[half:]], axis=1)
    out[10 * half :] = jnp.zeros((out.shape[0] - 10 * half, wide), f32)


def lines_of(gathered):
    devices, _, wide = gathered.shape
    half = wide // 2
    blocks = {}
    for v, others in enumerate(senders(devices)):
        for j, u in enumerate([v, *others]):
            if j < 4:
                rows = gathered[v, (j // 2) * half : (j // 2 + 1) * half]
                block = rows[:, (j % 2) * half : (j % 2 + 1) * half]
            else:
                rows = gathered[v, wide : wide + half // 2]
                block = jnp.concatenate([rows[:, :half], rows[:, half:]], axis=0)
            blocks[v, u] = block
    for v in range(devices):
        for u in range(devices):
            if (v, u) not in blocks:
                blocks[v, u] = blocks[u, v].T
    return [
        jnp.concatenate([blocks[v, u] for u in range(devices)], axis=1) for v in range(devices)
    ]


def sum_kernel(parts, out):
    total = parts[0]
    for i in range(1, parts.shape[0]):
        total = total + parts[i]
    for i in range(out.shape[0]):
        out[i] = total


def multiply(a, b, dims):
    ah, al = split(a)
    bh, bl = split(b)
    dot = functools.partial(lax.dot_general, dimension_numbers=dims, preferred_element_type=f32)
    return dot(ah, bh) + (dot(al, bh) + dot(ah, bl))


def inverse_kernel(count, gathered, out, scaled, factor):
    n = out.shape[0]
    half = gathered.shape[2] // 2
    for v, line in enumerate(lines_of(gathered)):
        scaled[v * half : (v + 1) * half, :] = line * (1.0 / count)
    rows = lax.broadcasted_iota(jnp.int32, (n, n), 0)
    cols = lax.broadcasted_iota(jnp.int32, (n, n), 1)
    on_diag = rows == cols
    weight = jnp.where(rows > cols, 1.0, jnp.where(on_diag, 0.5, 0.0))
    unit = jnp.where(on_diag, 1.0, 0.0)
    matrix = scaled[...]
    only_diag = jnp.where(on_diag, matrix, 0.0)
    scale_row = lax.rsqrt(jnp.sum(only_diag, axis=0, keepdims=True))
    scale_col = lax.rsqrt(jnp.sum(only_diag, axis=1, keepdims=True))
    matrix = matrix * scale_row * scale_col
    scaled[...] = matrix
    factor[...] = unit - weight * (matrix - unit)

    mid = n // 2
    dot = functools.partial(lax.dot_general, preferred_element_type=f32)
    square = (mid, mid)
    r, c = (lax.broadcasted_iota(jnp.int32, square, i) for i in range(2))
    small_weight = jnp.where(r > c, 1.0, jnp.where(r == c, 0.5, 0.0))
    small_unit = jnp.where(r == c, 1.0, 0.0)

    def improve(product, cut):
        s1 = cut(scaled[:, :mid])
        s2 = cut(scaled[:, mid:])
        top = cut(factor[:mid, :mid])
        side = cut(factor[mid:, :mid])
        low = cut(factor[mid:, mid:])
        lower = cut(factor[mid:, :])

        def part(x, piece):
            return tuple(y[piece] for y in x)

        t11 = cut(product(top, part(s1, slice(0, mid)), NN))
        t21 = cut(product(lower, s1, NN))
        t22 = cut(product(lower, s2, NN))
        e11 = product(t11, top, NT) - small_unit
        e21 = product(t21, top, NT)
        e22 = product(t21, side, NT) + product(t22, low, NT) - small_unit
        p11, p22 = small_weight * e11, small_weight * e22
        size = jnp.sum(p11 * p11 + p22 * p22 + e21 * e21)
        p11, p21, p22 = cut(p11), cut(e21), cut(p22)
        factor[:mid, :mid] = factor[:mid, :mid] - product(p11, top, NN)
        factor[mid:, :mid] = factor[mid:, :mid] - (
            product(p21, top, NN) + product(p22, side, NN)
        )
        factor[mid:, mid:] = factor[mid:, mid:] - product(p22, low, NN)
        return size

    def once(a, b, dims):
        return dot(a[0], b[0], dimension_numbers=dims)

    def thrice(a, b, dims):
        (ah, al), (bh, bl) = a, b
        return dot(ah, bh, dimension_numbers=dims) + (
            dot(al, bh, dimension_numbers=dims) + dot(ah, bl, dimension_numbers=dims)
        )

    improve(once, lambda x: (x.astype(bf16),))

    def go_on(state):
        step, size = state
        return jnp.logical_and(step < NEWTON_LIMIT, jnp.logical_not(size < NEWTON_DONE))

    def body(state):
        return state[0] + 1, improve(thrice, split)

    _, size = lax.while_loop(go_on, body, (jnp.int32(0), jnp.float32(1.0)))

    @pl.when(jnp.logical_not(size < NEWTON_DONE))
    def _():
        factor[...] = unit

        def eliminate(j, carry):
            pivot_row = scaled[pl.ds(j, 1), :]
            here = lax.broadcasted_iota(jnp.int32, (1, n), 1) == j
            pivot = jnp.sum(jnp.where(here, pivot_row, 0.0))
            a = scaled[...]
            column = jnp.sum(jnp.where(cols == j, a, 0.0), axis=1, keepdims=True) / pivot
            below = lax.broadcasted_iota(jnp.int32, (n, 1), 0) > j
            column = jnp.where(below, column, 0.0)
            r_row = factor[pl.ds(j, 1), :]
            scaled[...] = a - column * pivot_row
            factor[...] = factor[...] - column * r_row
            factor[pl.ds(j, 1), :] = r_row * lax.rsqrt(jnp.full_like(r_row, pivot))
            return carry

        lax.fori_loop(0, n, eliminate, 0)

    out[...] = factor[...] * scale_row


def basis_kernel(place, vectors, inverse, out):
    sites, columns, _ = out.shape
    mine = inverse[pl.ds(pl.multiple_of(place[0] * columns, columns), columns), :]
    for s in range(sites):
        block = jnp.concatenate(
            [vectors[u, s * columns : (s + 1) * columns] for u in range(vectors.shape[0])],
            axis=0,
        )
        out[s] = multiply(mine, block, NN)


def projected_kernel(count, place, moments, inverse, out):
    half = moments.shape[2] // 2
    moment = jnp.concatenate(lines_of(moments), axis=0)
    mine = inverse[pl.ds(pl.multiple_of(place[0] * half, half), half), :]
    half_way = multiply(mine, moment, NN)
    out[...] = multiply(half_way, inverse[...], NT) * (1.0 / count)


def passed_along(x, by):
    size = lax.axis_size("site")
    return lax.ppermute(x, "site", [(i, (i + by) % size) for i in range(size)])


def local(diag_blocks, hop_blocks, neighbors, start_basis):
    sites, both, cols = start_basis.shape
    half = both // 2
    devices = lax.axis_size("vec")
    slices = lax.axis_size("site")
    all_cols = cols * devices
    count = float(sites * both * slices)
    place = lax.axis_index("vec").astype(jnp.int32).reshape(1)
    shape = jax.ShapeDtypeStruct
    block = shape((sites, cols, both), f32)
    size = sites * cols * both * 4

    def matrices(blocks):
        return (shape((sites, blocks * both, both), bf16),) * 2

    def work(blocks):
        return sites * cols * blocks * 3 * both * both * 2

    current = jnp.swapaxes(start_basis, 1, 2)
    back, *back_mats, links = call(
        backward_kernel,
        (block, *matrices(1), shape(hop_blocks.shape, f32)),
        0,
        2,
        flops=work(1),
        moved=8 * size,
        name="backward",
    )(current, hop_blocks)
    mats = call(
        prepare_kernel,
        (*matrices(4), *matrices(1)),
        1,
        2,
        flops=1 << 24,
        moved=1 << 23,
        name="prepare",
    )(neighbors, diag_blocks, links)
    own_mats, ahead_mats = mats[:2], mats[2:]

    def apply(vectors, back, mode, *more):
        ahead = passed_along(vectors, -1)
        received = passed_along(back, 1)
        own = call(
            own_kernel,
            block,
            1,
            3,
            scratch=[pltpu.VMEM((sites, 2 * cols, both), bf16)],
            flops=work(4),
            moved=8 * size,
            name="own_slice",
        )(neighbors, vectors, *own_mats)
        if mode != "image":
            more = (*more, *back_mats)
        return call(
            functools.partial(step_kernel, mode),
            block if mode == "image" else (block, block),
            1,
            5 + len(more),
            flops=work(1),
            moved=8 * size,
            name="next_slices",
        )(neighbors, own, ahead, received, *ahead_mats, *more)

    previous = current
    current, back = apply(current, back, "first")
    for _ in range(DEGREE - 1):
        following, back = apply(current, back, "next", previous)
        previous, current = current, following

    image = apply(current, back, "image", current)
    table = senders(devices)
    others = [
        lax.ppermute(current, "vec", [(table[v][i], v) for v in range(devices)]) for i in range(4)
    ]
    kept = 5 * cols // 2
    products = call(
        product_kernel,
        shape((slices * 8, both), f32),
        0,
        6,
        flops=6 * 5 * cols * 2 * cols * sites * both,
        moved=1 << 22,
        name="products",
    )(current, image, *others)
    flat, _ = lax.optimization_barrier((current.reshape(sites * cols, both), products))
    everything = lax.all_gather(flat, "vec", axis=0)

    parts = lax.all_to_all(products.reshape(slices, 8, both), "site", 0, 0, tiled=True)
    summed = call(
        sum_kernel, shape((slices, 8, both), f32), 0, 1, moved=1 << 19, name="sum_parts"
    )(parts)
    whole = lax.all_to_all(summed, "site", 0, 0, tiled=True).reshape(slices * 8, both)
    whole, everything = lax.optimization_barrier((whole, everything))
    moments = lax.all_gather(whole[kept : kept + all_cols // 2], "vec", axis=0)
    gram = lax.all_gather(whole[:kept], "vec", axis=0)

    inverse = call(
        functools.partial(inverse_kernel, count),
        shape((all_cols, all_cols), f32),
        0,
        1,
        scratch=[pltpu.VMEM((all_cols, all_cols), f32)] * 2,
        flops=9 * 6 * all_cols**3,
        moved=1 << 21,
        name="inverse_factor",
    )(gram)
    basis = call(
        basis_kernel,
        block,
        1,
        2,
        flops=6 * all_cols * cols * sites * both,
        moved=1 << 22,
        name="basis",
    )(place, everything, inverse)
    projected = call(
        functools.partial(projected_kernel, count),
        shape((cols, all_cols), f32),
        1,
        2,
        flops=12 * all_cols * all_cols * cols,
        moved=1 << 22,
        name="projected",
    )(place, moments, inverse)
    return jnp.swapaxes(basis, 1, 2), projected.T


def solution(mesh):
    placed = (
        P("site", None, None),
        P("site", None, None, None),
        P("site", None),
        P("site", None, "vec"),
    )
    return jax.shard_map(
        local,
        mesh=mesh,
        in_specs=placed,
        out_specs=(P("site", None, "vec"), P(None, "vec")),
        check_vma=False,
    )
```

```python
import functools

import jax
import jax.numpy as jnp
from jax import lax
from jax.experimental import pallas as pl
from jax.experimental.pallas import tpu as pltpu
from jax.sharding import PartitionSpec as P

DEGREE = 4
CENTER = 3.7
RADIUS = 3.1
NEWTON_LIMIT = 12
NEWTON_DONE = 1e-6
VMEM_LIMIT = 44 * 1024 * 1024
VMEM_WHOLE = 44 * 1024 * 1024

f32 = jnp.float32
bf16 = jnp.bfloat16
VMEM_SPEC = pl.BlockSpec(memory_space=pltpu.VMEM)
SMEM_SPEC = pl.BlockSpec(memory_space=pltpu.SMEM)


def call(
    kernel,
    out_shape,
    n_smem,
    n_vmem,
    scratch=(),
    flops=0,
    moved=0,
    name=None,
):
    return pl.pallas_call(
        kernel,
        out_shape=out_shape,
        in_specs=[SMEM_SPEC] * n_smem + [VMEM_SPEC] * n_vmem,
        out_specs=jax.tree.map(lambda _: VMEM_SPEC, out_shape),
        scratch_shapes=list(scratch),
        compiler_params=pltpu.CompilerParams(vmem_limit_bytes=VMEM_LIMIT),
        cost_estimate=pl.CostEstimate(flops=flops, bytes_accessed=moved, transcendentals=0),
        name=name,
    )


def split(x):
    high = x.astype(bf16)
    return high, (x - high.astype(f32)).astype(bf16)


NT = (((1,), (1,)), ((), ()))
NN = (((1,), (0,)), ((), ()))


def stacked(x):
    return jnp.concatenate(split(x), axis=0)


def three_products(parts, high, low):
    m = parts.shape[0] // 2
    both = jnp.dot(parts, high, preferred_element_type=f32)
    return both[:m] + (both[m:] + jnp.dot(parts[:m], low, preferred_element_type=f32))


def low_lanes(shape):
    return lax.broadcasted_iota(jnp.int32, shape, len(shape) - 1) < shape[-1] // 2


def swapped(x):
    return pltpu.roll(x, x.shape[-1] // 2, axis=x.ndim - 1)


def transposed(block):
    turned = block.T
    half = turned.shape[0] // 2
    return jnp.concatenate([turned[:half], turned[half:]], axis=1)


def conjugated(block):
    return jnp.where(low_lanes(block.shape), block, -block)


def right_operand(block):
    turned = swapped(block)
    full = jnp.concatenate([block, jnp.where(low_lanes(block.shape), -turned, turned)], axis=0)
    return split(full * (1.0 / RADIUS))


def backward_kernel(x, hop, out, high, low, hop_out):
    for s in range(x.shape[0]):
        high[s], low[s] = right_operand(conjugated(hop[s, 3]))
        out[s] = three_products(stacked(x[s]), high[s], low[s])
        hop_out[s] = hop[s]


def prepare_kernel(near, diag, hop, own_high, own_low, ahead_high, ahead_low):
    sites, half, wide = diag.shape
    rows = lax.broadcasted_iota(jnp.int32, (half, wide), 0)
    cols = lax.broadcasted_iota(jnp.int32, (half, wide), 1)
    unit = jnp.where(rows == cols, CENTER, 0.0)
    for s in range(sites):
        own_high[s, :wide], own_low[s, :wide] = right_operand(transposed(diag[s]) - unit)
        for d in range(3):
            place = slice((1 + d) * wide, (2 + d) * wide)
            other = hop[lax.rem(near[s, 4 + d], sites), d]
            own_high[s, place], own_low[s, place] = right_operand(
                transposed(hop[s, d]) + conjugated(other)
            )
        ahead_high[s], ahead_low[s] = right_operand(transposed(hop[s, 3]))


def own_kernel(near, x, high, low, out, spread):
    sites = x.shape[0]
    for n in range(sites):
        spread[n] = stacked(x[n])
    for s in range(sites):
        index = [s] + [lax.rem(near[s, d], sites) for d in range(3)]
        parts = jnp.concatenate([spread[n] for n in index], axis=1)
        out[s] = three_products(parts, high[s], low[s])


def step_kernel(mode, near, own, ahead, received, ahead_high, ahead_low, *rest):
    sites = own.shape[0]
    more = rest[0] if mode != "first" else None
    if mode == "image":
        out, back = rest[-1], None
    else:
        back_high, back_low, out, back = rest[-4:]
    for s in range(sites):
        parts = stacked(ahead[lax.rem(near[s, 3], sites)])
        part = three_products(parts, ahead_high[s], ahead_low[s])
        applied = own[s] + (part + received[lax.rem(near[s, 7], sites)])
        if mode == "first":
            out[s] = applied
        elif mode == "next":
            out[s] = 2.0 * applied - more[s]
        else:
            out[s] = RADIUS * applied + CENTER * more[s]
    if back is not None:
        for s in range(sites):
            back[s] = three_products(stacked(out[s]), back_high[s], back_low[s])


def senders(devices):
    chips = devices // 2
    table = []
    for v in range(devices):
        x, c = v // 2, v % 2
        opposite = (x + chips // 2) % chips
        table.append(
            [
                2 * opposite + (1 - c if x < chips // 2 else c),
                2 * ((x + 1) % chips) + 1 - c,
                2 * ((x - 1 + 2 * c) % chips) + c,
                2 * x + 1 - c,
            ]
        )
    return table


def product_kernel(own, image, first, second, third, fourth, out):
    sites, cols, wide = own.shape

    def flat(ref):
        return jnp.concatenate([ref[s] for s in range(sites)], axis=1)

    f = flat(own)
    high, low = split(jnp.concatenate([f, flat(image)], axis=0))
    left = jnp.concatenate([high, low], axis=1)
    half = cols // 2
    dot = functools.partial(lax.dot_general, dimension_numbers=NT, preferred_element_type=f32)
    for p, group in enumerate(((own, first), (second, third), (fourth,))):
        h, l = split(jnp.concatenate([f if r is own else flat(r) for r in group], axis=0))
        tile = dot(left, jnp.concatenate([h, h], axis=1)) + dot(high, l)
        for i in range(2):
            part = tile[i * cols : (i + 1) * cols]
            start = i * (5 * half) + p * cols
            if len(group) == 2:
                out[start : start + cols] = part
            else:
                out[start : start + half] = jnp.concatenate([part[:half], part[half:]], axis=1)
    out[10 * half :] = jnp.zeros((out.shape[0] - 10 * half, wide), f32)


def lines_of(gathered):
    devices, _, wide = gathered.shape
    half = wide // 2
    blocks = {}
    for v, others in enumerate(senders(devices)):
        for j, u in enumerate([v, *others]):
            if j < 4:
                rows = gathered[v, (j // 2) * half : (j // 2 + 1) * half]
                block = rows[:, (j % 2) * half : (j % 2 + 1) * half]
            else:
                rows = gathered[v, wide : wide + half // 2]
                block = jnp.concatenate([rows[:, :half], rows[:, half:]], axis=0)
            blocks[v, u] = block
    for v in range(devices):
        for u in range(devices):
            if (v, u) not in blocks:
                blocks[v, u] = blocks[u, v].T
    return [
        jnp.concatenate([blocks[v, u] for u in range(devices)], axis=1) for v in range(devices)
    ]


def sum_kernel(parts, out):
    total = parts[0]
    for i in range(1, parts.shape[0]):
        total = total + parts[i]
    for i in range(out.shape[0]):
        out[i] = total


def multiply(a, b, dims):
    ah, al = split(a)
    bh, bl = split(b)
    dot = functools.partial(lax.dot_general, dimension_numbers=dims, preferred_element_type=f32)
    return dot(ah, bh) + (dot(al, bh) + dot(ah, bl))


def inverse_kernel(count, gathered, out, scaled, factor):
    n = out.shape[0]
    half = gathered.shape[2] // 2
    for v, line in enumerate(lines_of(gathered)):
        scaled[v * half : (v + 1) * half, :] = line * (1.0 / count)
    rows = lax.broadcasted_iota(jnp.int32, (n, n), 0)
    cols = lax.broadcasted_iota(jnp.int32, (n, n), 1)
    on_diag = rows == cols
    weight = jnp.where(rows > cols, 1.0, jnp.where(on_diag, 0.5, 0.0))
    unit = jnp.where(on_diag, 1.0, 0.0)
    matrix = scaled[...]
    only_diag = jnp.where(on_diag, matrix, 0.0)
    scale_row = lax.rsqrt(jnp.sum(only_diag, axis=0, keepdims=True))
    scale_col = lax.rsqrt(jnp.sum(only_diag, axis=1, keepdims=True))
    matrix = matrix * scale_row * scale_col
    scaled[...] = matrix
    factor[...] = unit - weight * (matrix - unit)

    mid = n // 2
    dot = functools.partial(lax.dot_general, preferred_element_type=f32)
    square = (mid, mid)
    r, c = (lax.broadcasted_iota(jnp.int32, square, i) for i in range(2))
    small_weight = jnp.where(r > c, 1.0, jnp.where(r == c, 0.5, 0.0))
    small_unit = jnp.where(r == c, 1.0, 0.0)

    def improve(product, cut):
        s1 = cut(scaled[:, :mid])
        s2 = cut(scaled[:, mid:])
        top = cut(factor[:mid, :mid])
        side = cut(factor[mid:, :mid])
        low = cut(factor[mid:, mid:])
        lower = cut(factor[mid:, :])

        def part(x, piece):
            return tuple(y[piece] for y in x)

        t11 = cut(product(top, part(s1, slice(0, mid)), NN))
        t21 = cut(product(lower, s1, NN))
        t22 = cut(product(lower, s2, NN))
        e11 = product(t11, top, NT) - small_unit
        e21 = product(t21, top, NT)
        e22 = product(t21, side, NT) + product(t22, low, NT) - small_unit
        p11, p22 = small_weight * e11, small_weight * e22
        size = jnp.sum(p11 * p11 + p22 * p22 + e21 * e21)
        p11, p21, p22 = cut(p11), cut(e21), cut(p22)
        factor[:mid, :mid] = factor[:mid, :mid] - product(p11, top, NN)
        factor[mid:, :mid] = factor[mid:, :mid] - (
            product(p21, top, NN) + product(p22, side, NN)
        )
        factor[mid:, mid:] = factor[mid:, mid:] - product(p22, low, NN)
        return size

    def once(a, b, dims):
        return dot(a[0], b[0], dimension_numbers=dims)

    def thrice(a, b, dims):
        (ah, al), (bh, bl) = a, b
        return dot(ah, bh, dimension_numbers=dims) + (
            dot(al, bh, dimension_numbers=dims) + dot(ah, bl, dimension_numbers=dims)
        )

    improve(once, lambda x: (x.astype(bf16),))

    def go_on(state):
        step, size = state
        return jnp.logical_and(step < NEWTON_LIMIT, jnp.logical_not(size < NEWTON_DONE))

    def body(state):
        return state[0] + 1, improve(thrice, split)

    _, size = lax.while_loop(go_on, body, (jnp.int32(0), jnp.float32(1.0)))

    @pl.when(jnp.logical_not(size < NEWTON_DONE))
    def _():
        factor[...] = unit

        def eliminate(j, carry):
            pivot_row = scaled[pl.ds(j, 1), :]
            here = lax.broadcasted_iota(jnp.int32, (1, n), 1) == j
            pivot = jnp.sum(jnp.where(here, pivot_row, 0.0))
            a = scaled[...]
            column = jnp.sum(jnp.where(cols == j, a, 0.0), axis=1, keepdims=True) / pivot
            below = lax.broadcasted_iota(jnp.int32, (n, 1), 0) > j
            column = jnp.where(below, column, 0.0)
            r_row = factor[pl.ds(j, 1), :]
            scaled[...] = a - column * pivot_row
            factor[...] = factor[...] - column * r_row
            factor[pl.ds(j, 1), :] = r_row * lax.rsqrt(jnp.full_like(r_row, pivot))
            return carry

        lax.fori_loop(0, n, eliminate, 0)

    out[...] = factor[...] * scale_row


def basis_kernel(place, vectors, inverse, out):
    sites, columns, _ = out.shape
    mine = inverse[pl.ds(pl.multiple_of(place[0] * columns, columns), columns), :]
    for s in range(sites):
        block = jnp.concatenate(
            [vectors[u, s * columns : (s + 1) * columns] for u in range(vectors.shape[0])],
            axis=0,
        )
        out[s] = multiply(mine, block, NN)


def projected_kernel(count, place, moments, inverse, out):
    half = moments.shape[2] // 2
    moment = jnp.concatenate(lines_of(moments), axis=0)
    mine = inverse[pl.ds(pl.multiple_of(place[0] * half, half), half), :]
    half_way = multiply(mine, moment, NN)
    out[...] = multiply(half_way, inverse[...], NT) * (1.0 / count)


def passed_along(x, by):
    size = lax.axis_size("site")
    return lax.ppermute(x, "site", [(i, (i + by) % size) for i in range(size)])


def local(diag_blocks, hop_blocks, neighbors, start_basis):
    sites, both, cols = start_basis.shape
    half = both // 2
    devices = lax.axis_size("vec")
    slices = lax.axis_size("site")
    all_cols = cols * devices
    count = float(sites * both * slices)
    place = lax.axis_index("vec").astype(jnp.int32).reshape(1)
    shape = jax.ShapeDtypeStruct
    block = shape((sites, cols, both), f32)
    size = sites * cols * both * 4

    def matrices(blocks):
        return (shape((sites, blocks * both, both), bf16),) * 2

    def work(blocks):
        return sites * cols * blocks * 3 * both * both * 2

    current = jnp.swapaxes(start_basis, 1, 2)
    back, *back_mats, links = call(
        backward_kernel,
        (block, *matrices(1), shape(hop_blocks.shape, f32)),
        0,
        2,
        flops=work(1),
        moved=8 * size,
        name="backward",
    )(current, hop_blocks)
    mats = call(
        prepare_kernel,
        (*matrices(4), *matrices(1)),
        1,
        2,
        flops=1 << 24,
        moved=1 << 23,
        name="prepare",
    )(neighbors, diag_blocks, links)
    own_mats, ahead_mats = mats[:2], mats[2:]

    def apply(vectors, back, mode, *more):
        ahead = passed_along(vectors, -1)
        received = passed_along(back, 1)
        own = call(
            own_kernel,
            block,
            1,
            3,
            scratch=[pltpu.VMEM((sites, 2 * cols, both), bf16)],
            flops=work(4),
            moved=8 * size,
            name="own_slice",
        )(neighbors, vectors, *own_mats)
        if mode != "image":
            more = (*more, *back_mats)
        return call(
            functools.partial(step_kernel, mode),
            block if mode == "image" else (block, block),
            1,
            5 + len(more),
            flops=work(1),
            moved=8 * size,
            name="next_slices",
        )(neighbors, own, ahead, received, *ahead_mats, *more)

    previous = current
    current, back = apply(current, back, "first")
    for _ in range(DEGREE - 1):
        following, back = apply(current, back, "next", previous)
        previous, current = current, following

    image = apply(current, back, "image", current)
    table = senders(devices)
    others = [
        lax.ppermute(current, "vec", [(table[v][i], v) for v in range(devices)]) for i in range(4)
    ]
    kept = 5 * cols // 2
    products = call(
        product_kernel,
        shape((slices * 8, both), f32),
        0,
        6,
        flops=6 * 5 * cols * 2 * cols * sites * both,
        moved=1 << 22,
        name="products",
    )(current, image, *others)
    flat, _ = lax.optimization_barrier((current.reshape(sites * cols, both), products))
    everything = lax.all_gather(flat, "vec", axis=0)

    parts = lax.all_to_all(products.reshape(slices, 8, both), "site", 0, 0, tiled=True)
    summed = call(
        sum_kernel, shape((slices, 8, both), f32), 0, 1, moved=1 << 19, name="sum_parts"
    )(parts)
    whole = lax.all_to_all(summed, "site", 0, 0, tiled=True).reshape(slices * 8, both)
    whole, everything = lax.optimization_barrier((whole, everything))
    moments = lax.all_gather(whole[kept : kept + all_cols // 2], "vec", axis=0)
    gram = lax.all_gather(whole[:kept], "vec", axis=0)

    inverse = call(
        functools.partial(inverse_kernel, count),
        shape((all_cols, all_cols), f32),
        0,
        1,
        scratch=[pltpu.VMEM((all_cols, all_cols), f32)] * 2,
        flops=9 * 6 * all_cols**3,
        moved=1 << 21,
        name="inverse_factor",
    )(gram)
    basis = call(
        basis_kernel,
        block,
        1,
        2,
        flops=6 * all_cols * cols * sites * both,
        moved=1 << 22,
        name="basis",
    )(place, everything, inverse)
    projected = call(
        functools.partial(projected_kernel, count),
        shape((cols, all_cols), f32),
        1,
        2,
        flops=12 * all_cols * all_cols * cols,
        moved=1 << 22,
        name="projected",
    )(place, moments, inverse)
    return jnp.swapaxes(basis, 1, 2), projected.T


def solution(mesh):
    placed = (
        P("site", None, None),
        P("site", None, None, None),
        P("site", None),
        P("site", None, "vec"),
    )
    return jax.shard_map(
        local,
        mesh=mesh,
        in_specs=placed,
        out_specs=(P("site", None, "vec"), P(None, "vec")),
        check_vma=False,
    )
```

```python
import functools

import jax
import jax.numpy as jnp
from jax import lax
from jax.experimental import pallas as pl
from jax.experimental.pallas import tpu as pltpu
from jax.sharding import PartitionSpec as P

DEGREE = 4
CENTER = 3.7
RADIUS = 3.1
NEWTON_LIMIT = 12
NEWTON_DONE = 1e-6
VMEM_LIMIT = 44 * 1024 * 1024
VMEM_WHOLE = 44 * 1024 * 1024

f32 = jnp.float32
bf16 = jnp.bfloat16
VMEM_SPEC = pl.BlockSpec(memory_space=pltpu.VMEM)
SMEM_SPEC = pl.BlockSpec(memory_space=pltpu.SMEM)


def call(
    kernel,
    out_shape,
    n_smem,
    n_vmem,
    scratch=(),
    flops=0,
    moved=0,
    name=None,
):
    return pl.pallas_call(
        kernel,
        out_shape=out_shape,
        in_specs=[SMEM_SPEC] * n_smem + [VMEM_SPEC] * n_vmem,
        out_specs=jax.tree.map(lambda _: VMEM_SPEC, out_shape),
        scratch_shapes=list(scratch),
        compiler_params=pltpu.CompilerParams(vmem_limit_bytes=VMEM_LIMIT),
        cost_estimate=pl.CostEstimate(flops=flops, bytes_accessed=moved, transcendentals=0),
        name=name,
    )


def split(x):
    high = x.astype(bf16)
    return high, (x - high.astype(f32)).astype(bf16)


def repeat_kernel(start, x, out):
    for i in range(out.shape[0]):
        out[i] = x[start : start + out.shape[1]]


NT = (((1,), (1,)), ((), ()))
NN = (((1,), (0,)), ((), ()))


def stacked(x):
    return jnp.concatenate(split(x), axis=0)


def three_products(parts, high, low):
    m = parts.shape[0] // 2
    both = jnp.dot(parts, high, preferred_element_type=f32)
    return both[:m] + (both[m:] + jnp.dot(parts[:m], low, preferred_element_type=f32))


def low_lanes(shape):
    return lax.broadcasted_iota(jnp.int32, shape, len(shape) - 1) < shape[-1] // 2


def swapped(x):
    return pltpu.roll(x, x.shape[-1] // 2, axis=x.ndim - 1)


def transposed(block):
    turned = block.T
    half = turned.shape[0] // 2
    return jnp.concatenate([turned[:half], turned[half:]], axis=1)


def conjugated(block):
    return jnp.where(low_lanes(block.shape), block, -block)


def right_operand(block):
    turned = swapped(block)
    full = jnp.concatenate([block, jnp.where(low_lanes(block.shape), -turned, turned)], axis=0)
    return split(full * (1.0 / RADIUS))


def backward_kernel(x, hop, out, high, low, hop_out):
    for s in range(x.shape[0]):
        high[s], low[s] = right_operand(conjugated(hop[s, 3]))
        out[s] = three_products(stacked(x[s]), high[s], low[s])
        hop_out[s] = hop[s]


def prepare_kernel(near, diag, hop, own_high, own_low, ahead_high, ahead_low):
    sites, half, wide = diag.shape
    rows = lax.broadcasted_iota(jnp.int32, (half, wide), 0)
    cols = lax.broadcasted_iota(jnp.int32, (half, wide), 1)
    unit = jnp.where(rows == cols, CENTER, 0.0)
    for s in range(sites):
        own_high[s, :wide], own_low[s, :wide] = right_operand(transposed(diag[s]) - unit)
        for d in range(3):
            place = slice((1 + d) * wide, (2 + d) * wide)
            other = hop[lax.rem(near[s, 4 + d], sites), d]
            own_high[s, place], own_low[s, place] = right_operand(
                transposed(hop[s, d]) + conjugated(other)
            )
        ahead_high[s], ahead_low[s] = right_operand(transposed(hop[s, 3]))


def own_kernel(near, x, high, low, out, spread):
    sites = x.shape[0]
    for n in range(sites):
        spread[n] = stacked(x[n])
    for s in range(sites):
        index = [s] + [lax.rem(near[s, d], sites) for d in range(3)]
        parts = jnp.concatenate([spread[n] for n in index], axis=1)
        out[s] = three_products(parts, high[s], low[s])


def step_kernel(mode, near, own, ahead, received, ahead_high, ahead_low, *rest):
    sites = own.shape[0]
    more = rest[0] if mode != "first" else None
    if mode == "image":
        out, back = rest[-1], None
    else:
        back_high, back_low, out, back = rest[-4:]
    for s in range(sites):
        parts = stacked(ahead[lax.rem(near[s, 3], sites)])
        part = three_products(parts, ahead_high[s], ahead_low[s])
        applied = own[s] + (part + received[lax.rem(near[s, 7], sites)])
        if mode == "first":
            out[s] = applied
        elif mode == "next":
            out[s] = 2.0 * applied - more[s]
        else:
            out[s] = RADIUS * applied + CENTER * more[s]
    if back is not None:
        for s in range(sites):
            back[s] = three_products(stacked(out[s]), back_high[s], back_low[s])


def senders(devices):
    chips = devices // 2
    table = []
    for v in range(devices):
        x, c = v // 2, v % 2
        opposite = (x + chips // 2) % chips
        table.append(
            [
                2 * ((x - 1 + 2 * c) % chips) + c,
                2 * ((x + 1) % chips) + 1 - c,
                2 * x + 1 - c,
                2 * opposite + (1 - c if x < chips // 2 else c),
            ]
        )
    return table


def product_kernel(own, image, first, second, third, fourth, out):
    sites, cols, wide = own.shape

    def flat(ref):
        return jnp.concatenate([ref[s] for s in range(sites)], axis=1)

    f = flat(own)
    high, low = split(jnp.concatenate([f, flat(image)], axis=0))
    left = jnp.concatenate([high, low], axis=1)
    half = cols // 2
    dot = functools.partial(lax.dot_general, dimension_numbers=NT, preferred_element_type=f32)
    for p, group in enumerate(((own, first), (second, third), (fourth,))):
        h, l = split(jnp.concatenate([f if r is own else flat(r) for r in group], axis=0))
        tile = dot(left, jnp.concatenate([h, h], axis=1)) + dot(high, l)
        for i in range(2):
            part = tile[i * cols : (i + 1) * cols]
            start = i * (5 * half) + p * cols
            if len(group) == 2:
                out[start : start + cols] = part
            else:
                out[start : start + half] = jnp.concatenate([part[:half], part[half:]], axis=1)
    out[10 * half :] = jnp.zeros((out.shape[0] - 10 * half, wide), f32)


def lines_of(gathered):
    devices, _, wide = gathered.shape
    half = wide // 2
    blocks = {}
    for v, others in enumerate(senders(devices)):
        for j, u in enumerate([v, *others]):
            if j < 4:
                rows = gathered[v, (j // 2) * half : (j // 2 + 1) * half]
                block = rows[:, (j % 2) * half : (j % 2 + 1) * half]
            else:
                rows = gathered[v, wide : wide + half // 2]
                block = jnp.concatenate([rows[:, :half], rows[:, half:]], axis=0)
            blocks[v, u] = block
    for v in range(devices):
        for u in range(devices):
            if (v, u) not in blocks:
                blocks[v, u] = blocks[u, v].T
    return [
        jnp.concatenate([blocks[v, u] for u in range(devices)], axis=1) for v in range(devices)
    ]


def sum_kernel(parts, out):
    total = parts[0]
    for i in range(1, parts.shape[0]):
        total = total + parts[i]
    for i in range(out.shape[0]):
        out[i] = total


def multiply(a, b, dims):
    ah, al = split(a)
    bh, bl = split(b)
    dot = functools.partial(lax.dot_general, dimension_numbers=dims, preferred_element_type=f32)
    return dot(ah, bh) + (dot(al, bh) + dot(ah, bl))


def inverse_kernel(count, gathered, out, scaled, factor):
    n = out.shape[0]
    half = gathered.shape[2] // 2
    for v, line in enumerate(lines_of(gathered)):
        scaled[v * half : (v + 1) * half, :] = line * (1.0 / count)
    rows = lax.broadcasted_iota(jnp.int32, (n, n), 0)
    cols = lax.broadcasted_iota(jnp.int32, (n, n), 1)
    on_diag = rows == cols
    weight = jnp.where(rows > cols, 1.0, jnp.where(on_diag, 0.5, 0.0))
    unit = jnp.where(on_diag, 1.0, 0.0)
    matrix = scaled[...]
    only_diag = jnp.where(on_diag, matrix, 0.0)
    scale_row = lax.rsqrt(jnp.sum(only_diag, axis=0, keepdims=True))
    scale_col = lax.rsqrt(jnp.sum(only_diag, axis=1, keepdims=True))
    matrix = matrix * scale_row * scale_col
    scaled[...] = matrix
    factor[...] = unit - weight * (matrix - unit)

    mid = n // 2
    dot = functools.partial(lax.dot_general, preferred_element_type=f32)
    square = (mid, mid)
    r, c = (lax.broadcasted_iota(jnp.int32, square, i) for i in range(2))
    small_weight = jnp.where(r > c, 1.0, jnp.where(r == c, 0.5, 0.0))
    small_unit = jnp.where(r == c, 1.0, 0.0)

    def improve(product, cut):
        s1 = cut(scaled[:, :mid])
        s2 = cut(scaled[:, mid:])
        top = cut(factor[:mid, :mid])
        side = cut(factor[mid:, :mid])
        low = cut(factor[mid:, mid:])
        lower = cut(factor[mid:, :])

        def part(x, piece):
            return tuple(y[piece] for y in x)

        t11 = cut(product(top, part(s1, slice(0, mid)), NN))
        t21 = cut(product(lower, s1, NN))
        t22 = cut(product(lower, s2, NN))
        e11 = product(t11, top, NT) - small_unit
        e21 = product(t21, top, NT)
        e22 = product(t21, side, NT) + product(t22, low, NT) - small_unit
        p11, p22 = small_weight * e11, small_weight * e22
        size = jnp.sum(p11 * p11 + p22 * p22 + e21 * e21)
        p11, p21, p22 = cut(p11), cut(e21), cut(p22)
        factor[:mid, :mid] = factor[:mid, :mid] - product(p11, top, NN)
        factor[mid:, :mid] = factor[mid:, :mid] - (
            product(p21, top, NN) + product(p22, side, NN)
        )
        factor[mid:, mid:] = factor[mid:, mid:] - product(p22, low, NN)
        return size

    def once(a, b, dims):
        return dot(a[0], b[0], dimension_numbers=dims)

    def thrice(a, b, dims):
        (ah, al), (bh, bl) = a, b
        return dot(ah, bh, dimension_numbers=dims) + (
            dot(al, bh, dimension_numbers=dims) + dot(ah, bl, dimension_numbers=dims)
        )

    improve(once, lambda x: (x.astype(bf16),))

    def go_on(state):
        step, size = state
        return jnp.logical_and(step < NEWTON_LIMIT, jnp.logical_not(size < NEWTON_DONE))

    def body(state):
        return state[0] + 1, improve(thrice, split)

    _, size = lax.while_loop(go_on, body, (jnp.int32(0), jnp.float32(1.0)))

    @pl.when(jnp.logical_not(size < NEWTON_DONE))
    def _():
        factor[...] = unit

        def eliminate(j, carry):
            pivot_row = scaled[pl.ds(j, 1), :]
            here = lax.broadcasted_iota(jnp.int32, (1, n), 1) == j
            pivot = jnp.sum(jnp.where(here, pivot_row, 0.0))
            a = scaled[...]
            column = jnp.sum(jnp.where(cols == j, a, 0.0), axis=1, keepdims=True) / pivot
            below = lax.broadcasted_iota(jnp.int32, (n, 1), 0) > j
            column = jnp.where(below, column, 0.0)
            r_row = factor[pl.ds(j, 1), :]
            scaled[...] = a - column * pivot_row
            factor[...] = factor[...] - column * r_row
            factor[pl.ds(j, 1), :] = r_row * lax.rsqrt(jnp.full_like(r_row, pivot))
            return carry

        lax.fori_loop(0, n, eliminate, 0)

    out[...] = factor[...] * scale_row


def basis_kernel(place, vectors, inverse, out):
    sites, columns, _ = out.shape
    mine = inverse[pl.ds(pl.multiple_of(place[0] * columns, columns), columns), :]
    for s in range(sites):
        block = jnp.concatenate(
            [vectors[u, s * columns : (s + 1) * columns] for u in range(vectors.shape[0])],
            axis=0,
        )
        out[s] = multiply(mine, block, NN)


def projected_kernel(count, place, moments, inverse, out):
    half = moments.shape[2] // 2
    moment = jnp.concatenate(lines_of(moments), axis=0)
    mine = inverse[pl.ds(pl.multiple_of(place[0] * half, half), half), :]
    half_way = multiply(mine, moment, NN)
    out[...] = multiply(half_way, inverse[...], NT) * (1.0 / count)


def passed_along(x, by):
    size = lax.axis_size("site")
    return lax.ppermute(x, "site", [(i, (i + by) % size) for i in range(size)])


def local(diag_blocks, hop_blocks, neighbors, start_basis):
    sites, both, cols = start_basis.shape
    half = both // 2
    devices = lax.axis_size("vec")
    slices = lax.axis_size("site")
    all_cols = cols * devices
    count = float(sites * both * slices)
    place = lax.axis_index("vec").astype(jnp.int32).reshape(1)
    shape = jax.ShapeDtypeStruct
    block = shape((sites, cols, both), f32)
    size = sites * cols * both * 4

    def matrices(blocks):
        return (shape((sites, blocks * both, both), bf16),) * 2

    def work(blocks):
        return sites * cols * blocks * 3 * both * both * 2

    current = jnp.swapaxes(start_basis, 1, 2)
    back, *back_mats, links = call(
        backward_kernel,
        (block, *matrices(1), shape(hop_blocks.shape, f32)),
        0,
        2,
        flops=work(1),
        moved=8 * size,
        name="backward",
    )(current, hop_blocks)
    mats = call(
        prepare_kernel,
        (*matrices(4), *matrices(1)),
        1,
        2,
        flops=1 << 24,
        moved=1 << 23,
        name="prepare",
    )(neighbors, diag_blocks, links)
    own_mats, ahead_mats = mats[:2], mats[2:]

    def apply(vectors, back, mode, *more):
        ahead = passed_along(vectors, -1)
        received = passed_along(back, 1)
        own = call(
            own_kernel,
            block,
            1,
            3,
            scratch=[pltpu.VMEM((sites, 2 * cols, both), bf16)],
            flops=work(4),
            moved=8 * size,
            name="own_slice",
        )(neighbors, vectors, *own_mats)
        if mode != "image":
            more = (*more, *back_mats)
        return call(
            functools.partial(step_kernel, mode),
            block if mode == "image" else (block, block),
            1,
            5 + len(more),
            flops=work(1),
            moved=8 * size,
            name="next_slices",
        )(neighbors, own, ahead, received, *ahead_mats, *more)

    previous = current
    current, back = apply(current, back, "first")
    for _ in range(DEGREE - 1):
        following, back = apply(current, back, "next", previous)
        previous, current = current, following

    image = apply(current, back, "image", current)
    table = senders(devices)
    others = [None] * 4
    for i in (3, 1, 0, 2):
        others[i] = lax.ppermute(current, "vec", [(table[v][i], v) for v in range(devices)])
    kept = 5 * cols // 2
    products = call(
        product_kernel,
        shape((slices * 8, both), f32),
        0,
        6,
        flops=6 * 5 * cols * 2 * cols * sites * both,
        moved=1 << 22,
        name="products",
    )(current, image, *others)
    flat, _ = lax.optimization_barrier((current.reshape(sites * cols, both), products))
    everything = lax.all_gather(flat, "vec", axis=0)

    parts = lax.all_to_all(products.reshape(slices, 8, both), "site", 0, 0, tiled=True)
    summed = call(
        sum_kernel, shape((slices, 8, both), f32), 0, 1, moved=1 << 19, name="sum_parts"
    )(parts)
    whole = lax.all_to_all(summed, "site", 0, 0, tiled=True).reshape(slices * 8, both)
    whole, everything = lax.optimization_barrier((whole, everything))
    copies = call(
        functools.partial(repeat_kernel, kept),
        shape((devices, kept + 13 * 8, both), f32),
        0,
        1,
        moved=1 << 21,
        name="repeat",
    )(whole)
    moments = lax.all_to_all(copies, "vec", 0, 0, tiled=True)
    gram = lax.all_gather(whole[:kept], "vec", axis=0)

    inverse = call(
        functools.partial(inverse_kernel, count),
        shape((all_cols, all_cols), f32),
        0,
        1,
        scratch=[pltpu.VMEM((all_cols, all_cols), f32)] * 2,
        flops=9 * 6 * all_cols**3,
        moved=1 << 21,
        name="inverse_factor",
    )(gram)
    basis = call(
        basis_kernel,
        block,
        1,
        2,
        flops=6 * all_cols * cols * sites * both,
        moved=1 << 22,
        name="basis",
    )(place, everything, inverse)
    projected = call(
        functools.partial(projected_kernel, count),
        shape((cols, all_cols), f32),
        1,
        2,
        flops=12 * all_cols * all_cols * cols,
        moved=1 << 22,
        name="projected",
    )(place, moments, inverse)
    return jnp.swapaxes(basis, 1, 2), projected.T


def solution(mesh):
    placed = (
        P("site", None, None),
        P("site", None, None, None),
        P("site", None),
        P("site", None, "vec"),
    )
    return jax.shard_map(
        local,
        mesh=mesh,
        in_specs=placed,
        out_specs=(P("site", None, "vec"), P(None, "vec")),
        check_vma=False,
    )
```

```python
import functools

import jax
import jax.numpy as jnp
from jax import lax
from jax.experimental import pallas as pl
from jax.experimental.pallas import tpu as pltpu
from jax.sharding import PartitionSpec as P

DEGREE = 4
CENTER = 3.7
RADIUS = 3.1
NEWTON_LIMIT = 12
NEWTON_DONE = 1e-6
VMEM_LIMIT = 44 * 1024 * 1024
VMEM_WHOLE = 44 * 1024 * 1024

f32 = jnp.float32
bf16 = jnp.bfloat16
VMEM_SPEC = pl.BlockSpec(memory_space=pltpu.VMEM)
SMEM_SPEC = pl.BlockSpec(memory_space=pltpu.SMEM)


def call(
    kernel,
    out_shape,
    n_smem,
    n_vmem,
    scratch=(),
    flops=0,
    moved=0,
    name=None,
):
    return pl.pallas_call(
        kernel,
        out_shape=out_shape,
        in_specs=[SMEM_SPEC] * n_smem + [VMEM_SPEC] * n_vmem,
        out_specs=jax.tree.map(lambda _: VMEM_SPEC, out_shape),
        scratch_shapes=list(scratch),
        compiler_params=pltpu.CompilerParams(vmem_limit_bytes=VMEM_LIMIT),
        cost_estimate=pl.CostEstimate(flops=flops, bytes_accessed=moved, transcendentals=0),
        name=name,
    )


def split(x):
    high = x.astype(bf16)
    return high, (x - high.astype(f32)).astype(bf16)


NT = (((1,), (1,)), ((), ()))
NN = (((1,), (0,)), ((), ()))


def stacked(x):
    return jnp.concatenate(split(x), axis=0)


def three_products(parts, high, low):
    m = parts.shape[0] // 2
    both = jnp.dot(parts, high, preferred_element_type=f32)
    return both[:m] + (both[m:] + jnp.dot(parts[:m], low, preferred_element_type=f32))


def low_lanes(shape):
    return lax.broadcasted_iota(jnp.int32, shape, len(shape) - 1) < shape[-1] // 2


def swapped(x):
    return pltpu.roll(x, x.shape[-1] // 2, axis=x.ndim - 1)


def transposed(block):
    turned = block.T
    half = turned.shape[0] // 2
    return jnp.concatenate([turned[:half], turned[half:]], axis=1)


def conjugated(block):
    return jnp.where(low_lanes(block.shape), block, -block)


def right_operand(block):
    turned = swapped(block)
    full = jnp.concatenate([block, jnp.where(low_lanes(block.shape), -turned, turned)], axis=0)
    return split(full * (1.0 / RADIUS))


def backward_kernel(x, hop, out, high, low, hop_out):
    for s in range(x.shape[0]):
        high[s], low[s] = right_operand(conjugated(hop[s, 3]))
        out[s] = three_products(stacked(x[s]), high[s], low[s])
        hop_out[s] = hop[s]


def prepare_kernel(near, diag, hop, own_high, own_low, ahead_high, ahead_low):
    sites, half, wide = diag.shape
    rows = lax.broadcasted_iota(jnp.int32, (half, wide), 0)
    cols = lax.broadcasted_iota(jnp.int32, (half, wide), 1)
    unit = jnp.where(rows == cols, CENTER, 0.0)
    for s in range(sites):
        own_high[s, :wide], own_low[s, :wide] = right_operand(transposed(diag[s]) - unit)
        for d in range(3):
            place = slice((1 + d) * wide, (2 + d) * wide)
            other = hop[lax.rem(near[s, 4 + d], sites), d]
            own_high[s, place], own_low[s, place] = right_operand(
                transposed(hop[s, d]) + conjugated(other)
            )
        ahead_high[s], ahead_low[s] = right_operand(transposed(hop[s, 3]))


def own_kernel(near, x, high, low, out, spread):
    sites = x.shape[0]
    for n in range(sites):
        spread[n] = stacked(x[n])
    for s in range(sites):
        index = [s] + [lax.rem(near[s, d], sites) for d in range(3)]
        parts = jnp.concatenate([spread[n] for n in index], axis=1)
        out[s] = three_products(parts, high[s], low[s])


def step_kernel(mode, near, own, ahead, received, ahead_high, ahead_low, *rest):
    sites = own.shape[0]
    more = rest[0] if mode != "first" else None
    if mode == "image":
        out, back = rest[-1], None
    else:
        back_high, back_low, out, back = rest[-4:]
    for s in range(sites):
        parts = stacked(ahead[lax.rem(near[s, 3], sites)])
        part = three_products(parts, ahead_high[s], ahead_low[s])
        applied = own[s] + (part + received[lax.rem(near[s, 7], sites)])
        if mode == "first":
            out[s] = applied
        elif mode == "next":
            out[s] = 2.0 * applied - more[s]
        else:
            out[s] = RADIUS * applied + CENTER * more[s]
    if back is not None:
        for s in range(sites):
            back[s] = three_products(stacked(out[s]), back_high[s], back_low[s])


def senders(devices):
    chips = devices // 2
    table = []
    for v in range(devices):
        x, c = v // 2, v % 2
        opposite = (x + chips // 2) % chips
        table.append(
            [
                2 * ((x - 1 + 2 * c) % chips) + c,
                2 * ((x + 1) % chips) + 1 - c,
                2 * x + 1 - c,
                2 * opposite + (1 - c if x < chips // 2 else c),
            ]
        )
    return table


def product_kernel(own, image, first, second, third, fourth, out):
    sites, cols, wide = own.shape

    def flat(ref):
        return jnp.concatenate([ref[s] for s in range(sites)], axis=1)

    f = flat(own)
    high, low = split(jnp.concatenate([f, flat(image)], axis=0))
    left = jnp.concatenate([high, low], axis=1)
    half = cols // 2
    dot = functools.partial(lax.dot_general, dimension_numbers=NT, preferred_element_type=f32)
    for p, group in enumerate(((own, first), (second, third), (fourth,))):
        h, l = split(jnp.concatenate([f if r is own else flat(r) for r in group], axis=0))
        tile = dot(left, jnp.concatenate([h, h], axis=1)) + dot(high, l)
        for i in range(2):
            part = tile[i * cols : (i + 1) * cols]
            start = i * (5 * half) + p * cols
            if len(group) == 2:
                out[start : start + cols] = part
            else:
                out[start : start + half] = jnp.concatenate([part[:half], part[half:]], axis=1)
    out[10 * half :] = jnp.zeros((out.shape[0] - 10 * half, wide), f32)


def lines_of(gathered):
    devices, _, wide = gathered.shape
    half = wide // 2
    blocks = {}
    for v, others in enumerate(senders(devices)):
        for j, u in enumerate([v, *others]):
            if j < 4:
                rows = gathered[v, (j // 2) * half : (j // 2 + 1) * half]
                block = rows[:, (j % 2) * half : (j % 2 + 1) * half]
            else:
                rows = gathered[v, wide : wide + half // 2]
                block = jnp.concatenate([rows[:, :half], rows[:, half:]], axis=0)
            blocks[v, u] = block
    for v in range(devices):
        for u in range(devices):
            if (v, u) not in blocks:
                blocks[v, u] = blocks[u, v].T
    return [
        jnp.concatenate([blocks[v, u] for u in range(devices)], axis=1) for v in range(devices)
    ]


def sum_kernel(parts, out):
    total = parts[0]
    for i in range(1, parts.shape[0]):
        total = total + parts[i]
    for i in range(out.shape[0]):
        out[i] = total


def multiply(a, b, dims):
    (ah, al), (bh, bl) = a, b
    dot = functools.partial(lax.dot_general, dimension_numbers=dims, preferred_element_type=f32)
    return dot(ah, bh) + (dot(al, bh) + dot(ah, bl))


def inverse_kernel(count, gathered, high, low, scaled, factor):
    n = high.shape[0]
    half = gathered.shape[2] // 2
    for v, line in enumerate(lines_of(gathered)):
        scaled[v * half : (v + 1) * half, :] = line * (1.0 / count)
    rows = lax.broadcasted_iota(jnp.int32, (n, n), 0)
    cols = lax.broadcasted_iota(jnp.int32, (n, n), 1)
    on_diag = rows == cols
    weight = jnp.where(rows > cols, 1.0, jnp.where(on_diag, 0.5, 0.0))
    unit = jnp.where(on_diag, 1.0, 0.0)
    matrix = scaled[...]
    only_diag = jnp.where(on_diag, matrix, 0.0)
    scale_row = lax.rsqrt(jnp.sum(only_diag, axis=0, keepdims=True))
    scale_col = lax.rsqrt(jnp.sum(only_diag, axis=1, keepdims=True))
    matrix = matrix * scale_row * scale_col
    scaled[...] = matrix
    factor[...] = unit - weight * (matrix - unit)

    mid = n // 2
    dot = functools.partial(lax.dot_general, preferred_element_type=f32)
    square = (mid, mid)
    r, c = (lax.broadcasted_iota(jnp.int32, square, i) for i in range(2))
    small_weight = jnp.where(r > c, 1.0, jnp.where(r == c, 0.5, 0.0))
    small_unit = jnp.where(r == c, 1.0, 0.0)

    def improve(product, cut):
        s1 = cut(scaled[:, :mid])
        s2 = cut(scaled[:, mid:])
        top = cut(factor[:mid, :mid])
        side = cut(factor[mid:, :mid])
        corner = cut(factor[mid:, mid:])
        lower = cut(factor[mid:, :])

        def part(x, piece):
            return tuple(y[piece] for y in x)

        t11 = cut(product(top, part(s1, slice(0, mid)), NN))
        t21 = cut(product(lower, s1, NN))
        t22 = cut(product(lower, s2, NN))
        e11 = product(t11, top, NT) - small_unit
        e21 = product(t21, top, NT)
        e22 = product(t21, side, NT) + product(t22, corner, NT) - small_unit
        p11, p22 = small_weight * e11, small_weight * e22
        size = jnp.sum(p11 * p11 + p22 * p22 + e21 * e21)
        p11, p21, p22 = cut(p11), cut(e21), cut(p22)
        factor[:mid, :mid] = factor[:mid, :mid] - product(p11, top, NN)
        factor[mid:, :mid] = factor[mid:, :mid] - (
            product(p21, top, NN) + product(p22, side, NN)
        )
        factor[mid:, mid:] = factor[mid:, mid:] - product(p22, corner, NN)
        return size

    def once(a, b, dims):
        return dot(a[0], b[0], dimension_numbers=dims)

    improve(once, lambda x: (x.astype(bf16),))

    def go_on(state):
        step, size = state
        return jnp.logical_and(step < NEWTON_LIMIT, jnp.logical_not(size < NEWTON_DONE))

    def body(state):
        return state[0] + 1, improve(multiply, split)

    _, size = lax.while_loop(go_on, body, (jnp.int32(0), jnp.float32(1.0)))

    @pl.when(jnp.logical_not(size < NEWTON_DONE))
    def _():
        factor[...] = unit

        def eliminate(j, carry):
            pivot_row = scaled[pl.ds(j, 1), :]
            here = lax.broadcasted_iota(jnp.int32, (1, n), 1) == j
            pivot = jnp.sum(jnp.where(here, pivot_row, 0.0))
            a = scaled[...]
            column = jnp.sum(jnp.where(cols == j, a, 0.0), axis=1, keepdims=True) / pivot
            below = lax.broadcasted_iota(jnp.int32, (n, 1), 0) > j
            column = jnp.where(below, column, 0.0)
            r_row = factor[pl.ds(j, 1), :]
            scaled[...] = a - column * pivot_row
            factor[...] = factor[...] - column * r_row
            factor[pl.ds(j, 1), :] = r_row * lax.rsqrt(jnp.full_like(r_row, pivot))
            return carry

        lax.fori_loop(0, n, eliminate, 0)

    high[...], low[...] = split(factor[...] * scale_row)


def own_rows(place, high, low, count):
    rows = pl.ds(pl.multiple_of(place[0] * count, count), count)
    return high[rows, :], low[rows, :]


def basis_kernel(place, vectors, high, low, out):
    sites, columns, _ = out.shape
    mine = own_rows(place, high, low, columns)
    for s in range(sites):
        block = jnp.concatenate(
            [vectors[u, s * columns : (s + 1) * columns] for u in range(vectors.shape[0])],
            axis=0,
        )
        out[s] = multiply(mine, split(block), NN)


def projected_kernel(count, place, moments, high, low, out):
    moment = jnp.concatenate(lines_of(moments), axis=0)
    mine = own_rows(place, high, low, out.shape[0])
    half_way = multiply(mine, split(moment), NN)
    out[...] = multiply(split(half_way), (high[...], low[...]), NT) * (1.0 / count)


def passed_along(x, by):
    size = lax.axis_size("site")
    return lax.ppermute(x, "site", [(i, (i + by) % size) for i in range(size)])


def local(diag_blocks, hop_blocks, neighbors, start_basis):
    sites, both, cols = start_basis.shape
    half = both // 2
    devices = lax.axis_size("vec")
    slices = lax.axis_size("site")
    all_cols = cols * devices
    count = float(sites * both * slices)
    place = lax.axis_index("vec").astype(jnp.int32).reshape(1)
    shape = jax.ShapeDtypeStruct
    block = shape((sites, cols, both), f32)
    size = sites * cols * both * 4

    def matrices(blocks):
        return (shape((sites, blocks * both, both), bf16),) * 2

    def work(blocks):
        return sites * cols * blocks * 3 * both * both * 2

    current = jnp.swapaxes(start_basis, 1, 2)
    back, *back_mats, links = call(
        backward_kernel,
        (block, *matrices(1), shape(hop_blocks.shape, f32)),
        0,
        2,
        flops=work(1),
        moved=8 * size,
        name="backward",
    )(current, hop_blocks)
    mats = call(
        prepare_kernel,
        (*matrices(4), *matrices(1)),
        1,
        2,
        flops=1 << 24,
        moved=1 << 23,
        name="prepare",
    )(neighbors, diag_blocks, links)
    own_mats, ahead_mats = mats[:2], mats[2:]

    def apply(vectors, back, mode, *more):
        ahead = passed_along(vectors, -1)
        received = passed_along(back, 1)
        own = call(
            own_kernel,
            block,
            1,
            3,
            scratch=[pltpu.VMEM((sites, 2 * cols, both), bf16)],
            flops=work(4),
            moved=8 * size,
            name="own_slice",
        )(neighbors, vectors, *own_mats)
        if mode != "image":
            more = (*more, *back_mats)
        return call(
            functools.partial(step_kernel, mode),
            block if mode == "image" else (block, block),
            1,
            5 + len(more),
            flops=work(1),
            moved=8 * size,
            name="next_slices",
        )(neighbors, own, ahead, received, *ahead_mats, *more)

    previous = current
    current, back = apply(current, back, "first")
    for _ in range(DEGREE - 1):
        following, back = apply(current, back, "next", previous)
        previous, current = current, following

    image = apply(current, back, "image", current)
    table = senders(devices)
    others = [None] * 4
    for i in (3, 1, 0, 2):
        others[i] = lax.ppermute(current, "vec", [(table[v][i], v) for v in range(devices)])
    kept = 5 * cols // 2
    products = call(
        product_kernel,
        shape((slices * 8, both), f32),
        0,
        6,
        flops=6 * 5 * cols * 2 * cols * sites * both,
        moved=1 << 22,
        name="products",
    )(current, image, *others)
    flat, _ = lax.optimization_barrier((current.reshape(sites * cols, both), products))
    everything = lax.all_gather(flat, "vec", axis=0)

    parts = lax.all_to_all(products.reshape(slices, 8, both), "site", 0, 0, tiled=True)
    summed = call(
        sum_kernel, shape((slices, 8, both), f32), 0, 1, moved=1 << 19, name="sum_parts"
    )(parts)
    whole = lax.all_to_all(summed, "site", 0, 0, tiled=True).reshape(slices * 8, both)
    whole, everything = lax.optimization_barrier((whole, everything))
    moments = lax.all_gather(whole[kept : kept + all_cols // 2], "vec", axis=0)
    gram = lax.all_gather(whole[:kept], "vec", axis=0)

    inverse = call(
        functools.partial(inverse_kernel, count),
        (shape((all_cols, all_cols), bf16),) * 2,
        0,
        1,
        scratch=[pltpu.VMEM((all_cols, all_cols), f32)] * 2,
        flops=9 * 6 * all_cols**3,
        moved=1 << 21,
        name="inverse_factor",
    )(gram)
    basis = call(
        basis_kernel,
        block,
        1,
        3,
        flops=6 * all_cols * cols * sites * both,
        moved=1 << 22,
        name="basis",
    )(place, everything, *inverse)
    projected = call(
        functools.partial(projected_kernel, count),
        shape((cols, all_cols), f32),
        1,
        3,
        flops=12 * all_cols * all_cols * cols,
        moved=1 << 22,
        name="projected",
    )(place, moments, *inverse)
    return jnp.swapaxes(basis, 1, 2), projected.T


def solution(mesh):
    placed = (
        P("site", None, None),
        P("site", None, None, None),
        P("site", None),
        P("site", None, "vec"),
    )
    return jax.shard_map(
        local,
        mesh=mesh,
        in_specs=placed,
        out_specs=(P("site", None, "vec"), P(None, "vec")),
        check_vma=False,
    )
```

```python
import functools

import jax
import jax.numpy as jnp
from jax import lax
from jax.experimental import pallas as pl
from jax.experimental.pallas import tpu as pltpu
from jax.sharding import PartitionSpec as P

DEGREE = 4
CENTER = 3.7
RADIUS = 3.1
NEWTON_LIMIT = 12
NEWTON_DONE = 1e-6
VMEM_LIMIT = 44 * 1024 * 1024
VMEM_WHOLE = 44 * 1024 * 1024

f32 = jnp.float32
bf16 = jnp.bfloat16
VMEM_SPEC = pl.BlockSpec(memory_space=pltpu.VMEM)
SMEM_SPEC = pl.BlockSpec(memory_space=pltpu.SMEM)


def call(
    kernel,
    out_shape,
    n_smem,
    n_vmem,
    scratch=(),
    flops=0,
    moved=0,
    name=None,
):
    return pl.pallas_call(
        kernel,
        out_shape=out_shape,
        in_specs=[SMEM_SPEC] * n_smem + [VMEM_SPEC] * n_vmem,
        out_specs=jax.tree.map(lambda _: VMEM_SPEC, out_shape),
        scratch_shapes=list(scratch),
        compiler_params=pltpu.CompilerParams(vmem_limit_bytes=VMEM_LIMIT),
        cost_estimate=pl.CostEstimate(flops=flops, bytes_accessed=moved, transcendentals=0),
        name=name,
    )


def split(x):
    high = x.astype(bf16)
    return high, (x - high.astype(f32)).astype(bf16)


NT = (((1,), (1,)), ((), ()))
NN = (((1,), (0,)), ((), ()))


def stacked(x):
    return jnp.concatenate(split(x), axis=0)


def three_products(parts, high, low):
    m = parts.shape[0] // 2
    both = jnp.dot(parts, high, preferred_element_type=f32)
    return both[:m] + (both[m:] + jnp.dot(parts[:m], low, preferred_element_type=f32))


def low_lanes(shape):
    return lax.broadcasted_iota(jnp.int32, shape, len(shape) - 1) < shape[-1] // 2


def swapped(x):
    return pltpu.roll(x, x.shape[-1] // 2, axis=x.ndim - 1)


def transposed(block):
    turned = block.T
    half = turned.shape[0] // 2
    return jnp.concatenate([turned[:half], turned[half:]], axis=1)


def conjugated(block):
    return jnp.where(low_lanes(block.shape), block, -block)


def right_operand(block):
    turned = swapped(block)
    full = jnp.concatenate([block, jnp.where(low_lanes(block.shape), -turned, turned)], axis=0)
    return split(full * (1.0 / RADIUS))


def backward_kernel(x, hop, out, high, low, hop_out):
    for s in range(x.shape[0]):
        high[s], low[s] = right_operand(conjugated(hop[s, 3]))
        out[s] = three_products(stacked(x[s]), high[s], low[s])
        hop_out[s] = hop[s]


def prepare_kernel(near, diag, hop, own_high, own_low, ahead_high, ahead_low):
    sites, half, wide = diag.shape
    rows = lax.broadcasted_iota(jnp.int32, (half, wide), 0)
    cols = lax.broadcasted_iota(jnp.int32, (half, wide), 1)
    unit = jnp.where(rows == cols, CENTER, 0.0)
    for s in range(sites):
        own_high[s, :wide], own_low[s, :wide] = right_operand(transposed(diag[s]) - unit)
        for d in range(3):
            place = slice((1 + d) * wide, (2 + d) * wide)
            other = hop[lax.rem(near[s, 4 + d], sites), d]
            own_high[s, place], own_low[s, place] = right_operand(
                transposed(hop[s, d]) + conjugated(other)
            )
        ahead_high[s], ahead_low[s] = right_operand(transposed(hop[s, 3]))


def own_kernel(near, x, high, low, out, spread):
    sites = x.shape[0]
    for n in range(sites):
        spread[n] = stacked(x[n])
    for s in range(sites):
        index = [s] + [lax.rem(near[s, d], sites) for d in range(3)]
        parts = jnp.concatenate([spread[n] for n in index], axis=1)
        out[s] = three_products(parts, high[s], low[s])


def step_kernel(mode, near, own, ahead, received, ahead_high, ahead_low, *rest):
    sites = own.shape[0]
    more = rest[0] if mode != "first" else None
    if mode == "image":
        out, back = rest[-1], None
    else:
        back_high, back_low, out, back = rest[-4:]
    for s in range(sites):
        parts = stacked(ahead[lax.rem(near[s, 3], sites)])
        part = three_products(parts, ahead_high[s], ahead_low[s])
        applied = own[s] + (part + received[lax.rem(near[s, 7], sites)])
        if mode == "first":
            out[s] = applied
        elif mode == "next":
            out[s] = 2.0 * applied - more[s]
        else:
            out[s] = RADIUS * applied + CENTER * more[s]
    if back is not None:
        for s in range(sites):
            back[s] = three_products(stacked(out[s]), back_high[s], back_low[s])


def senders(devices):
    chips = devices // 2
    table = []
    for v in range(devices):
        x, c = v // 2, v % 2
        opposite = (x + chips // 2) % chips
        table.append(
            [
                2 * ((x - 1 + 2 * c) % chips) + c,
                2 * ((x + 1) % chips) + 1 - c,
                2 * x + 1 - c,
                2 * opposite + (1 - c if x < chips // 2 else c),
            ]
        )
    return table


def product_kernel(own, image, fourth, second, first, third, out):
    sites, cols, wide = own.shape

    def flat(ref):
        return jnp.concatenate([ref[s] for s in range(sites)], axis=1)

    f = flat(own)
    high, low = split(jnp.concatenate([f, flat(image)], axis=0))
    left = jnp.concatenate([high, low], axis=1)
    half = cols // 2
    dot = functools.partial(lax.dot_general, dimension_numbers=NT, preferred_element_type=f32)
    for p, group in enumerate(((own, first), (second, third), (fourth,))):
        h, l = split(jnp.concatenate([f if r is own else flat(r) for r in group], axis=0))
        tile = dot(left, jnp.concatenate([h, h], axis=1)) + dot(high, l)
        for i in range(2):
            part = tile[i * cols : (i + 1) * cols]
            start = i * (5 * half) + p * cols
            if len(group) == 2:
                out[start : start + cols] = part
            else:
                out[start : start + half] = jnp.concatenate([part[:half], part[half:]], axis=1)
    out[10 * half :] = jnp.zeros((out.shape[0] - 10 * half, wide), f32)


def lines_of(gathered):
    devices, _, wide = gathered.shape
    half = wide // 2
    blocks = {}
    for v, others in enumerate(senders(devices)):
        for j, u in enumerate([v, *others]):
            if j < 4:
                rows = gathered[v, (j // 2) * half : (j // 2 + 1) * half]
                block = rows[:, (j % 2) * half : (j % 2 + 1) * half]
            else:
                rows = gathered[v, wide : wide + half // 2]
                block = jnp.concatenate([rows[:, :half], rows[:, half:]], axis=0)
            blocks[v, u] = block
    for v in range(devices):
        for u in range(devices):
            if (v, u) not in blocks:
                blocks[v, u] = blocks[u, v].T
    return [
        jnp.concatenate([blocks[v, u] for u in range(devices)], axis=1) for v in range(devices)
    ]


def sum_kernel(parts, out):
    total = parts[0]
    for i in range(1, parts.shape[0]):
        total = total + parts[i]
    for i in range(out.shape[0]):
        out[i] = total


def multiply(a, b, dims):
    (ah, al), (bh, bl) = a, b
    dot = functools.partial(lax.dot_general, dimension_numbers=dims, preferred_element_type=f32)
    return dot(ah, bh) + (dot(al, bh) + dot(ah, bl))


def inverse_kernel(count, gathered, high, low, scaled, factor):
    n = high.shape[0]
    half = gathered.shape[2] // 2
    for v, line in enumerate(lines_of(gathered)):
        scaled[v * half : (v + 1) * half, :] = line * (1.0 / count)
    rows = lax.broadcasted_iota(jnp.int32, (n, n), 0)
    cols = lax.broadcasted_iota(jnp.int32, (n, n), 1)
    on_diag = rows == cols
    weight = jnp.where(rows > cols, 1.0, jnp.where(on_diag, 0.5, 0.0))
    unit = jnp.where(on_diag, 1.0, 0.0)
    matrix = scaled[...]
    only_diag = jnp.where(on_diag, matrix, 0.0)
    scale_row = lax.rsqrt(jnp.sum(only_diag, axis=0, keepdims=True))
    scale_col = lax.rsqrt(jnp.sum(only_diag, axis=1, keepdims=True))
    matrix = matrix * scale_row * scale_col
    scaled[...] = matrix
    factor[...] = unit - weight * (matrix - unit)

    mid = n // 2
    dot = functools.partial(lax.dot_general, preferred_element_type=f32)
    square = (mid, mid)
    r, c = (lax.broadcasted_iota(jnp.int32, square, i) for i in range(2))
    small_weight = jnp.where(r > c, 1.0, jnp.where(r == c, 0.5, 0.0))
    small_unit = jnp.where(r == c, 1.0, 0.0)

    def improve(product, cut):
        s1 = cut(scaled[:, :mid])
        s2 = cut(scaled[:, mid:])
        top = cut(factor[:mid, :mid])
        side = cut(factor[mid:, :mid])
        corner = cut(factor[mid:, mid:])
        lower = cut(factor[mid:, :])

        def part(x, piece):
            return tuple(y[piece] for y in x)

        t11 = cut(product(top, part(s1, slice(0, mid)), NN))
        t21 = cut(product(lower, s1, NN))
        t22 = cut(product(lower, s2, NN))
        e11 = product(t11, top, NT) - small_unit
        e21 = product(t21, top, NT)
        e22 = product(t21, side, NT) + product(t22, corner, NT) - small_unit
        p11, p22 = small_weight * e11, small_weight * e22
        size = jnp.sum(p11 * p11 + p22 * p22 + e21 * e21)
        p11, p21, p22 = cut(p11), cut(e21), cut(p22)
        factor[:mid, :mid] = factor[:mid, :mid] - product(p11, top, NN)
        factor[mid:, :mid] = factor[mid:, :mid] - (
            product(p21, top, NN) + product(p22, side, NN)
        )
        factor[mid:, mid:] = factor[mid:, mid:] - product(p22, corner, NN)
        return size

    def once(a, b, dims):
        return dot(a[0], b[0], dimension_numbers=dims)

    improve(once, lambda x: (x.astype(bf16),))

    def go_on(state):
        step, size = state
        return jnp.logical_and(step < NEWTON_LIMIT, jnp.logical_not(size < NEWTON_DONE))

    def body(state):
        return state[0] + 1, improve(multiply, split)

    _, size = lax.while_loop(go_on, body, (jnp.int32(0), jnp.float32(1.0)))

    @pl.when(jnp.logical_not(size < NEWTON_DONE))
    def _():
        factor[...] = unit

        def eliminate(j, carry):
            pivot_row = scaled[pl.ds(j, 1), :]
            here = lax.broadcasted_iota(jnp.int32, (1, n), 1) == j
            pivot = jnp.sum(jnp.where(here, pivot_row, 0.0))
            a = scaled[...]
            column = jnp.sum(jnp.where(cols == j, a, 0.0), axis=1, keepdims=True) / pivot
            below = lax.broadcasted_iota(jnp.int32, (n, 1), 0) > j
            column = jnp.where(below, column, 0.0)
            r_row = factor[pl.ds(j, 1), :]
            scaled[...] = a - column * pivot_row
            factor[...] = factor[...] - column * r_row
            factor[pl.ds(j, 1), :] = r_row * lax.rsqrt(jnp.full_like(r_row, pivot))
            return carry

        lax.fori_loop(0, n, eliminate, 0)

    high[...], low[...] = split(factor[...] * scale_row)


def own_rows(place, high, low, count):
    rows = pl.ds(pl.multiple_of(place[0] * count, count), count)
    return high[rows, :], low[rows, :]


def basis_kernel(place, vectors, high, low, out):
    sites, columns, _ = out.shape
    mine = own_rows(place, high, low, columns)
    for s in range(sites):
        block = jnp.concatenate(
            [vectors[u, s * columns : (s + 1) * columns] for u in range(vectors.shape[0])],
            axis=0,
        )
        out[s] = multiply(mine, split(block), NN)


def projected_kernel(count, place, moments, high, low, out):
    moment = jnp.concatenate(lines_of(moments), axis=0)
    mine = own_rows(place, high, low, out.shape[0])
    half_way = multiply(mine, split(moment), NN)
    out[...] = multiply(split(half_way), (high[...], low[...]), NT) * (1.0 / count)


def passed_along(x, by):
    size = lax.axis_size("site")
    return lax.ppermute(x, "site", [(i, (i + by) % size) for i in range(size)])


def local(diag_blocks, hop_blocks, neighbors, start_basis):
    sites, both, cols = start_basis.shape
    half = both // 2
    devices = lax.axis_size("vec")
    slices = lax.axis_size("site")
    all_cols = cols * devices
    count = float(sites * both * slices)
    place = lax.axis_index("vec").astype(jnp.int32).reshape(1)
    shape = jax.ShapeDtypeStruct
    block = shape((sites, cols, both), f32)
    size = sites * cols * both * 4

    def matrices(blocks):
        return (shape((sites, blocks * both, both), bf16),) * 2

    def work(blocks):
        return sites * cols * blocks * 3 * both * both * 2

    current = jnp.swapaxes(start_basis, 1, 2)
    back, *back_mats, links = call(
        backward_kernel,
        (block, *matrices(1), shape(hop_blocks.shape, f32)),
        0,
        2,
        flops=work(1),
        moved=8 * size,
        name="backward",
    )(current, hop_blocks)
    mats = call(
        prepare_kernel,
        (*matrices(4), *matrices(1)),
        1,
        2,
        flops=1 << 24,
        moved=1 << 23,
        name="prepare",
    )(neighbors, diag_blocks, links)
    own_mats, ahead_mats = mats[:2], mats[2:]

    def apply(vectors, back, mode, *more):
        ahead = passed_along(vectors, -1)
        received = passed_along(back, 1)
        own = call(
            own_kernel,
            block,
            1,
            3,
            scratch=[pltpu.VMEM((sites, 2 * cols, both), bf16)],
            flops=work(4),
            moved=8 * size,
            name="own_slice",
        )(neighbors, vectors, *own_mats)
        if mode != "image":
            more = (*more, *back_mats)
        return call(
            functools.partial(step_kernel, mode),
            block if mode == "image" else (block, block),
            1,
            5 + len(more),
            flops=work(1),
            moved=8 * size,
            name="next_slices",
        )(neighbors, own, ahead, received, *ahead_mats, *more)

    previous = current
    current, back = apply(current, back, "first")
    for _ in range(DEGREE - 1):
        following, back = apply(current, back, "next", previous)
        previous, current = current, following

    image = apply(current, back, "image", current)
    table = senders(devices)
    others = [
        lax.ppermute(current, "vec", [(table[v][i], v) for v in range(devices)])
        for i in (3, 1, 0, 2)
    ]
    kept = 5 * cols // 2
    products = call(
        product_kernel,
        shape((slices * 8, both), f32),
        0,
        6,
        flops=6 * 5 * cols * 2 * cols * sites * both,
        moved=1 << 22,
        name="products",
    )(current, image, *others)
    flat, _ = lax.optimization_barrier((current.reshape(sites * cols, both), products))
    everything = lax.all_gather(flat, "vec", axis=0)

    parts = lax.all_to_all(products.reshape(slices, 8, both), "site", 0, 0, tiled=True)
    summed = call(
        sum_kernel, shape((slices, 8, both), f32), 0, 1, moved=1 << 19, name="sum_parts"
    )(parts)
    whole = lax.all_to_all(summed, "site", 0, 0, tiled=True).reshape(slices * 8, both)
    whole, everything = lax.optimization_barrier((whole, everything))
    moments = lax.all_gather(whole[kept : kept + all_cols // 2], "vec", axis=0)
    gram = lax.all_gather(whole[:kept], "vec", axis=0)

    inverse = call(
        functools.partial(inverse_kernel, count),
        (shape((all_cols, all_cols), bf16),) * 2,
        0,
        1,
        scratch=[pltpu.VMEM((all_cols, all_cols), f32)] * 2,
        flops=9 * 6 * all_cols**3,
        moved=1 << 21,
        name="inverse_factor",
    )(gram)
    basis = call(
        basis_kernel,
        block,
        1,
        3,
        flops=6 * all_cols * cols * sites * both,
        moved=1 << 22,
        name="basis",
    )(place, everything, *inverse)
    projected = call(
        functools.partial(projected_kernel, count),
        shape((cols, all_cols), f32),
        1,
        3,
        flops=12 * all_cols * all_cols * cols,
        moved=1 << 22,
        name="projected",
    )(place, moments, *inverse)
    return jnp.swapaxes(basis, 1, 2), projected.T


def solution(mesh):
    placed = (
        P("site", None, None),
        P("site", None, None, None),
        P("site", None),
        P("site", None, "vec"),
    )
    return jax.shard_map(
        local,
        mesh=mesh,
        in_specs=placed,
        out_specs=(P("site", None, "vec"), P(None, "vec")),
        check_vma=False,
    )
```

```python
import functools

import jax
import jax.numpy as jnp
from jax import lax
from jax.experimental import pallas as pl
from jax.experimental.pallas import tpu as pltpu
from jax.sharding import PartitionSpec as P

DEGREE = 4
CENTER = 3.7
RADIUS = 3.1
NEWTON_LIMIT = 12
NEWTON_DONE = 1e-6
VMEM_LIMIT = 44 * 1024 * 1024
VMEM_WHOLE = 44 * 1024 * 1024

f32 = jnp.float32
bf16 = jnp.bfloat16
VMEM_SPEC = pl.BlockSpec(memory_space=pltpu.VMEM)
SMEM_SPEC = pl.BlockSpec(memory_space=pltpu.SMEM)


def call(
    kernel,
    out_shape,
    n_smem,
    n_vmem,
    scratch=(),
    flops=0,
    moved=0,
    name=None,
):
    return pl.pallas_call(
        kernel,
        out_shape=out_shape,
        in_specs=[SMEM_SPEC] * n_smem + [VMEM_SPEC] * n_vmem,
        out_specs=jax.tree.map(lambda _: VMEM_SPEC, out_shape),
        scratch_shapes=list(scratch),
        compiler_params=pltpu.CompilerParams(vmem_limit_bytes=VMEM_LIMIT),
        cost_estimate=pl.CostEstimate(flops=flops, bytes_accessed=moved, transcendentals=0),
        name=name,
    )


def split(x):
    high = x.astype(bf16)
    return high, (x - high.astype(f32)).astype(bf16)


NT = (((1,), (1,)), ((), ()))
NN = (((1,), (0,)), ((), ()))


def stacked(x):
    return jnp.concatenate(split(x), axis=0)


def three_products(parts, high, low):
    m = parts.shape[0] // 2
    both = jnp.dot(parts, high, preferred_element_type=f32)
    return both[:m] + (both[m:] + jnp.dot(parts[:m], low, preferred_element_type=f32))


def low_lanes(shape):
    return lax.broadcasted_iota(jnp.int32, shape, len(shape) - 1) < shape[-1] // 2


def swapped(x):
    return pltpu.roll(x, x.shape[-1] // 2, axis=x.ndim - 1)


def transposed(block):
    turned = block.T
    half = turned.shape[0] // 2
    return jnp.concatenate([turned[:half], turned[half:]], axis=1)


def conjugated(block):
    return jnp.where(low_lanes(block.shape), block, -block)


def right_operand(block):
    turned = swapped(block)
    full = jnp.concatenate([block, jnp.where(low_lanes(block.shape), -turned, turned)], axis=0)
    return split(full * (1.0 / RADIUS))


def backward_kernel(x, hop, out, high, low, hop_out):
    for s in range(x.shape[0]):
        high[s], low[s] = right_operand(conjugated(hop[s, 3]))
        out[s] = three_products(stacked(x[s]), high[s], low[s])
        hop_out[s] = hop[s]


def prepare_kernel(near, diag, hop, own_high, own_low, ahead_high, ahead_low):
    sites, half, wide = diag.shape
    rows = lax.broadcasted_iota(jnp.int32, (half, wide), 0)
    cols = lax.broadcasted_iota(jnp.int32, (half, wide), 1)
    unit = jnp.where(rows == cols, CENTER, 0.0)
    for s in range(sites):
        own_high[s, :wide], own_low[s, :wide] = right_operand(transposed(diag[s]) - unit)
        for d in range(3):
            place = slice((1 + d) * wide, (2 + d) * wide)
            other = hop[lax.rem(near[s, 4 + d], sites), d]
            own_high[s, place], own_low[s, place] = right_operand(
                transposed(hop[s, d]) + conjugated(other)
            )
        ahead_high[s], ahead_low[s] = right_operand(transposed(hop[s, 3]))


def own_kernel(near, x, high, low, out, spread):
    sites = x.shape[0]
    for n in range(sites):
        spread[n] = stacked(x[n])
    for s in range(sites):
        index = [s] + [lax.rem(near[s, d], sites) for d in range(3)]
        parts = jnp.concatenate([spread[n] for n in index], axis=1)
        out[s] = three_products(parts, high[s], low[s])


def step_kernel(mode, near, own, ahead, received, ahead_high, ahead_low, *rest):
    sites = own.shape[0]
    more = rest[0] if mode != "first" else None
    if mode == "image":
        out, back = rest[-1], None
    else:
        back_high, back_low, out, back = rest[-4:]
    for s in range(sites):
        parts = stacked(ahead[lax.rem(near[s, 3], sites)])
        part = three_products(parts, ahead_high[s], ahead_low[s])
        applied = own[s] + (part + received[lax.rem(near[s, 7], sites)])
        if mode == "first":
            out[s] = applied
        elif mode == "next":
            out[s] = 2.0 * applied - more[s]
        else:
            out[s] = RADIUS * applied + CENTER * more[s]
    if back is not None:
        for s in range(sites):
            back[s] = three_products(stacked(out[s]), back_high[s], back_low[s])


def senders(devices):
    chips = devices // 2
    table = []
    for v in range(devices):
        x, c = v // 2, v % 2
        opposite = (x + chips // 2) % chips
        table.append(
            [
                2 * ((x - 1 + 2 * c) % chips) + c,
                2 * ((x - 1) % chips) + 1 - c,
                2 * x + 1 - c,
                2 * opposite + (1 - c if x < chips // 2 else c),
            ]
        )
    return table


def product_kernel(own, image, fourth, second, first, third, out):
    sites, cols, wide = own.shape

    def flat(ref):
        return jnp.concatenate([ref[s] for s in range(sites)], axis=1)

    f = flat(own)
    high, low = split(jnp.concatenate([f, flat(image)], axis=0))
    left = jnp.concatenate([high, low], axis=1)
    half = cols // 2
    dot = functools.partial(lax.dot_general, dimension_numbers=NT, preferred_element_type=f32)
    for p, group in enumerate(((own, first), (second, third), (fourth,))):
        h, l = split(jnp.concatenate([f if r is own else flat(r) for r in group], axis=0))
        tile = dot(left, jnp.concatenate([h, h], axis=1)) + dot(high, l)
        for i in range(2):
            part = tile[i * cols : (i + 1) * cols]
            start = i * (5 * half) + p * cols
            if len(group) == 2:
                out[start : start + cols] = part
            else:
                out[start : start + half] = jnp.concatenate([part[:half], part[half:]], axis=1)
    out[10 * half :] = jnp.zeros((out.shape[0] - 10 * half, wide), f32)


def lines_of(gathered):
    devices, _, wide = gathered.shape
    half = wide // 2
    blocks = {}
    for v, others in enumerate(senders(devices)):
        for j, u in enumerate([v, *others]):
            if j < 4:
                rows = gathered[v, (j // 2) * half : (j // 2 + 1) * half]
                block = rows[:, (j % 2) * half : (j % 2 + 1) * half]
            else:
                rows = gathered[v, wide : wide + half // 2]
                block = jnp.concatenate([rows[:, :half], rows[:, half:]], axis=0)
            blocks[v, u] = block
    for v in range(devices):
        for u in range(devices):
            if (v, u) not in blocks:
                blocks[v, u] = blocks[u, v].T
    return [
        jnp.concatenate([blocks[v, u] for u in range(devices)], axis=1) for v in range(devices)
    ]


def sum_kernel(parts, out):
    total = parts[0]
    for i in range(1, parts.shape[0]):
        total = total + parts[i]
    for i in range(out.shape[0]):
        out[i] = total


def multiply(a, b, dims):
    (ah, al), (bh, bl) = a, b
    dot = functools.partial(lax.dot_general, dimension_numbers=dims, preferred_element_type=f32)
    return dot(ah, bh) + (dot(al, bh) + dot(ah, bl))


def inverse_kernel(count, gathered, high, low, scaled, factor):
    n = high.shape[0]
    half = gathered.shape[2] // 2
    for v, line in enumerate(lines_of(gathered)):
        scaled[v * half : (v + 1) * half, :] = line * (1.0 / count)
    rows = lax.broadcasted_iota(jnp.int32, (n, n), 0)
    cols = lax.broadcasted_iota(jnp.int32, (n, n), 1)
    on_diag = rows == cols
    weight = jnp.where(rows > cols, 1.0, jnp.where(on_diag, 0.5, 0.0))
    unit = jnp.where(on_diag, 1.0, 0.0)
    matrix = scaled[...]
    only_diag = jnp.where(on_diag, matrix, 0.0)
    scale_row = lax.rsqrt(jnp.sum(only_diag, axis=0, keepdims=True))
    scale_col = lax.rsqrt(jnp.sum(only_diag, axis=1, keepdims=True))
    matrix = matrix * scale_row * scale_col
    scaled[...] = matrix
    factor[...] = unit - weight * (matrix - unit)

    mid = n // 2
    dot = functools.partial(lax.dot_general, preferred_element_type=f32)
    square = (mid, mid)
    r, c = (lax.broadcasted_iota(jnp.int32, square, i) for i in range(2))
    small_weight = jnp.where(r > c, 1.0, jnp.where(r == c, 0.5, 0.0))
    small_unit = jnp.where(r == c, 1.0, 0.0)

    def improve(product, cut):
        s1 = cut(scaled[:, :mid])
        s2 = cut(scaled[:, mid:])
        top = cut(factor[:mid, :mid])
        side = cut(factor[mid:, :mid])
        corner = cut(factor[mid:, mid:])
        lower = cut(factor[mid:, :])

        def part(x, piece):
            return tuple(y[piece] for y in x)

        t11 = cut(product(top, part(s1, slice(0, mid)), NN))
        t21 = cut(product(lower, s1, NN))
        t22 = cut(product(lower, s2, NN))
        e11 = product(t11, top, NT) - small_unit
        e21 = product(t21, top, NT)
        e22 = product(t21, side, NT) + product(t22, corner, NT) - small_unit
        p11, p22 = small_weight * e11, small_weight * e22
        size = jnp.sum(p11 * p11 + p22 * p22 + e21 * e21)
        p11, p21, p22 = cut(p11), cut(e21), cut(p22)
        factor[:mid, :mid] = factor[:mid, :mid] - product(p11, top, NN)
        factor[mid:, :mid] = factor[mid:, :mid] - (
            product(p21, top, NN) + product(p22, side, NN)
        )
        factor[mid:, mid:] = factor[mid:, mid:] - product(p22, corner, NN)
        return size

    def once(a, b, dims):
        return dot(a[0], b[0], dimension_numbers=dims)

    improve(once, lambda x: (x.astype(bf16),))

    def go_on(state):
        step, size = state
        return jnp.logical_and(step < NEWTON_LIMIT, jnp.logical_not(size < NEWTON_DONE))

    def body(state):
        return state[0] + 1, improve(multiply, split)

    _, size = lax.while_loop(go_on, body, (jnp.int32(0), jnp.float32(1.0)))

    @pl.when(jnp.logical_not(size < NEWTON_DONE))
    def _():
        factor[...] = unit

        def eliminate(j, carry):
            pivot_row = scaled[pl.ds(j, 1), :]
            here = lax.broadcasted_iota(jnp.int32, (1, n), 1) == j
            pivot = jnp.sum(jnp.where(here, pivot_row, 0.0))
            a = scaled[...]
            column = jnp.sum(jnp.where(cols == j, a, 0.0), axis=1, keepdims=True) / pivot
            below = lax.broadcasted_iota(jnp.int32, (n, 1), 0) > j
            column = jnp.where(below, column, 0.0)
            r_row = factor[pl.ds(j, 1), :]
            scaled[...] = a - column * pivot_row
            factor[...] = factor[...] - column * r_row
            factor[pl.ds(j, 1), :] = r_row * lax.rsqrt(jnp.full_like(r_row, pivot))
            return carry

        lax.fori_loop(0, n, eliminate, 0)

    high[...], low[...] = split(factor[...] * scale_row)


def own_rows(place, high, low, count):
    rows = pl.ds(pl.multiple_of(place[0] * count, count), count)
    return high[rows, :], low[rows, :]


def basis_kernel(place, vectors, high, low, out):
    sites, columns, _ = out.shape
    mine = own_rows(place, high, low, columns)
    for s in range(sites):
        block = jnp.concatenate(
            [vectors[u, s * columns : (s + 1) * columns] for u in range(vectors.shape[0])],
            axis=0,
        )
        out[s] = multiply(mine, split(block), NN)


def projected_kernel(count, place, moments, high, low, out):
    moment = jnp.concatenate(lines_of(moments), axis=0)
    mine = own_rows(place, high, low, out.shape[0])
    half_way = multiply(mine, split(moment), NN)
    out[...] = multiply(split(half_way), (high[...], low[...]), NT) * (1.0 / count)


def passed_along(x, by):
    size = lax.axis_size("site")
    return lax.ppermute(x, "site", [(i, (i + by) % size) for i in range(size)])


def local(diag_blocks, hop_blocks, neighbors, start_basis):
    sites, both, cols = start_basis.shape
    half = both // 2
    devices = lax.axis_size("vec")
    slices = lax.axis_size("site")
    all_cols = cols * devices
    count = float(sites * both * slices)
    place = lax.axis_index("vec").astype(jnp.int32).reshape(1)
    shape = jax.ShapeDtypeStruct
    block = shape((sites, cols, both), f32)
    size = sites * cols * both * 4

    def matrices(blocks):
        return (shape((sites, blocks * both, both), bf16),) * 2

    def work(blocks):
        return sites * cols * blocks * 3 * both * both * 2

    current = jnp.swapaxes(start_basis, 1, 2)
    back, *back_mats, links = call(
        backward_kernel,
        (block, *matrices(1), shape(hop_blocks.shape, f32)),
        0,
        2,
        flops=work(1),
        moved=8 * size,
        name="backward",
    )(current, hop_blocks)
    mats = call(
        prepare_kernel,
        (*matrices(4), *matrices(1)),
        1,
        2,
        flops=1 << 24,
        moved=1 << 23,
        name="prepare",
    )(neighbors, diag_blocks, links)
    own_mats, ahead_mats = mats[:2], mats[2:]

    def apply(vectors, back, mode, *more):
        ahead = passed_along(vectors, -1)
        received = passed_along(back, 1)
        own = call(
            own_kernel,
            block,
            1,
            3,
            scratch=[pltpu.VMEM((sites, 2 * cols, both), bf16)],
            flops=work(4),
            moved=8 * size,
            name="own_slice",
        )(neighbors, vectors, *own_mats)
        if mode != "image":
            more = (*more, *back_mats)
        return call(
            functools.partial(step_kernel, mode),
            block if mode == "image" else (block, block),
            1,
            5 + len(more),
            flops=work(1),
            moved=8 * size,
            name="next_slices",
        )(neighbors, own, ahead, received, *ahead_mats, *more)

    previous = current
    current, back = apply(current, back, "first")
    for _ in range(DEGREE - 1):
        following, back = apply(current, back, "next", previous)
        previous, current = current, following

    image = apply(current, back, "image", current)
    table = senders(devices)
    others = [
        lax.ppermute(current, "vec", [(table[v][i], v) for v in range(devices)])
        for i in (3, 1, 0, 2)
    ]
    kept = 5 * cols // 2
    products = call(
        product_kernel,
        shape((slices * 8, both), f32),
        0,
        6,
        flops=6 * 5 * cols * 2 * cols * sites * both,
        moved=1 << 22,
        name="products",
    )(current, image, *others)
    flat, _ = lax.optimization_barrier((current.reshape(sites * cols, both), products))
    everything = lax.all_gather(flat, "vec", axis=0)

    parts = lax.all_to_all(products.reshape(slices, 8, both), "site", 0, 0, tiled=True)
    summed = call(
        sum_kernel, shape((slices, 8, both), f32), 0, 1, moved=1 << 19, name="sum_parts"
    )(parts)
    whole = lax.all_to_all(summed, "site", 0, 0, tiled=True).reshape(slices * 8, both)
    whole, everything = lax.optimization_barrier((whole, everything))
    moments = lax.all_gather(whole[kept : kept + all_cols // 2], "vec", axis=0)
    gram = lax.all_gather(whole[:kept], "vec", axis=0)

    inverse = call(
        functools.partial(inverse_kernel, count),
        (shape((all_cols, all_cols), bf16),) * 2,
        0,
        1,
        scratch=[pltpu.VMEM((all_cols, all_cols), f32)] * 2,
        flops=9 * 6 * all_cols**3,
        moved=1 << 21,
        name="inverse_factor",
    )(gram)
    basis = call(
        basis_kernel,
        block,
        1,
        3,
        flops=6 * all_cols * cols * sites * both,
        moved=1 << 22,
        name="basis",
    )(place, everything, *inverse)
    projected = call(
        functools.partial(projected_kernel, count),
        shape((cols, all_cols), f32),
        1,
        3,
        flops=12 * all_cols * all_cols * cols,
        moved=1 << 22,
        name="projected",
    )(place, moments, *inverse)
    return jnp.swapaxes(basis, 1, 2), projected.T


def solution(mesh):
    placed = (
        P("site", None, None),
        P("site", None, None, None),
        P("site", None),
        P("site", None, "vec"),
    )
    return jax.shard_map(
        local,
        mesh=mesh,
        in_specs=placed,
        out_specs=(P("site", None, "vec"), P(None, "vec")),
        check_vma=False,
    )
```

```python
import functools

import jax
import jax.numpy as jnp
from jax import lax
from jax.experimental import pallas as pl
from jax.experimental.pallas import tpu as pltpu
from jax.sharding import PartitionSpec as P

DEGREE = 4
CENTER = 3.7
RADIUS = 3.1
NEWTON_LIMIT = 12
NEWTON_DONE = 1e-6
VMEM_LIMIT = 44 * 1024 * 1024
VMEM_WHOLE = 44 * 1024 * 1024

f32 = jnp.float32
bf16 = jnp.bfloat16
VMEM_SPEC = pl.BlockSpec(memory_space=pltpu.VMEM)
SMEM_SPEC = pl.BlockSpec(memory_space=pltpu.SMEM)


def call(
    kernel,
    out_shape,
    n_smem,
    n_vmem,
    scratch=(),
    flops=0,
    moved=0,
    name=None,
):
    return pl.pallas_call(
        kernel,
        out_shape=out_shape,
        in_specs=[SMEM_SPEC] * n_smem + [VMEM_SPEC] * n_vmem,
        out_specs=jax.tree.map(lambda _: VMEM_SPEC, out_shape),
        scratch_shapes=list(scratch),
        compiler_params=pltpu.CompilerParams(vmem_limit_bytes=VMEM_LIMIT),
        cost_estimate=pl.CostEstimate(flops=flops, bytes_accessed=moved, transcendentals=0),
        name=name,
    )


def split(x):
    high = x.astype(bf16)
    return high, (x - high.astype(f32)).astype(bf16)


NT = (((1,), (1,)), ((), ()))
NN = (((1,), (0,)), ((), ()))


def stacked(x):
    return jnp.concatenate(split(x), axis=0)


def three_products(parts, high, low):
    m = parts.shape[0] // 2
    both = jnp.dot(parts, high, preferred_element_type=f32)
    return both[:m] + (both[m:] + jnp.dot(parts[:m], low, preferred_element_type=f32))


def low_lanes(shape):
    return lax.broadcasted_iota(jnp.int32, shape, len(shape) - 1) < shape[-1] // 2


def swapped(x):
    return pltpu.roll(x, x.shape[-1] // 2, axis=x.ndim - 1)


def transposed(block):
    turned = block.T
    half = turned.shape[0] // 2
    return jnp.concatenate([turned[:half], turned[half:]], axis=1)


def conjugated(block):
    return jnp.where(low_lanes(block.shape), block, -block)


def right_operand(block):
    turned = swapped(block)
    full = jnp.concatenate([block, jnp.where(low_lanes(block.shape), -turned, turned)], axis=0)
    return split(full * (1.0 / RADIUS))


def backward_kernel(x, hop, out, high, low, hop_out):
    for s in range(x.shape[0]):
        high[s], low[s] = right_operand(conjugated(hop[s, 3]))
        out[s] = three_products(stacked(x[s]), high[s], low[s])
        hop_out[s] = hop[s]


def prepare_kernel(near, diag, hop, own_high, own_low, ahead_high, ahead_low):
    sites, half, wide = diag.shape
    rows = lax.broadcasted_iota(jnp.int32, (half, wide), 0)
    cols = lax.broadcasted_iota(jnp.int32, (half, wide), 1)
    unit = jnp.where(rows == cols, CENTER, 0.0)
    for s in range(sites):
        own_high[s, :wide], own_low[s, :wide] = right_operand(transposed(diag[s]) - unit)
        for d in range(3):
            place = slice((1 + d) * wide, (2 + d) * wide)
            other = hop[lax.rem(near[s, 4 + d], sites), d]
            own_high[s, place], own_low[s, place] = right_operand(
                transposed(hop[s, d]) + conjugated(other)
            )
        ahead_high[s], ahead_low[s] = right_operand(transposed(hop[s, 3]))


def own_kernel(near, x, high, low, out, spread):
    sites = x.shape[0]
    for n in range(sites):
        spread[n] = stacked(x[n])
    for s in range(sites):
        index = [s] + [lax.rem(near[s, d], sites) for d in range(3)]
        parts = jnp.concatenate([spread[n] for n in index], axis=1)
        out[s] = three_products(parts, high[s], low[s])


def step_kernel(mode, near, own, ahead, received, ahead_high, ahead_low, *rest):
    sites = own.shape[0]
    more = rest[0] if mode != "first" else None
    if mode == "image":
        out, back = rest[-1], None
    else:
        back_high, back_low, out, back = rest[-4:]
    for s in range(sites):
        parts = stacked(ahead[lax.rem(near[s, 3], sites)])
        part = three_products(parts, ahead_high[s], ahead_low[s])
        applied = own[s] + (part + received[lax.rem(near[s, 7], sites)])
        if mode == "first":
            out[s] = applied
        elif mode == "next":
            out[s] = 2.0 * applied - more[s]
        else:
            out[s] = RADIUS * applied + CENTER * more[s]
    if back is not None:
        for s in range(sites):
            back[s] = three_products(stacked(out[s]), back_high[s], back_low[s])


def senders(devices):
    chips = devices // 2
    table = []
    for v in range(devices):
        x, c = v // 2, v % 2
        opposite = (x + chips // 2) % chips
        table.append(
            [
                2 * ((x - 1) % chips) + c,
                2 * ((x - 1) % chips) + 1 - c,
                2 * x + 1 - c,
                2 * opposite + (1 - c if x < chips // 2 else c),
            ]
        )
    return table


def product_kernel(own, image, fourth, second, first, third, out):
    sites, cols, wide = own.shape

    def flat(ref):
        return jnp.concatenate([ref[s] for s in range(sites)], axis=1)

    f = flat(own)
    high, low = split(jnp.concatenate([f, flat(image)], axis=0))
    left = jnp.concatenate([high, low], axis=1)
    half = cols // 2
    dot = functools.partial(lax.dot_general, dimension_numbers=NT, preferred_element_type=f32)
    for p, group in enumerate(((own, first), (second, third), (fourth,))):
        h, l = split(jnp.concatenate([f if r is own else flat(r) for r in group], axis=0))
        tile = dot(left, jnp.concatenate([h, h], axis=1)) + dot(high, l)
        for i in range(2):
            part = tile[i * cols : (i + 1) * cols]
            start = i * (5 * half) + p * cols
            if len(group) == 2:
                out[start : start + cols] = part
            else:
                out[start : start + half] = jnp.concatenate([part[:half], part[half:]], axis=1)
    out[10 * half :] = jnp.zeros((out.shape[0] - 10 * half, wide), f32)


def lines_of(gathered):
    devices, _, wide = gathered.shape
    half = wide // 2
    blocks = {}
    for v, others in enumerate(senders(devices)):
        for j, u in enumerate([v, *others]):
            if j < 4:
                rows = gathered[v, (j // 2) * half : (j // 2 + 1) * half]
                block = rows[:, (j % 2) * half : (j % 2 + 1) * half]
            else:
                rows = gathered[v, wide : wide + half // 2]
                block = jnp.concatenate([rows[:, :half], rows[:, half:]], axis=0)
            blocks[v, u] = block
    for v in range(devices):
        for u in range(devices):
            if (v, u) not in blocks:
                blocks[v, u] = blocks[u, v].T
    return [
        jnp.concatenate([blocks[v, u] for u in range(devices)], axis=1) for v in range(devices)
    ]


def sum_kernel(parts, out):
    total = parts[0]
    for i in range(1, parts.shape[0]):
        total = total + parts[i]
    for i in range(out.shape[0]):
        out[i] = total


def multiply(a, b, dims):
    (ah, al), (bh, bl) = a, b
    dot = functools.partial(lax.dot_general, dimension_numbers=dims, preferred_element_type=f32)
    return dot(ah, bh) + (dot(al, bh) + dot(ah, bl))


def inverse_kernel(count, gathered, high, low, scaled, factor):
    n = high.shape[0]
    half = gathered.shape[2] // 2
    for v, line in enumerate(lines_of(gathered)):
        scaled[v * half : (v + 1) * half, :] = line * (1.0 / count)
    rows = lax.broadcasted_iota(jnp.int32, (n, n), 0)
    cols = lax.broadcasted_iota(jnp.int32, (n, n), 1)
    on_diag = rows == cols
    weight = jnp.where(rows > cols, 1.0, jnp.where(on_diag, 0.5, 0.0))
    unit = jnp.where(on_diag, 1.0, 0.0)
    matrix = scaled[...]
    only_diag = jnp.where(on_diag, matrix, 0.0)
    scale_row = lax.rsqrt(jnp.sum(only_diag, axis=0, keepdims=True))
    scale_col = lax.rsqrt(jnp.sum(only_diag, axis=1, keepdims=True))
    matrix = matrix * scale_row * scale_col
    scaled[...] = matrix
    factor[...] = unit - weight * (matrix - unit)

    mid = n // 2
    dot = functools.partial(lax.dot_general, preferred_element_type=f32)
    square = (mid, mid)
    r, c = (lax.broadcasted_iota(jnp.int32, square, i) for i in range(2))
    small_weight = jnp.where(r > c, 1.0, jnp.where(r == c, 0.5, 0.0))
    small_unit = jnp.where(r == c, 1.0, 0.0)

    def improve(product, cut):
        s1 = cut(scaled[:, :mid])
        s2 = cut(scaled[:, mid:])
        top = cut(factor[:mid, :mid])
        side = cut(factor[mid:, :mid])
        corner = cut(factor[mid:, mid:])
        lower = cut(factor[mid:, :])

        def part(x, piece):
            return tuple(y[piece] for y in x)

        t11 = cut(product(top, part(s1, slice(0, mid)), NN))
        t21 = cut(product(lower, s1, NN))
        t22 = cut(product(lower, s2, NN))
        e11 = product(t11, top, NT) - small_unit
        e21 = product(t21, top, NT)
        e22 = product(t21, side, NT) + product(t22, corner, NT) - small_unit
        p11, p22 = small_weight * e11, small_weight * e22
        size = jnp.sum(p11 * p11 + p22 * p22 + e21 * e21)
        p11, p21, p22 = cut(p11), cut(e21), cut(p22)
        factor[:mid, :mid] = factor[:mid, :mid] - product(p11, top, NN)
        factor[mid:, :mid] = factor[mid:, :mid] - (
            product(p21, top, NN) + product(p22, side, NN)
        )
        factor[mid:, mid:] = factor[mid:, mid:] - product(p22, corner, NN)
        return size

    def once(a, b, dims):
        return dot(a[0], b[0], dimension_numbers=dims)

    improve(once, lambda x: (x.astype(bf16),))

    def go_on(state):
        step, size = state
        return jnp.logical_and(step < NEWTON_LIMIT, jnp.logical_not(size < NEWTON_DONE))

    def body(state):
        return state[0] + 1, improve(multiply, split)

    _, size = lax.while_loop(go_on, body, (jnp.int32(0), jnp.float32(1.0)))

    @pl.when(jnp.logical_not(size < NEWTON_DONE))
    def _():
        factor[...] = unit

        def eliminate(j, carry):
            pivot_row = scaled[pl.ds(j, 1), :]
            here = lax.broadcasted_iota(jnp.int32, (1, n), 1) == j
            pivot = jnp.sum(jnp.where(here, pivot_row, 0.0))
            a = scaled[...]
            column = jnp.sum(jnp.where(cols == j, a, 0.0), axis=1, keepdims=True) / pivot
            below = lax.broadcasted_iota(jnp.int32, (n, 1), 0) > j
            column = jnp.where(below, column, 0.0)
            r_row = factor[pl.ds(j, 1), :]
            scaled[...] = a - column * pivot_row
            factor[...] = factor[...] - column * r_row
            factor[pl.ds(j, 1), :] = r_row * lax.rsqrt(jnp.full_like(r_row, pivot))
            return carry

        lax.fori_loop(0, n, eliminate, 0)

    high[...], low[...] = split(factor[...] * scale_row)


def own_rows(place, high, low, count):
    rows = pl.ds(pl.multiple_of(place[0] * count, count), count)
    return high[rows, :], low[rows, :]


def basis_kernel(place, vectors, high, low, out):
    sites, columns, _ = out.shape
    mine = own_rows(place, high, low, columns)
    for s in range(sites):
        block = jnp.concatenate(
            [vectors[u, s * columns : (s + 1) * columns] for u in range(vectors.shape[0])],
            axis=0,
        )
        out[s] = multiply(mine, split(block), NN)


def projected_kernel(count, place, moments, high, low, out):
    moment = jnp.concatenate(lines_of(moments), axis=0)
    mine = own_rows(place, high, low, out.shape[0])
    half_way = multiply(mine, split(moment), NN)
    out[...] = multiply(split(half_way), (high[...], low[...]), NT) * (1.0 / count)


def passed_along(x, by):
    size = lax.axis_size("site")
    return lax.ppermute(x, "site", [(i, (i + by) % size) for i in range(size)])


def local(diag_blocks, hop_blocks, neighbors, start_basis):
    sites, both, cols = start_basis.shape
    half = both // 2
    devices = lax.axis_size("vec")
    slices = lax.axis_size("site")
    all_cols = cols * devices
    count = float(sites * both * slices)
    place = lax.axis_index("vec").astype(jnp.int32).reshape(1)
    shape = jax.ShapeDtypeStruct
    block = shape((sites, cols, both), f32)
    size = sites * cols * both * 4

    def matrices(blocks):
        return (shape((sites, blocks * both, both), bf16),) * 2

    def work(blocks):
        return sites * cols * blocks * 3 * both * both * 2

    current = jnp.swapaxes(start_basis, 1, 2)
    back, *back_mats, links = call(
        backward_kernel,
        (block, *matrices(1), shape(hop_blocks.shape, f32)),
        0,
        2,
        flops=work(1),
        moved=8 * size,
        name="backward",
    )(current, hop_blocks)
    mats = call(
        prepare_kernel,
        (*matrices(4), *matrices(1)),
        1,
        2,
        flops=1 << 24,
        moved=1 << 23,
        name="prepare",
    )(neighbors, diag_blocks, links)
    own_mats, ahead_mats = mats[:2], mats[2:]

    def apply(vectors, back, mode, *more):
        ahead = passed_along(vectors, -1)
        received = passed_along(back, 1)
        own = call(
            own_kernel,
            block,
            1,
            3,
            scratch=[pltpu.VMEM((sites, 2 * cols, both), bf16)],
            flops=work(4),
            moved=8 * size,
            name="own_slice",
        )(neighbors, vectors, *own_mats)
        if mode != "image":
            more = (*more, *back_mats)
        return call(
            functools.partial(step_kernel, mode),
            block if mode == "image" else (block, block),
            1,
            5 + len(more),
            flops=work(1),
            moved=8 * size,
            name="next_slices",
        )(neighbors, own, ahead, received, *ahead_mats, *more)

    previous = current
    current, back = apply(current, back, "first")
    for _ in range(DEGREE - 1):
        following, back = apply(current, back, "next", previous)
        previous, current = current, following

    image = apply(current, back, "image", current)
    table = senders(devices)
    others = [
        lax.ppermute(current, "vec", [(table[v][i], v) for v in range(devices)])
        for i in (3, 1, 0, 2)
    ]
    kept = 5 * cols // 2
    products = call(
        product_kernel,
        shape((slices * 8, both), f32),
        0,
        6,
        flops=6 * 5 * cols * 2 * cols * sites * both,
        moved=1 << 22,
        name="products",
    )(current, image, *others)
    flat, _ = lax.optimization_barrier((current.reshape(sites * cols, both), products))
    everything = lax.all_gather(flat, "vec", axis=0)

    parts = lax.all_to_all(products.reshape(slices, 8, both), "site", 0, 0, tiled=True)
    summed = call(
        sum_kernel, shape((slices, 8, both), f32), 0, 1, moved=1 << 19, name="sum_parts"
    )(parts)
    whole = lax.all_to_all(summed, "site", 0, 0, tiled=True).reshape(slices * 8, both)
    whole, everything = lax.optimization_barrier((whole, everything))
    moments = lax.all_gather(whole[kept : kept + all_cols // 2], "vec", axis=0)
    gram = lax.all_gather(whole[:kept], "vec", axis=0)

    inverse = call(
        functools.partial(inverse_kernel, count),
        (shape((all_cols, all_cols), bf16),) * 2,
        0,
        1,
        scratch=[pltpu.VMEM((all_cols, all_cols), f32)] * 2,
        flops=9 * 6 * all_cols**3,
        moved=1 << 21,
        name="inverse_factor",
    )(gram)
    basis = call(
        basis_kernel,
        block,
        1,
        3,
        flops=6 * all_cols * cols * sites * both,
        moved=1 << 22,
        name="basis",
    )(place, everything, *inverse)
    projected = call(
        functools.partial(projected_kernel, count),
        shape((cols, all_cols), f32),
        1,
        3,
        flops=12 * all_cols * all_cols * cols,
        moved=1 << 22,
        name="projected",
    )(place, moments, *inverse)
    return jnp.swapaxes(basis, 1, 2), projected.T


def solution(mesh):
    placed = (
        P("site", None, None),
        P("site", None, None, None),
        P("site", None),
        P("site", None, "vec"),
    )
    return jax.shard_map(
        local,
        mesh=mesh,
        in_specs=placed,
        out_specs=(P("site", None, "vec"), P(None, "vec")),
        check_vma=False,
    )
```
